128 devices in a mesh: quad: 8 (over z, x_lo), row: 16 (over x_hi, y, core).
Axes of the slice: x: 4 (x_hi: 2, x_lo: 2; x = x_hi * 2 + x_lo), y: 4, z: 4, core: 2. Of those that a mesh axis runs over, the one named last changes fastest.
Arguments:
- hamiltonian: bfloat16 [1024, 64, 1536], P('row'), may hold values from -0.15625 to 0.15625
- columns: int32 [1024, 24], P('row'), may hold values from 0 to 1023, as said below
- counts: int32 [1024], P('row'), may hold values from 2 to 24, as said below
- precond: bfloat16 [16, 1024, 64, 128], P('quad', 'row'), may hold values from -0.5 to 0.5
- rhs: bfloat16 [65536, 128], P('row'), may hold values from -6 to 6
Outputs:
- moments_out: float32 [8, 65536, 128], P('quad', 'row')
- blocks_out: float32 [8, 128, 128], P('quad')
The draws below stay inside these ranges and needn't reach their ends.
Inputs may be any that keep to these rules, and one draw needn't show every extreme that they name: `columns`: slot 0 of row block b holds b itself; slot 1 holds b - 64 for even b and b + 64 for odd b, reflected at the ends (an index -m becomes m, an index 1023 + m becomes 1024 - 1 - m); every column block lies within 64 blocks of its row block. `counts`: every run of 64 row blocks starting at a multiple of 64 holds a row block with all 24 slots live.
All inputs are finite; a program needn't handle non-finite values.
Results may differ from the reference program's by a relative error of at most 0.02.
Values may be sent and summed in bfloat16 or wider, within the bound.
No kernel may reach another device: no remote copies, remote signals or barrier semaphores. Data moves between devices by JAX's collectives and lax.ppermute only.
A program may use at most 128 MiB of HBM per device.

```python
import math
import jax
import jax.numpy as jnp
from jax import lax

BS = 64
K = 24
COLS = 128
RB_DEV = 64
Q_DEV = 2
ITERS = 2
MOMENTS = 8
REACH = 64
NB = 1024
NR = 65536
QUADS = 16
N_QUAD = 8
N_ROW = 16


def draw_columns(key, part):
    first_key = jax.random.fold_in(key, 11)
    second_key = jax.random.fold_in(key, 12)
    blocks = jnp.arange(NB, dtype=jnp.int32)[:, None]
    offsets = jax.random.randint(first_key, (NB, K), -REACH, REACH + 1, dtype=jnp.int32)
    signs = jnp.where(jax.random.randint(second_key, (NB, 1), 0, 2, dtype=jnp.int32) == 0, -1, 1)
    slot_ids = jnp.arange(K, dtype=jnp.int32)[None, :]
    forced = 1 + jnp.arange(NB, dtype=jnp.int32) % (K - 1)
    offsets = jnp.where(slot_ids == forced[:, None], signs * REACH, offsets)
    alternate = jnp.where(blocks % 2 == 0, -REACH, REACH)
    offsets = jnp.where(slot_ids == 1, alternate, offsets)
    offsets = jnp.where(slot_ids == 0, 0, offsets)
    target = jnp.abs(blocks + offsets)
    target = jnp.where(target > NB - 1, 2 * (NB - 1) - target, target)
    return target.astype(jnp.int32)


def draw_counts(key, part):
    first_key = jax.random.fold_in(key, 21)
    second_key = jax.random.fold_in(key, 22)
    values = jax.random.randint(first_key, (NB,), 2, K + 1, dtype=jnp.int32)
    position = jax.random.randint(second_key, (), 0, RB_DEV, dtype=jnp.int32)
    blocks = jnp.arange(NB, dtype=jnp.int32)
    return jnp.where(blocks % RB_DEV == position, K, values).astype(jnp.int32)


def shard_levels(own_key, shape, cuts, least, high):
    gain, own = 1.0, jax.random.fold_in(own_key, 6)
    for dim, blocks in cuts:
        heights = jnp.exp(jax.random.uniform(jax.random.fold_in(own, dim), (blocks,), jnp.float32, least / len(cuts), high / len(cuts)))
        gain = gain * jnp.repeat(heights, shape[dim] // blocks).reshape([-1 if axis == dim else 1 for axis in range(len(shape))])
    return gain


def noise(key, shape, scale, reach, split=(), kind=jnp.bfloat16):
    values = scale * jax.random.normal(key, shape, jnp.float32)
    if split:
        values = values * shard_levels(key, shape, split, -0.22, 0.18)
    return jnp.clip(values, -reach, reach).astype(kind)


def setup_inputs(seed: int = 0) -> dict:
    arg_keys = jax.random.split(jax.random.key(seed), 6)
    hamiltonian = noise(arg_keys[0], (NB, BS, K * BS), (K * BS) ** -0.5, 0.15625, ((0, 16),))
    columns = draw_columns(jax.random.fold_in(arg_keys[5], 71), 0)
    counts = draw_counts(jax.random.fold_in(arg_keys[5], 71), 0)
    precond = noise(arg_keys[3], (QUADS, NB, BS, 2 * BS), (2 * BS) ** -0.5, 0.5, ((0, 8), (1, 16)))
    rhs = noise(arg_keys[4], (NR, COLS), 1.0, 6.0, ((0, 16),))
    return {"hamiltonian": hamiltonian, "columns": columns, "counts": counts, "precond": precond, "rhs": rhs}


def rotate(values):
    half_cols = values.shape[-1] // 2
    return jnp.concatenate([-values[..., half_cols:], values[..., :half_cols]], axis=-1)

def apply_inverse(blocks_pre, resid):
    pre_float = blocks_pre.astype(jnp.float32)
    res_float = resid.astype(jnp.float32)
    stacked = jnp.concatenate([res_float, rotate(res_float)], axis=1)
    return jnp.einsum('bij,bjc->bic', pre_float, stacked)

def multiply(hamiltonian, index_table, iterate):
    padded = jnp.concatenate([iterate, jnp.zeros((1, BS, COLS), iterate.dtype)], axis=0)
    ham_groups = hamiltonian.reshape(N_ROW, RB_DEV, BS, K * BS)
    idx_groups = index_table.reshape(N_ROW, RB_DEV, K)

    def one_group(pair):
        ham_block, idx_block = pair
        gathered = padded[idx_block].astype(jnp.float32).reshape(RB_DEV, K * BS, COLS)
        return jnp.einsum('bij,bjc->bic', ham_block.astype(jnp.float32), gathered)
    return lax.map(one_group, (ham_groups, idx_groups)).reshape(NB, BS, COLS)

def reference(hamiltonian, columns, counts, precond, rhs):
    live = jnp.arange(K)[None, :] < counts[:, None]
    index_table = jnp.where(live, columns, NB).astype(jnp.int32)
    rhs_blocks = rhs.reshape(NB, BS, COLS)
    rhs_float = rhs_blocks.astype(jnp.float32)

    def solve_point(pair):
        point, blocks_pre = pair
        theta = 2.0 * jnp.pi * (point.astype(jnp.float32) + 0.5) / QUADS
        zreal = jnp.cos(theta)
        zimag = jnp.sin(theta)
        iterate = apply_inverse(blocks_pre, rhs_blocks).astype(jnp.bfloat16)
        for sweep in range(ITERS):
            product = multiply(hamiltonian, index_table, iterate)
            current = iterate.astype(jnp.float32)
            shifted = zreal * current + zimag * rotate(current)
            resid = (rhs_float - (shifted - product)).astype(jnp.bfloat16)
            iterate = (current + apply_inverse(blocks_pre, resid)).astype(jnp.bfloat16)
        return iterate
    solutions = lax.map(solve_point, (jnp.arange(QUADS, dtype=jnp.int32), precond))
    scale = 1.0 / math.sqrt(NR)
    flat_rhs = rhs.astype(jnp.float32)
    moment_list = []
    block_list = []
    for moment in range(MOMENTS):
        total = jnp.zeros((NB, BS, COLS), jnp.float32)
        for group in range(N_QUAD):
            part = jnp.zeros((NB, BS, COLS), jnp.float32)
            for inner in range(Q_DEV):
                point = group * Q_DEV + inner
                theta = 2.0 * math.pi * (point + 0.5) / QUADS
                coef_a = math.cos((moment + 1) * theta) / QUADS
                coef_b = math.sin((moment + 1) * theta) / QUADS
                current = solutions[point].astype(jnp.float32)
                part = part + coef_a * current + coef_b * rotate(current)
            held = lax.optimization_barrier(part.astype(jnp.bfloat16))
            total = total + held.astype(jnp.float32)
        flat_total = total.reshape(NR, COLS)
        moment_list.append(flat_total)
        block_list.append(jnp.dot(flat_rhs.T, flat_total, precision=lax.Precision.HIGHEST) * scale)
    return (jnp.stack(moment_list), jnp.stack(block_list))
```

```python
import math

import jax
import jax.numpy as jnp
import numpy as np
from jax import lax
from jax.experimental import pallas as pl
from jax.experimental.pallas import tpu as pltpu
from jax.sharding import PartitionSpec as P

ITERS = 2
MOMENTS = 8
POINTS = 16
BS = 64
SLOTS = 24
RB = 64
LANES = 128
GROUP = 64
HALF = 32
STEP = 8
F32 = jnp.float32
BF16 = jnp.bfloat16


def unit_lanes():
    table = np.zeros((LANES, 4 * LANES), np.float32)
    for unit in range(2):
        for lane in range(LANES):
            part, col = (lane // HALF) % 2, lane % HALF
            src = unit * HALF + col
            table[part * GROUP + src, unit * LANES + lane] = 1.0
            sign = -1.0 if part == 0 else 1.0
            table[(1 - part) * GROUP + src, (2 + unit) * LANES + lane] = sign
    return table


def lane_ids(shape):
    return lax.broadcasted_iota(jnp.int32, shape, len(shape) - 1)


def split_points(top, bottom):
    lane = lane_ids(top.shape) % LANES
    first = lane < GROUP
    zero = jnp.zeros_like(top)
    return jnp.concatenate(
        [
            jnp.where(first, top, zero),
            jnp.where(first, bottom, zero),
            jnp.where(first, zero, top),
            jnp.where(first, zero, bottom),
        ],
        axis=0,
    )


def init_kernel(x_ref, pre_ref, map_ref, rhs_a_ref, rhs_b_ref, y_a_ref, y_b_ref):
    spread = jnp.dot(x_ref[...], map_ref[...], preferred_element_type=F32)
    rhs_a_ref[...] = spread[:, :LANES].astype(BF16).reshape(STEP, BS, LANES)
    rhs_b_ref[...] = spread[:, LANES : 2 * LANES].astype(BF16).reshape(STEP, BS, LANES)
    for b in range(STEP):
        rows = slice(b * BS, (b + 1) * BS)
        right = split_points(spread[rows, : 2 * LANES], spread[rows, 2 * LANES :]).astype(BF16)
        left = jnp.concatenate([pre_ref[0, b], pre_ref[1, b]], axis=1)
        out = jnp.dot(left, right, preferred_element_type=F32)
        y_a_ref[b] = out[:, :LANES].astype(BF16)
        y_b_ref[b] = out[:, LANES:].astype(BF16)


def initial(rhs, precond):
    block = jax.ShapeDtypeStruct((RB, BS, LANES), BF16)
    out_spec = pl.BlockSpec((STEP, BS, LANES), lambda i: (i, 0, 0))
    return pl.pallas_call(
        init_kernel,
        grid=(RB // STEP,),
        in_specs=[
            pl.BlockSpec((STEP * BS, LANES), lambda i: (i, 0)),
            pl.BlockSpec((2, STEP, BS, LANES), lambda i: (0, i, 0, 0)),
            pl.BlockSpec((LANES, 4 * LANES), lambda i: (0, 0)),
        ],
        out_specs=[out_spec] * 4,
        out_shape=[block] * 4,
        name="initial",
    )(rhs, precond, jnp.asarray(unit_lanes(), BF16))


def rotate_lanes(x):
    lane = lane_ids(x.shape) % GROUP
    up = pltpu.roll(x, LANES - HALF, axis=x.ndim - 1)
    down = pltpu.roll(x, HALF, axis=x.ndim - 1)
    return jnp.where(lane < HALF, -up, down)


def sweep_kernel(
    last, index_ref, ham_ref, pre_ref, rhs_ref, z_ref, local_ref, before_ref, after_ref, x_ref,
    out_ref, *rest
):
    if last:
        gram_ref, held, sems = rest
    else:
        held, sems = rest
    step = pl.program_id(0)

    @pl.when(step == 0)
    def _():
        copies = []
        for n, ref in enumerate((before_ref, local_ref, after_ref)):
            copies.append(
                pltpu.make_async_copy(ref, held.at[pl.ds(n * RB, RB)], sems.at[n])
            )
            copies[-1].start()
        held[3 * RB] = jnp.zeros((BS, LANES), BF16)
        if last:
            gram_ref[...] = jnp.zeros_like(gram_ref)
        for copy in copies:
            copy.wait()

    zreal = z_ref[0:1, :]
    zimag = z_ref[1:2, :]
    for b in range(STEP):
        row = step * STEP + b
        total = jnp.zeros((BS, LANES), F32)
        for g in range(SLOTS // 4):
            right = jnp.concatenate(
                [held[index_ref[row * SLOTS + g * 4 + s]] for s in range(4)], axis=0
            )
            left = ham_ref[b, :, g * 4 * BS : (g + 1) * 4 * BS]
            total = total + jnp.dot(left, right, preferred_element_type=F32)
        current = held[RB + row].astype(F32)
        shifted = zreal * current + zimag * rotate_lanes(current)
        resid = (rhs_ref[b].astype(F32) - (shifted - total)).astype(BF16).astype(F32)
        right = split_points(resid, rotate_lanes(resid)).astype(BF16)
        left = jnp.concatenate([pre_ref[0, b], pre_ref[1, b]], axis=1)
        out_ref[b] = (current + jnp.dot(left, right, preferred_element_type=F32)).astype(BF16)
    if last:
        gram_ref[...] += lax.dot_general(
            x_ref[...],
            out_ref[...].reshape(STEP * BS, LANES),
            (((0,), (0,)), ((), ())),
            preferred_element_type=F32,
        )


def sweep(index, ham, precond, rhs_unit, z, local, before, after, rhs, last):
    block = pl.BlockSpec((STEP, BS, LANES), lambda i, n: (i, 0, 0))
    anywhere = pl.BlockSpec(memory_space=pl.ANY)
    out_specs = [block]
    out_shape = [jax.ShapeDtypeStruct((RB, BS, LANES), BF16)]
    if last:
        out_specs.append(pl.BlockSpec((LANES, LANES), lambda i, n: (0, 0)))
        out_shape.append(jax.ShapeDtypeStruct((LANES, LANES), F32))

    def kernel(*refs):
        sweep_kernel(last, *refs)

    return pl.pallas_call(
        kernel,
        grid_spec=pltpu.PrefetchScalarGridSpec(
            num_scalar_prefetch=1,
            grid=(RB // STEP,),
            in_specs=[
                pl.BlockSpec((STEP, BS, SLOTS * BS), lambda i, n: (i, 0, 0)),
                pl.BlockSpec((2, STEP, BS, LANES), lambda i, n: (0, i, 0, 0)),
                block,
                pl.BlockSpec((8, LANES), lambda i, n: (0, 0)),
                anywhere,
                anywhere,
                anywhere,
                pl.BlockSpec((STEP * BS, LANES), lambda i, n: (i, 0)),
            ],
            out_specs=out_specs,
            scratch_shapes=[
                pltpu.VMEM((3 * RB + 1, BS, LANES), BF16),
                pltpu.SemaphoreType.DMA((3,)),
            ],
        ),
        out_shape=out_shape,
        cost_estimate=pl.CostEstimate(
            flops=2 * RB * BS * SLOTS * BS * LANES, bytes_accessed=20 << 20, transcendentals=0
        ),
        name="sweep_last" if last else "sweep",
    )(index, ham, precond, rhs_unit, z, local, before, after, rhs)


def combine_kernel(own_ref, peer_ref, hi_ref, lo_ref, send_ref, keep_ref):
    both = jnp.concatenate([own_ref[...], peer_ref[...]], axis=1)
    out = jnp.dot(both, hi_ref[...], preferred_element_type=F32)
    out = out + jnp.dot(both, lo_ref[...], preferred_element_type=F32)
    send_ref[...] = out[:, :LANES].astype(BF16)
    keep_ref[...] = out[:, LANES:]


def combine(own, peer, weights, rows_step, offset):
    rows = peer.shape[0]
    hi, lo = weights
    base = offset // rows_step
    row_spec = pl.BlockSpec((rows_step, LANES), lambda i: (i, 0))
    mat = pl.BlockSpec((2 * LANES, 2 * LANES), lambda i: (0, 0))
    return pl.pallas_call(
        combine_kernel,
        grid=(rows // rows_step,),
        in_specs=[pl.BlockSpec((rows_step, LANES), lambda i: (i + base, 0)), row_spec, mat, mat],
        out_specs=[row_spec, row_spec],
        out_shape=[
            jax.ShapeDtypeStruct((rows, LANES), BF16),
            jax.ShapeDtypeStruct((rows, LANES), F32),
        ],
        cost_estimate=pl.CostEstimate(
            flops=2 * rows * 256 * 512, bytes_accessed=rows * LANES * 12, transcendentals=0
        ),
        name="combine",
    )(own, peer, hi, lo)


def fold_kernel(keep1_ref, got1_ref, keep2_ref, got2_ref, send_ref, own_ref):
    top = keep1_ref[...] + got1_ref[...].astype(F32)
    bottom = keep2_ref[...] + got2_ref[...].astype(F32)
    first = lane_ids(top.shape) < GROUP
    send_ref[...] = jnp.where(first, pltpu.roll(top, GROUP, axis=1), bottom).astype(BF16)
    own_ref[...] = jnp.where(first, top, pltpu.roll(bottom, GROUP, axis=1))


def fold(keep1, got1, keep2, got2, rows_step):
    rows = keep1.shape[0]
    spec = pl.BlockSpec((rows_step, LANES), lambda i: (i, 0))
    return pl.pallas_call(
        fold_kernel,
        grid=(rows // rows_step,),
        in_specs=[spec] * 4,
        out_specs=[spec, spec],
        out_shape=[
            jax.ShapeDtypeStruct((rows, LANES), BF16),
            jax.ShapeDtypeStruct((rows, LANES), F32),
        ],
        cost_estimate=pl.CostEstimate(
            flops=rows * LANES * 8, bytes_accessed=rows * LANES * 18, transcendentals=0
        ),
        name="fold",
    )(keep1, got1, keep2, got2)


def finish_kernel(own_a_ref, got_a_ref, own_b_ref, got_b_ref, out_ref):
    unit_a = own_a_ref[...] + got_a_ref[...].astype(F32)
    unit_b = own_b_ref[...] + got_b_ref[...].astype(F32)
    quarter = lane_ids(unit_a.shape) // HALF

    def turn(x, shift):
        return pltpu.roll(x, shift, axis=1)

    def merge(first, second, third, fourth):
        low = jnp.where(quarter == 0, first, second)
        high = jnp.where(quarter == 2, third, fourth)
        return jnp.where(quarter < 2, low, high)

    out_ref[0, 0] = merge(unit_a, turn(unit_b, HALF), turn(unit_a, HALF), turn(unit_b, GROUP))
    out_ref[0, 1] = merge(turn(unit_a, GROUP), turn(unit_b, 96), turn(unit_a, 96), unit_b)


def finish(own_a, got_a, own_b, got_b, rows_step):
    rows = own_a.shape[0]
    spec = pl.BlockSpec((rows_step, LANES), lambda i: (i, 0))
    return pl.pallas_call(
        finish_kernel,
        grid=(rows // rows_step,),
        in_specs=[spec] * 4,
        out_specs=pl.BlockSpec((1, 2, rows_step, LANES), lambda i: (0, 0, i, 0)),
        out_shape=jax.ShapeDtypeStruct((1, 2, rows, LANES), F32),
        name="finish",
    )(own_a, got_a, own_b, got_b)


def moment_weights(owners, orders):
    shape = (2 * LANES, 2 * LANES)
    r = lax.broadcasted_iota(jnp.int32, shape, 0)
    c = lax.broadcasted_iota(jnp.int32, shape, 1)
    owner = jnp.where(r < LANES, owners[0], owners[1])
    point = owner * 2 + (r // GROUP) % 2
    slot = c // GROUP
    order = jnp.where(
        slot < 2,
        jnp.where(slot == 0, orders[0], orders[1]),
        jnp.where(slot == 2, orders[2], orders[3]),
    )
    turns = ((order + 1) * (2 * point + 1)) % (2 * POINTS)
    phase = turns.astype(F32) * (math.pi / POINTS)
    part_in, part_out = (r // HALF) % 2, (c // HALF) % 2
    sine = jnp.where(part_out == 0, -1.0, 1.0) * jnp.sin(phase)
    value = jnp.where(part_in == part_out, jnp.cos(phase), sine) / POINTS
    value = jnp.where(r % HALF == c % HALF, value, 0.0)
    high = lax.reduce_precision(value, 8, 7)
    return high.astype(BF16), (value - high).astype(BF16)


def shards(hamiltonian, columns, counts, precond, rhs):
    row_index = lax.axis_index("row")
    quad_index = lax.axis_index("quad")
    z_at, x_at = quad_index // 2, quad_index % 2

    def swap(x, axis, peer_of):
        size = lax.axis_size(axis)
        return lax.ppermute(x, axis, [(i, peer_of(i)) for i in range(size)])

    def by_pair(i):
        return (((i // 2) ^ 1) * 2) + i % 2

    def by_mirror(i):
        return ((3 - i // 2) * 2) + i % 2

    def by_x(i):
        return i ^ 1

    up = [(i, i + 1) for i in range(15)]
    down = [(i + 1, i) for i in range(15)]

    rhs_a, rhs_b, y_a, y_b = initial(rhs, precond)

    live = jnp.arange(SLOTS)[None, :] < counts[:, None]
    index = jnp.where(live, columns - (row_index - 1) * RB, 3 * RB).reshape(RB * SLOTS)
    lane = jnp.arange(LANES)[None, :]
    theta = 2.0 * jnp.pi * ((quad_index * 2 + lane // GROUP).astype(F32) + 0.5) / POINTS
    z = jnp.concatenate([jnp.cos(theta), jnp.sin(theta), jnp.zeros((6, LANES), F32)], axis=0)

    units = [y_a, y_b]
    rhs_units = [rhs_a, rhs_b]
    grams = [None, None]
    for unit in range(2):
        for it in range(ITERS):
            y = units[unit]
            before = lax.ppermute(y, "row", up)
            after = lax.ppermute(y, "row", down)
            last = it == ITERS - 1
            got = sweep(
                index, hamiltonian, precond, rhs_units[unit], z, y, before, after, rhs, last
            )
            units[unit] = got[0]
            if last:
                grams[unit] = got[1]

    mine, other = quad_index, quad_index ^ 1
    pair, mirror = by_pair(quad_index), by_mirror(quad_index)
    w_pair = moment_weights((mine, pair), (mirror, mirror ^ 1, mine, other))
    w_mirror = moment_weights((mine, mirror), (pair, pair ^ 1, mine, other))

    half_rows = RB * BS // 2
    sums = []
    for unit in range(2):
        flat = units[unit].reshape(RB * BS, LANES)
        got1 = swap(flat[:half_rows], "quad", by_pair)
        got2 = swap(flat[half_rows:], "quad", by_mirror)
        send1, keep1 = combine(flat, got1, w_pair, 512, 0)
        send2, keep2 = combine(flat, got2, w_mirror, 512, half_rows)
        back1 = swap(send1, "quad", by_mirror)
        back2 = swap(send2, "quad", by_pair)
        send3, own = fold(keep1, back1, keep2, back2, 512)
        sums.append((send3, own))

    gram = jnp.concatenate(grams, axis=0)
    for bit in (1, 2, 4, 8):
        gram = gram + swap(gram, "row", lambda i, bit=bit: i ^ bit)
    gram = gram.astype(BF16)
    send_g, keep_g = combine(gram, swap(gram, "quad", by_pair), w_pair, 256, 0)
    gram_sum = keep_g + swap(send_g, "quad", by_mirror).astype(F32)
    gram_got = swap(gram_sum[:, GROUP:].astype(BF16), "quad", by_x)
    blocks = gram_sum[:, :GROUP] + gram_got.astype(F32)
    blocks = blocks.reshape(2, LANES, 2, HALF).transpose(1, 2, 0, 3).reshape(1, LANES, LANES)
    blocks = blocks * (1.0 / math.sqrt(RB * BS * 16))

    got_a = swap(sums[0][0], "quad", by_x)
    got_b = swap(sums[1][0], "quad", by_x)
    moments = finish(sums[0][1], got_a, sums[1][1], got_b, 512)
    return moments.reshape(1, RB * BS, LANES), blocks


def solution(mesh):
    return jax.shard_map(
        shards,
        mesh=mesh,
        in_specs=(
            P("row", None, None),
            P("row", None),
            P("row"),
            P("quad", "row", None, None),
            P("row", None),
        ),
        out_specs=(P("quad", "row", None), P("quad", None, None)),
        check_vma=False,
    )
```

```python
import math

import jax
import jax.numpy as jnp
import numpy as np
from jax import lax
from jax.experimental import pallas as pl
from jax.experimental.pallas import tpu as pltpu
from jax.sharding import PartitionSpec as P

ITERS = 2
MOMENTS = 8
POINTS = 16
BS = 64
SLOTS = 24
RB = 64
LANES = 128
GROUP = 64
HALF = 32
STEP = 8
F32 = jnp.float32
BF16 = jnp.bfloat16


def unit_lanes():
    table = np.zeros((LANES, 4 * LANES), np.float32)
    for unit in range(2):
        for lane in range(LANES):
            part, col = (lane // HALF) % 2, lane % HALF
            src = unit * HALF + col
            table[part * GROUP + src, unit * LANES + lane] = 1.0
            sign = -1.0 if part == 0 else 1.0
            table[(1 - part) * GROUP + src, (2 + unit) * LANES + lane] = sign
    return table


def lane_ids(shape):
    return lax.broadcasted_iota(jnp.int32, shape, len(shape) - 1)


def split_points(top, bottom):
    lane = lane_ids(top.shape) % LANES
    first = lane < GROUP
    zero = jnp.zeros_like(top)
    return jnp.concatenate(
        [
            jnp.where(first, top, zero),
            jnp.where(first, bottom, zero),
            jnp.where(first, zero, top),
            jnp.where(first, zero, bottom),
        ],
        axis=0,
    )


def init_kernel(x_ref, pre_ref, map_ref, rhs_a_ref, rhs_b_ref, y_a_ref, y_b_ref):
    spread = jnp.dot(x_ref[...], map_ref[...], preferred_element_type=F32)
    rhs_a_ref[...] = spread[:, :LANES].astype(BF16).reshape(STEP, BS, LANES)
    rhs_b_ref[...] = spread[:, LANES : 2 * LANES].astype(BF16).reshape(STEP, BS, LANES)
    for b in range(STEP):
        rows = slice(b * BS, (b + 1) * BS)
        right = split_points(spread[rows, : 2 * LANES], spread[rows, 2 * LANES :]).astype(BF16)
        left = jnp.concatenate([pre_ref[0, b], pre_ref[1, b]], axis=1)
        out = jnp.dot(left, right, preferred_element_type=F32)
        y_a_ref[b] = out[:, :LANES].astype(BF16)
        y_b_ref[b] = out[:, LANES:].astype(BF16)


def initial(rhs, precond):
    block = jax.ShapeDtypeStruct((RB, BS, LANES), BF16)
    out_spec = pl.BlockSpec((STEP, BS, LANES), lambda i: (i, 0, 0))
    return pl.pallas_call(
        init_kernel,
        grid=(RB // STEP,),
        in_specs=[
            pl.BlockSpec((STEP * BS, LANES), lambda i: (i, 0)),
            pl.BlockSpec((2, STEP, BS, LANES), lambda i: (0, i, 0, 0)),
            pl.BlockSpec((LANES, 4 * LANES), lambda i: (0, 0)),
        ],
        out_specs=[out_spec] * 4,
        out_shape=[block] * 4,
        compiler_params=pltpu.CompilerParams(vmem_limit_bytes=8 << 20),
        name="initial",
    )(rhs, precond, jnp.asarray(unit_lanes(), BF16))


def rotate_lanes(x):
    lane = lane_ids(x.shape) % GROUP
    up = pltpu.roll(x, LANES - HALF, axis=x.ndim - 1)
    down = pltpu.roll(x, HALF, axis=x.ndim - 1)
    return jnp.where(lane < HALF, -up, down)


def sweep_kernel(
    last, index_ref, ham_ref, pre_ref, rhs_ref, z_ref, local_ref, before_ref, after_ref, x_ref,
    out_ref, *rest,
):
    if last:
        second_ref, gram_ref, held, sems, fresh = rest
    else:
        held, sems = rest
        fresh = out_ref
    step = pl.program_id(0)

    @pl.when(step == 0)
    def _():
        copies = []
        for n, ref in enumerate((before_ref, local_ref, after_ref)):
            copies.append(
                pltpu.make_async_copy(ref, held.at[pl.ds(n * RB, RB)], sems.at[n])
            )
            copies[-1].start()
        held[3 * RB] = jnp.zeros((BS, LANES), BF16)
        if last:
            gram_ref[...] = jnp.zeros_like(gram_ref)
        for copy in copies:
            copy.wait()

    zreal = z_ref[0:1, :]
    zimag = z_ref[1:2, :]
    totals = []
    for b in range(STEP):
        row = step * STEP + b
        right = jnp.concatenate(
            [held[index_ref[row * SLOTS + s]] for s in range(SLOTS)], axis=0
        )
        totals.append(jnp.dot(ham_ref[b], right, preferred_element_type=F32))
    rights = []
    for b in range(STEP):
        current = held[RB + step * STEP + b].astype(F32)
        shifted = zreal * current + zimag * rotate_lanes(current)
        resid = (rhs_ref[b].astype(F32) - (shifted - totals[b])).astype(BF16).astype(F32)
        rights.append(split_points(resid, rotate_lanes(resid)).astype(BF16))
    for b in range(STEP):
        current = held[RB + step * STEP + b].astype(F32)
        left = jnp.concatenate([pre_ref[0, b], pre_ref[1, b]], axis=1)
        fresh[b] = (current + jnp.dot(left, rights[b], preferred_element_type=F32)).astype(BF16)
    if last:
        gram_ref[...] += lax.dot_general(
            x_ref[...],
            fresh[...].reshape(STEP * BS, LANES),
            (((0,), (0,)), ((), ())),
            preferred_element_type=F32,
        )
        steps = pl.num_programs(0)

        @pl.when(step < steps // 2)
        def _():
            out_ref[...] = fresh[...]

        @pl.when(step >= steps // 2)
        def _():
            second_ref[...] = fresh[...]


def sweep(index, ham, precond, rhs_unit, z, local, before, after, rhs, last):
    block = pl.BlockSpec((STEP, BS, LANES), lambda i, n: (i, 0, 0))
    anywhere = pl.BlockSpec(memory_space=pl.ANY)
    scratch = [
        pltpu.VMEM((3 * RB + 1, BS, LANES), BF16),
        pltpu.SemaphoreType.DMA((3,)),
    ]
    if last:
        half = RB // STEP // 2
        out_specs = [
            pl.BlockSpec((STEP, BS, LANES), lambda i, n: (jnp.minimum(i, half - 1), 0, 0)),
            pl.BlockSpec((STEP, BS, LANES), lambda i, n: (jnp.maximum(i - half, 0), 0, 0)),
            pl.BlockSpec((LANES, LANES), lambda i, n: (0, 0)),
        ]
        out_shape = [jax.ShapeDtypeStruct((RB // 2, BS, LANES), BF16)] * 2
        out_shape.append(jax.ShapeDtypeStruct((LANES, LANES), F32))
        scratch.append(pltpu.VMEM((STEP, BS, LANES), BF16))
    else:
        out_specs = [block]
        out_shape = [jax.ShapeDtypeStruct((RB, BS, LANES), BF16)]

    def kernel(*refs):
        sweep_kernel(last, *refs)

    return pl.pallas_call(
        kernel,
        grid_spec=pltpu.PrefetchScalarGridSpec(
            num_scalar_prefetch=1,
            grid=(RB // STEP,),
            in_specs=[
                pl.BlockSpec((STEP, BS, SLOTS * BS), lambda i, n: (i, 0, 0)),
                pl.BlockSpec((2, STEP, BS, LANES), lambda i, n: (0, i, 0, 0)),
                block,
                pl.BlockSpec((8, LANES), lambda i, n: (0, 0)),
                anywhere,
                anywhere,
                anywhere,
                pl.BlockSpec((STEP * BS, LANES), lambda i, n: (i, 0)),
            ],
            out_specs=out_specs,
            scratch_shapes=scratch,
        ),
        out_shape=out_shape,
        cost_estimate=pl.CostEstimate(
            flops=2 * RB * BS * SLOTS * BS * LANES, bytes_accessed=20 << 20, transcendentals=0
        ),
        compiler_params=pltpu.CompilerParams(vmem_limit_bytes=14 << 20),
        name="sweep_last" if last else "sweep",
    )(index, ham, precond, rhs_unit, z, local, before, after, rhs)


def combine_kernel(own_ref, peer_ref, weight_ref, send_ref, keep_ref):
    own, peer = own_ref[...], peer_ref[...]
    both = jnp.concatenate([own, peer, own, peer], axis=1)
    out = jnp.dot(both, weight_ref[...], preferred_element_type=F32)
    send_ref[...] = out[:, :LANES].astype(BF16)
    keep_ref[...] = out[:, LANES:]


def combine(own, peer, weights, rows_step):
    rows = peer.shape[0]
    row_spec = pl.BlockSpec((rows_step, LANES), lambda i: (i, 0))
    return pl.pallas_call(
        combine_kernel,
        grid=(rows // rows_step,),
        in_specs=[row_spec, row_spec, pl.BlockSpec((4 * LANES, 2 * LANES), lambda i: (0, 0))],
        out_specs=[row_spec, row_spec],
        out_shape=[
            jax.ShapeDtypeStruct((rows, LANES), BF16),
            jax.ShapeDtypeStruct((rows, LANES), F32),
        ],
        compiler_params=pltpu.CompilerParams(vmem_limit_bytes=8 << 20),
        cost_estimate=pl.CostEstimate(
            flops=2 * rows * 256 * 512, bytes_accessed=rows * LANES * 12, transcendentals=0
        ),
        name="combine",
    )(own, peer, weights)


def fold_kernel(keep1_ref, got1_ref, keep2_ref, got2_ref, send_ref, own_ref):
    top = keep1_ref[...] + got1_ref[...].astype(F32)
    bottom = keep2_ref[...] + got2_ref[...].astype(F32)
    first = lane_ids(top.shape) < GROUP
    send_ref[...] = jnp.where(first, pltpu.roll(top, GROUP, axis=1), bottom).astype(BF16)
    own_ref[...] = jnp.where(first, top, pltpu.roll(bottom, GROUP, axis=1))


def fold(keep1, got1, keep2, got2, rows_step):
    rows = keep1.shape[0]
    spec = pl.BlockSpec((rows_step, LANES), lambda i: (i, 0))
    return pl.pallas_call(
        fold_kernel,
        grid=(rows // rows_step,),
        in_specs=[spec] * 4,
        out_specs=[spec, spec],
        out_shape=[
            jax.ShapeDtypeStruct((rows, LANES), BF16),
            jax.ShapeDtypeStruct((rows, LANES), F32),
        ],
        cost_estimate=pl.CostEstimate(
            flops=rows * LANES * 8, bytes_accessed=rows * LANES * 18, transcendentals=0
        ),
        compiler_params=pltpu.CompilerParams(vmem_limit_bytes=10 << 20),
        name="fold",
    )(keep1, got1, keep2, got2)


def finish_kernel(own_a_ref, got_a_ref, own_b_ref, got_b_ref, out_ref):
    unit_a = own_a_ref[...] + got_a_ref[...].astype(F32)
    unit_b = own_b_ref[...] + got_b_ref[...].astype(F32)
    quarter = lane_ids(unit_a.shape) // HALF

    def turn(x, shift):
        return pltpu.roll(x, shift, axis=1)

    def merge(first, second, third, fourth):
        low = jnp.where(quarter == 0, first, second)
        high = jnp.where(quarter == 2, third, fourth)
        return jnp.where(quarter < 2, low, high)

    out_ref[0, 0] = merge(unit_a, turn(unit_b, HALF), turn(unit_a, HALF), turn(unit_b, GROUP))
    out_ref[0, 1] = merge(turn(unit_a, GROUP), turn(unit_b, 96), turn(unit_a, 96), unit_b)


def finish(own_a, got_a, own_b, got_b, rows_step):
    rows = own_a.shape[0]
    spec = pl.BlockSpec((rows_step, LANES), lambda i: (i, 0))
    return pl.pallas_call(
        finish_kernel,
        grid=(rows // rows_step,),
        in_specs=[spec] * 4,
        out_specs=pl.BlockSpec((1, 2, rows_step, LANES), lambda i: (0, 0, i, 0)),
        out_shape=jax.ShapeDtypeStruct((1, 2, rows, LANES), F32),
        compiler_params=pltpu.CompilerParams(vmem_limit_bytes=10 << 20),
        name="finish",
    )(own_a, got_a, own_b, got_b)


def moment_weights(owners, orders):
    shape = (2 * LANES, 2 * LANES)
    r = lax.broadcasted_iota(jnp.int32, shape, 0)
    c = lax.broadcasted_iota(jnp.int32, shape, 1)
    owner = jnp.where(r < LANES, owners[0], owners[1])
    point = owner * 2 + (r // GROUP) % 2
    slot = c // GROUP
    order = jnp.where(
        slot < 2,
        jnp.where(slot == 0, orders[0], orders[1]),
        jnp.where(slot == 2, orders[2], orders[3]),
    )
    turns = ((order + 1) * (2 * point + 1)) % (2 * POINTS)
    phase = turns.astype(F32) * (math.pi / POINTS)
    part_in, part_out = (r // HALF) % 2, (c // HALF) % 2
    sine = jnp.where(part_out == 0, -1.0, 1.0) * jnp.sin(phase)
    value = jnp.where(part_in == part_out, jnp.cos(phase), sine) / POINTS
    value = jnp.where(r % HALF == c % HALF, value, 0.0)
    high = lax.reduce_precision(value, 8, 7)
    return jnp.concatenate([high.astype(BF16), (value - high).astype(BF16)], axis=0)


def shards(hamiltonian, columns, counts, precond, rhs):
    row_index = lax.axis_index("row")
    quad_index = lax.axis_index("quad")
    z_at, x_at = quad_index // 2, quad_index % 2

    def swap(x, axis, peer_of):
        size = lax.axis_size(axis)
        return lax.ppermute(x, axis, [(i, peer_of(i)) for i in range(size)])

    def by_pair(i):
        return (((i // 2) ^ 1) * 2) + i % 2

    def by_mirror(i):
        return ((3 - i // 2) * 2) + i % 2

    def by_x(i):
        return i ^ 1

    up = [(i, i + 1) for i in range(15)]
    down = [(i + 1, i) for i in range(15)]

    rhs_a, rhs_b, y_a, y_b = initial(rhs, precond)

    live = jnp.arange(SLOTS)[None, :] < counts[:, None]
    index = jnp.where(live, columns - (row_index - 1) * RB, 3 * RB).reshape(RB * SLOTS)
    lane = jnp.arange(LANES)[None, :]
    theta = 2.0 * jnp.pi * ((quad_index * 2 + lane // GROUP).astype(F32) + 0.5) / POINTS
    z = jnp.concatenate([jnp.cos(theta), jnp.sin(theta), jnp.zeros((6, LANES), F32)], axis=0)

    units = [y_a, y_b]
    rhs_units = [rhs_a, rhs_b]
    grams = [None, None]
    for unit in range(2):
        for it in range(ITERS):
            y = units[unit]
            before = lax.ppermute(y, "row", up)
            after = lax.ppermute(y, "row", down)
            last = it == ITERS - 1
            got = sweep(
                index, hamiltonian, precond, rhs_units[unit], z, y, before, after, rhs, last
            )
            units[unit] = got[0]
            if last:
                units[unit] = got[:2]
                grams[unit] = got[2]

    mine, other = quad_index, quad_index ^ 1
    pair, mirror = by_pair(quad_index), by_mirror(quad_index)
    w_pair = moment_weights((mine, pair), (mirror, mirror ^ 1, mine, other))
    w_mirror = moment_weights((mine, mirror), (pair, pair ^ 1, mine, other))

    half_rows = RB * BS // 2
    sums = []
    for unit in range(2):
        top, bottom = (part.reshape(half_rows, LANES) for part in units[unit])
        got1 = swap(top, "quad", by_pair)
        got2 = swap(bottom, "quad", by_mirror)
        send1, keep1 = combine(top, got1, w_pair, 1024)
        send2, keep2 = combine(bottom, got2, w_mirror, 1024)
        back1 = swap(send1, "quad", by_mirror)
        back2 = swap(send2, "quad", by_pair)
        send3, own = fold(keep1, back1, keep2, back2, 1024)
        sums.append((send3, own))

    gram = jnp.concatenate(grams, axis=0)
    for bit in (1, 2, 4, 8):
        gram = gram + swap(gram, "row", lambda i, bit=bit: i ^ bit)
    gram = gram.astype(BF16)
    send_g, keep_g = combine(gram, swap(gram, "quad", by_pair), w_pair, 256)
    gram_sum = keep_g + swap(send_g, "quad", by_mirror).astype(F32)
    gram_got = swap(gram_sum[:, GROUP:].astype(BF16), "quad", by_x)
    blocks = gram_sum[:, :GROUP] + gram_got.astype(F32)
    blocks = blocks.reshape(2, LANES, 2, HALF).transpose(1, 2, 0, 3).reshape(1, LANES, LANES)
    blocks = blocks * (1.0 / math.sqrt(RB * BS * 16))

    got_a = swap(sums[0][0], "quad", by_x)
    got_b = swap(sums[1][0], "quad", by_x)
    moments = finish(sums[0][1], got_a, sums[1][1], got_b, 512)
    return moments.reshape(1, RB * BS, LANES), blocks


def solution(mesh):
    return jax.shard_map(
        shards,
        mesh=mesh,
        in_specs=(
            P("row", None, None),
            P("row", None),
            P("row"),
            P("quad", "row", None, None),
            P("row", None),
        ),
        out_specs=(P("quad", "row", None), P("quad", None, None)),
        check_vma=False,
    )
```

```python
import math

import jax
import jax.numpy as jnp
import numpy as np
from jax import lax
from jax.experimental import pallas as pl
from jax.experimental.pallas import tpu as pltpu
from jax.sharding import PartitionSpec as P

ITERS = 2
POINTS = 16
BS = 64
SLOTS = 24
RB = 64
LANES = 128
GROUP = 64
HALF = 32
STEP = 8
F32 = jnp.float32
BF16 = jnp.bfloat16


def unit_lanes(points):
    table = np.zeros((points * LANES, 2 * LANES), np.float32)
    for unit in range(2):
        for lane in range(LANES):
            point, part, col = lane // GROUP, (lane // HALF) % 2, lane % HALF
            src = (point % points) * LANES + part * GROUP + unit * HALF + col
            table[src, unit * LANES + lane] = 1.0
    return table


def lane_ids(shape):
    return lax.broadcasted_iota(jnp.int32, shape, len(shape) - 1)


def split_points(top, bottom):
    lane = lane_ids(top.shape) % LANES
    first = lane < GROUP
    zero = jnp.zeros_like(top)
    return jnp.concatenate(
        [
            jnp.where(first, top, zero),
            jnp.where(first, bottom, zero),
            jnp.where(first, zero, top),
            jnp.where(first, zero, bottom),
        ],
        axis=0,
    )


def init_kernel(x_ref, pre_ref, map_ref, y_a_ref, y_b_ref):
    firsts, seconds = [], []
    for b in range(STEP):
        x = x_ref[b * BS : (b + 1) * BS].astype(F32)
        turned = pltpu.roll(x, GROUP, axis=1)
        turned = jnp.where(lane_ids(x.shape) < GROUP, -turned, turned)
        right = jnp.concatenate([x, turned], axis=0).astype(BF16)
        left = jnp.concatenate([pre_ref[0, b], pre_ref[1, b]], axis=0)
        out = jnp.dot(left, right, preferred_element_type=F32).astype(BF16)
        firsts.append(out[:BS])
        seconds.append(out[BS:])
    both = jnp.concatenate(
        [jnp.concatenate(firsts, axis=0), jnp.concatenate(seconds, axis=0)], axis=1
    )
    out = jnp.dot(both, map_ref[...], preferred_element_type=F32).astype(BF16)
    y_a_ref[...] = out[:, :LANES].reshape(STEP, BS, LANES)
    y_b_ref[...] = out[:, LANES:].reshape(STEP, BS, LANES)


def initial(rhs, precond):
    block = jax.ShapeDtypeStruct((RB, BS, LANES), BF16)
    out_spec = pl.BlockSpec((STEP, BS, LANES), lambda i: (i, 0, 0))
    return pl.pallas_call(
        init_kernel,
        grid=(RB // STEP,),
        in_specs=[
            pl.BlockSpec((STEP * BS, LANES), lambda i: (i, 0)),
            pl.BlockSpec((2, STEP, BS, LANES), lambda i: (0, i, 0, 0)),
            pl.BlockSpec((2 * LANES, 2 * LANES), lambda i: (0, 0)),
        ],
        out_specs=[out_spec] * 2,
        out_shape=[block] * 2,
        name="initial",
    )(rhs, precond, jnp.asarray(unit_lanes(2), BF16))


def spread_kernel(x_ref, map_ref, coef_ref, rhs_a_ref, rhs_b_ref, weight_ref):
    out = jnp.dot(x_ref[...], map_ref[...], preferred_element_type=F32).astype(BF16)
    rhs_a_ref[...] = out[:, :LANES].reshape(rhs_a_ref.shape)
    rhs_b_ref[...] = out[:, LANES:].reshape(rhs_b_ref.shape)
    shape = (GROUP, 2 * LANES)
    r = lax.broadcasted_iota(jnp.int32, shape, 0)
    c = lax.broadcasted_iota(jnp.int32, shape, 1)
    same = r % HALF == c % HALF
    straight = same & ((r // HALF) == (c // HALF) % 2)
    crossed = same & ((r // HALF) != (c // HALF) % 2)
    for point in range(4):
        rows = coef_ref[0, point * 8 : point * 8 + 8]
        cosine, sine = rows[0:1, :], rows[1:2, :]
        value = jnp.where(straight, cosine, jnp.where(crossed, sine, 0.0))
        high = value.astype(BF16)
        weight_ref[0, point * GROUP : (point + 1) * GROUP] = high
        weight_ref[0, (4 + point) * GROUP : (5 + point) * GROUP] = (
            value - high.astype(F32)
        ).astype(BF16)


def spread(rhs, coefs):
    block = jax.ShapeDtypeStruct((RB, BS, LANES), BF16)
    out_spec = pl.BlockSpec((RB // 4, BS, LANES), lambda i: (i, 0, 0))
    return pl.pallas_call(
        spread_kernel,
        grid=(4,),
        in_specs=[
            pl.BlockSpec((RB // 4 * BS, LANES), lambda i: (i, 0)),
            pl.BlockSpec((LANES, 2 * LANES), lambda i: (0, 0)),
            pl.BlockSpec((1, 32, 2 * LANES), lambda i: (i, 0, 0)),
        ],
        out_specs=[out_spec, out_spec, pl.BlockSpec((1, 512, 256), lambda i: (i, 0, 0))],
        out_shape=[block, block, jax.ShapeDtypeStruct((4, 512, 256), BF16)],
        compiler_params=pltpu.CompilerParams(vmem_limit_bytes=14 << 20),
        cost_estimate=pl.CostEstimate(
            flops=2 * RB * BS * LANES * 256, bytes_accessed=3 << 20, transcendentals=0
        ),
        name="spread",
    )(rhs, jnp.asarray(unit_lanes(1), BF16), coefs)


def rotate_lanes(x):
    lane = lane_ids(x.shape) % GROUP
    up = pltpu.roll(x, LANES - HALF, axis=x.ndim - 1)
    down = pltpu.roll(x, HALF, axis=x.ndim - 1)
    return jnp.where(lane < HALF, -up, down)


def sweep_kernel(
    last, index_ref, ham_ref, pre_ref, rhs_ref, z_ref, local_ref, near_ref, far_ref, x_ref,
    out_ref, *rest,
):
    if last:
        second_ref, gram_ref, held, sems, ham_buf, pre_buf, fresh = rest
    else:
        held, sems, ham_buf, pre_buf = rest
        fresh = out_ref
    step = pl.program_id(0)
    steps = pl.num_programs(0)
    slot = step % 2

    def fetch(at, to):
        blocks = pl.ds(pl.multiple_of(at * STEP, STEP), STEP)
        return (
            pltpu.make_async_copy(ham_ref.at[blocks], ham_buf.at[to], sems.at[3 + to]),
            pltpu.make_async_copy(pre_ref.at[:, blocks], pre_buf.at[to], sems.at[5 + to]),
        )

    @pl.when(step == 0)
    def _():
        copies = []
        near_at = index_ref[RB * SLOTS]
        places = (near_at, RB, 2 * RB - near_at)
        for n, ref in enumerate((near_ref, local_ref, far_ref)):
            place = pl.multiple_of(places[n], RB)
            copies.append(pltpu.make_async_copy(ref, held.at[pl.ds(place, RB)], sems.at[n]))
            copies[-1].start()
        for copy in fetch(0, 0):
            copy.start()
        held[3 * RB] = jnp.zeros((BS, LANES), BF16)
        if last:
            gram_ref[...] = jnp.zeros_like(gram_ref)
        for copy in copies:
            copy.wait()

    @pl.when(step + 1 < steps)
    def _():
        for copy in fetch(step + 1, 1 - slot):
            copy.start()

    for copy in fetch(step, slot):
        copy.wait()

    zreal = z_ref[0:1, :]
    zimag = z_ref[1:2, :]
    totals = []
    for b in range(STEP):
        row = step * STEP + b
        right = jnp.concatenate(
            [held[index_ref[row * SLOTS + s]] for s in range(SLOTS)], axis=0
        )
        totals.append(jnp.dot(ham_buf[slot, b], right, preferred_element_type=F32))
    rights = []
    for b in range(STEP):
        current = held[RB + step * STEP + b].astype(F32)
        shifted = zreal * current + zimag * rotate_lanes(current)
        resid = (rhs_ref[b].astype(F32) - (shifted - totals[b])).astype(BF16).astype(F32)
        rights.append(split_points(resid, rotate_lanes(resid)).astype(BF16))
    for b in range(STEP):
        current = held[RB + step * STEP + b].astype(F32)
        left = jnp.concatenate([pre_buf[slot, 0, b], pre_buf[slot, 1, b]], axis=1)
        fresh[b] = (current + jnp.dot(left, rights[b], preferred_element_type=F32)).astype(BF16)
    if last:
        gram_ref[...] += lax.dot_general(
            x_ref[...],
            fresh[...].reshape(STEP * BS, LANES),
            (((0,), (0,)), ((), ())),
            preferred_element_type=F32,
        )

        @pl.when(step < steps // 2)
        def _():
            out_ref[...] = fresh[...]

        @pl.when(step >= steps // 2)
        def _():
            second_ref[...] = fresh[...]


def sweep(index, ham, precond, rhs_unit, z, local, near, far, rhs, last):
    block = pl.BlockSpec((STEP, BS, LANES), lambda i, n: (i, 0, 0))
    anywhere = pl.BlockSpec(memory_space=pl.ANY)
    in_hbm = pl.BlockSpec(memory_space=pltpu.MemorySpace.HBM)
    scratch = [
        pltpu.VMEM((3 * RB + 1, BS, LANES), BF16),
        pltpu.SemaphoreType.DMA((7,)),
        pltpu.VMEM((2, STEP, BS, SLOTS * BS), BF16),
        pltpu.VMEM((2, 2, STEP, BS, LANES), BF16),
    ]
    if last:
        half = RB // STEP // 2
        out_specs = [
            pl.BlockSpec((STEP, BS, LANES), lambda i, n: (jnp.minimum(i, half - 1), 0, 0)),
            pl.BlockSpec((STEP, BS, LANES), lambda i, n: (jnp.maximum(i - half, 0), 0, 0)),
            pl.BlockSpec((LANES, LANES), lambda i, n: (0, 0)),
        ]
        out_shape = [jax.ShapeDtypeStruct((RB // 2, BS, LANES), BF16)] * 2
        out_shape.append(jax.ShapeDtypeStruct((LANES, LANES), F32))
        scratch.append(pltpu.VMEM((STEP, BS, LANES), BF16))
    else:
        out_specs = [block]
        out_shape = [jax.ShapeDtypeStruct((RB, BS, LANES), BF16)]

    def kernel(*refs):
        sweep_kernel(last, *refs)

    return pl.pallas_call(
        kernel,
        grid_spec=pltpu.PrefetchScalarGridSpec(
            num_scalar_prefetch=1,
            grid=(RB // STEP,),
            in_specs=[
                in_hbm,
                in_hbm,
                block,
                pl.BlockSpec((8, LANES), lambda i, n: (0, 0)),
                anywhere,
                anywhere,
                anywhere,
                pl.BlockSpec((STEP * BS, LANES), lambda i, n: (i, 0)),
            ],
            out_specs=out_specs,
            scratch_shapes=scratch,
        ),
        out_shape=out_shape,
        cost_estimate=pl.CostEstimate(
            flops=2 * RB * BS * SLOTS * BS * LANES, bytes_accessed=20 << 20, transcendentals=0
        ),
        compiler_params=pltpu.CompilerParams(vmem_limit_bytes=48 << 20),
        name="sweep_last" if last else "sweep",
    )(index, ham, precond, rhs_unit, z, local, near, far, rhs)


def combine_kernel(own_ref, peer_ref, weight_ref, send_ref, keep_ref):
    own, peer = own_ref[...], peer_ref[...]
    both = jnp.concatenate([own, peer, own, peer], axis=1)
    out = jnp.dot(both, weight_ref[0], preferred_element_type=F32)
    send_ref[...] = out[:, :LANES].astype(BF16)
    keep_ref[...] = out[:, LANES:]


def combine(own, peer, weights, which, rows_step):
    rows = peer.shape[0]
    row_spec = pl.BlockSpec((rows_step, LANES), lambda i: (i, 0))
    return pl.pallas_call(
        combine_kernel,
        grid=(rows // rows_step,),
        in_specs=[row_spec, row_spec, pl.BlockSpec((1, 4 * LANES, 2 * LANES), lambda i: (which, 0, 0))],
        out_specs=[row_spec, row_spec],
        out_shape=[
            jax.ShapeDtypeStruct((rows, LANES), BF16),
            jax.ShapeDtypeStruct((rows, LANES), F32),
        ],
        compiler_params=pltpu.CompilerParams(vmem_limit_bytes=8 << 20),
        cost_estimate=pl.CostEstimate(
            flops=2 * rows * 256 * 512, bytes_accessed=rows * LANES * 12, transcendentals=0
        ),
        name="combine",
    )(own, peer, weights)


def fold_kernel(keep1_ref, got1_ref, keep2_ref, got2_ref, send_ref, own_ref):
    top = keep1_ref[...] + got1_ref[...].astype(F32)
    bottom = keep2_ref[...] + got2_ref[...].astype(F32)
    first = lane_ids(top.shape) < GROUP
    send_ref[...] = jnp.where(first, pltpu.roll(top, GROUP, axis=1), bottom).astype(BF16)
    own_ref[...] = jnp.where(first, top, pltpu.roll(bottom, GROUP, axis=1))


def fold(keep1, got1, keep2, got2, rows, shift):
    step = 1024
    spec = pl.BlockSpec((step, LANES), lambda i: (i, 0))
    late = pl.BlockSpec((step, LANES), lambda i: (i + shift // step, 0))
    return pl.pallas_call(
        fold_kernel,
        grid=(rows // step,),
        in_specs=[spec, spec, late, late],
        out_specs=[spec, spec],
        out_shape=[
            jax.ShapeDtypeStruct((rows, LANES), BF16),
            jax.ShapeDtypeStruct((rows, LANES), F32),
        ],
        compiler_params=pltpu.CompilerParams(vmem_limit_bytes=10 << 20),
        cost_estimate=pl.CostEstimate(
            flops=rows * LANES * 8, bytes_accessed=rows * LANES * 18, transcendentals=0
        ),
        name="fold",
    )(keep1, got1, keep2, got2)


def finish_kernel(own1_ref, got1_ref, own2_ref, got2_ref, own_b_ref, got_b_ref, out_ref):
    def turn(x, shift):
        return pltpu.roll(x, shift, axis=1)

    late = pl.program_id(0) >= pl.num_programs(0) // 2
    top_a = own1_ref[...] + got1_ref[...].astype(F32)
    top_a = jnp.where(late, turn(top_a, GROUP), top_a)
    bottom_a = own2_ref[...] + got2_ref[...].astype(F32)
    bottom_a = jnp.where(late, turn(bottom_a, GROUP), bottom_a)
    unit_b = own_b_ref[...] + got_b_ref[...].astype(F32)
    quarter = lane_ids(unit_b.shape) // HALF

    def merge(first, second, third, fourth):
        low = jnp.where(quarter == 0, first, second)
        high = jnp.where(quarter == 2, third, fourth)
        return jnp.where(quarter < 2, low, high)

    out_ref[0, 0] = merge(top_a, turn(unit_b, HALF), turn(top_a, HALF), turn(unit_b, GROUP))
    out_ref[0, 1] = merge(bottom_a, turn(unit_b, 96), turn(bottom_a, HALF), unit_b)


def finish(own1, got1, own2, got2, own_b, got_b, step):
    rows = own_b.shape[0]
    half = rows // 2 // step
    spec = pl.BlockSpec((step, LANES), lambda i: (i, 0))
    spec_a = pl.BlockSpec((step, LANES), lambda i: (i % half, 0))
    return pl.pallas_call(
        finish_kernel,
        grid=(rows // step,),
        in_specs=[spec_a] * 4 + [spec] * 2,
        out_specs=pl.BlockSpec((1, 2, step, LANES), lambda i: (0, 0, i, 0)),
        out_shape=jax.ShapeDtypeStruct((1, 2, rows, LANES), F32),
        compiler_params=pltpu.CompilerParams(vmem_limit_bytes=10 << 20),
        name="finish",
    )(own1, got1, own2, got2, own_b, got_b)


def moment_coefs(plans):
    lane = lax.broadcasted_iota(jnp.int32, (1, 32, 2 * LANES), 2)
    line = lax.broadcasted_iota(jnp.int32, (1, 32, 2 * LANES), 1)
    slot, point, kind = lane // GROUP, line // 8, line % 8
    tables = []
    for owners, orders in plans:
        owner = jnp.where(point < 2, owners[0], owners[1])
        low = jnp.where(slot == 0, orders[0], orders[1])
        high = jnp.where(slot == 2, orders[2], orders[3])
        order = jnp.where(slot < 2, low, high)
        turns = ((order + 1) * (2 * (owner * 2 + point % 2) + 1)) % (2 * POINTS)
        sign = jnp.where((lane // HALF) % 2 == 0, -1.0, 1.0)
        phase = turns.astype(F32) * (math.pi / POINTS)
        quarter = jnp.where(kind == 0, math.pi / 2, 0.0)
        tables.append(jnp.where(kind == 0, 1.0, sign) * jnp.sin(phase + quarter) / POINTS)
    return jnp.concatenate(tables, axis=0)


def step(hamiltonian, columns, counts, precond, rhs):
    row_index = lax.axis_index("row")
    quad_index = lax.axis_index("quad")

    def swap(x, axis, peer_of):
        peers = [(i, peer_of(i)) for i in range(lax.axis_size(axis))]
        return lax.ppermute(x, axis, [(i, j) for i, j in peers if 0 <= j < len(peers)])

    def by_pair(i):
        return (((i // 2) ^ 1) * 2) + i % 2

    def by_mirror(i):
        return ((3 - i // 2) * 2) + i % 2

    def by_x(i):
        return i ^ 1

    def near_row(i):
        return i ^ 1

    def far_row(i):
        return i + 1 if i % 2 else i - 1

    units = list(initial(rhs, precond))

    live = jnp.arange(SLOTS)[None, :] < counts[:, None]
    index = jnp.where(live, columns - (row_index - 1) * RB, 3 * RB).reshape(RB * SLOTS)
    near_at = jnp.where(row_index % 2 == 1, 0, 2 * RB)
    index = jnp.concatenate([index, jnp.full((LANES,), near_at, jnp.int32)])
    lane = jnp.arange(LANES)[None, :]
    theta = 2.0 * jnp.pi * ((quad_index * 2 + lane // GROUP).astype(F32) + 0.5) / POINTS
    z = jnp.concatenate([jnp.cos(theta), jnp.sin(theta), jnp.zeros((6, LANES), F32)], axis=0)

    mine, other = quad_index, quad_index ^ 1
    pair, mirror = by_pair(quad_index), by_mirror(quad_index)
    coefs = moment_coefs(
        (
            ((mine, pair), (other, mirror ^ 1, mine, mirror)),
            ((mine, mirror), (other, pair ^ 1, mine, pair)),
            ((mine, pair), (mirror, mirror ^ 1, mine, other)),
            ((mine, mirror), (pair, pair ^ 1, mine, other)),
        ),
    )
    *rhs_units, weights = spread(rhs, coefs)

    grams = [None, None]
    for it in range(ITERS):
        for unit in range(2):
            y = units[unit]
            far = swap(y, "row", far_row)
            near = swap(y, "row", near_row)
            last = it == ITERS - 1
            got = sweep(index, hamiltonian, precond, rhs_units[unit], z, y, near, far, rhs, last)
            units[unit] = got[0]
            if last:
                units[unit] = got[:2]
                grams[unit] = got[2]

    half_rows = RB * BS // 2

    def first_stage(unit):
        top, bottom = (part.reshape(half_rows, LANES) for part in units[unit])
        got1 = swap(top, "quad", by_pair)
        got2 = swap(bottom, "quad", by_mirror)
        out1 = combine(top, got1, weights, 2 * unit, 1024)
        return out1 + combine(bottom, got2, weights, 2 * unit + 1, 1024)

    send_a1, keep_a1, send_a2, keep_a2 = first_stage(0)
    got_a1 = swap(send_a1, "quad", by_x)
    got_a2 = swap(send_a2, "quad", by_x)
    quarter = half_rows // 2
    send_a1, own_a1 = fold(keep_a1, got_a1, keep_a1, got_a1, quarter, quarter)
    send_a2, own_a2 = fold(keep_a2, got_a2, keep_a2, got_a2, quarter, quarter)

    send_b1, keep_b1, send_b2, keep_b2 = first_stage(1)
    got_b1 = swap(send_b1, "quad", by_mirror)
    got_b2 = swap(send_b2, "quad", by_pair)
    send_b, own_b = fold(keep_b1, got_b1, keep_b2, got_b2, half_rows, 0)

    gram = jnp.concatenate(grams, axis=0)
    for bit in (1, 2, 4, 8):
        gram = gram + swap(gram, "row", lambda i, bit=bit: i ^ bit)
    gram = gram.astype(BF16)
    send_g, keep_g = combine(gram, swap(gram, "quad", by_pair), weights, 2, 256)
    gram_sum = keep_g + swap(send_g, "quad", by_mirror).astype(F32)
    gram_got = swap(gram_sum[:, GROUP:].astype(BF16), "quad", by_x)
    blocks = gram_sum[:, :GROUP] + gram_got.astype(F32)
    blocks = blocks.reshape(2, LANES, 2, HALF).transpose(1, 2, 0, 3).reshape(1, LANES, LANES)
    blocks = blocks * (1.0 / math.sqrt(RB * BS * 16))

    got_a1 = swap(send_a1, "quad", by_mirror)
    got_a2 = swap(send_a2, "quad", by_pair)
    got_b = swap(send_b, "quad", by_x)
    moments = finish(own_a1, got_a1, own_a2, got_a2, own_b, got_b, 512)
    return moments.reshape(1, RB * BS, LANES), blocks


def solution(mesh):
    return jax.shard_map(
        step,
        mesh=mesh,
        in_specs=(
            P("row", None, None),
            P("row", None),
            P("row"),
            P("quad", "row", None, None),
            P("row", None),
        ),
        out_specs=(P("quad", "row", None), P("quad", None, None)),
        check_vma=False,
    )
```

```python
import math

import jax
import jax.numpy as jnp
import numpy as np
from jax import lax
from jax.experimental import pallas as pl
from jax.experimental.pallas import tpu as pltpu
from jax.sharding import PartitionSpec as P

ITERS = 2
POINTS = 16
BS = 64
SLOTS = 24
RB = 64
LANES = 128
GROUP = 64
HALF = 32
STEP = 8
F32 = jnp.float32
BF16 = jnp.bfloat16


def unit_lanes(points):
    table = np.zeros((points * LANES, 2 * LANES), np.float32)
    for unit in range(2):
        for lane in range(LANES):
            point, part, col = lane // GROUP, (lane // HALF) % 2, lane % HALF
            src = (point % points) * LANES + part * GROUP + unit * HALF + col
            table[src, unit * LANES + lane] = 1.0
    return table


def lane_ids(shape):
    return lax.broadcasted_iota(jnp.int32, shape, len(shape) - 1)


def split_points(top, bottom):
    lane = lane_ids(top.shape) % LANES
    first = lane < GROUP
    zero = jnp.zeros_like(top)
    return jnp.concatenate(
        [
            jnp.where(first, top, zero),
            jnp.where(first, bottom, zero),
            jnp.where(first, zero, top),
            jnp.where(first, zero, bottom),
        ],
        axis=0,
    )


def init_kernel(x_ref, pre_ref, map_ref, y_a_ref, y_b_ref):
    rights = []
    for b in range(STEP):
        x = x_ref[b * BS : (b + 1) * BS].astype(F32)
        turned = pltpu.roll(x, GROUP, axis=1)
        turned = jnp.where(lane_ids(x.shape) < GROUP, -turned, turned)
        rights.append(jnp.concatenate([x, turned], axis=0).astype(BF16))
    outs = []
    for b in range(STEP):
        left = jnp.concatenate([pre_ref[0, b], pre_ref[1, b]], axis=0)
        outs.append(jnp.dot(left, rights[b], preferred_element_type=F32))
    outs = [out.astype(BF16) for out in outs]
    firsts = [out[:BS] for out in outs]
    seconds = [out[BS:] for out in outs]
    both = jnp.concatenate(
        [jnp.concatenate(firsts, axis=0), jnp.concatenate(seconds, axis=0)], axis=1
    )
    out = jnp.dot(both, map_ref[...], preferred_element_type=F32).astype(BF16)
    y_a_ref[...] = out[:, :LANES].reshape(STEP, BS, LANES)
    y_b_ref[...] = out[:, LANES:].reshape(STEP, BS, LANES)


def initial(rhs, precond):
    block = jax.ShapeDtypeStruct((RB, BS, LANES), BF16)
    out_spec = pl.BlockSpec((STEP, BS, LANES), lambda i: (i, 0, 0))
    return pl.pallas_call(
        init_kernel,
        grid=(RB // STEP,),
        in_specs=[
            pl.BlockSpec((STEP * BS, LANES), lambda i: (i, 0)),
            pl.BlockSpec((2, STEP, BS, LANES), lambda i: (0, i, 0, 0)),
            pl.BlockSpec((2 * LANES, 2 * LANES), lambda i: (0, 0)),
        ],
        out_specs=[out_spec] * 2,
        out_shape=[block] * 2,
        name="initial",
    )(rhs, precond, jnp.asarray(unit_lanes(2), BF16))


def spread_kernel(x_ref, map_ref, coef_ref, rhs_a_ref, rhs_b_ref, weight_ref):
    out = jnp.dot(x_ref[...], map_ref[...], preferred_element_type=F32).astype(BF16)
    rhs_a_ref[...] = out[:, :LANES].reshape(rhs_a_ref.shape)
    rhs_b_ref[...] = out[:, LANES:].reshape(rhs_b_ref.shape)
    shape = (GROUP, 2 * LANES)
    r = lax.broadcasted_iota(jnp.int32, shape, 0)
    c = lax.broadcasted_iota(jnp.int32, shape, 1)
    same = r % HALF == c % HALF
    straight = same & ((r // HALF) == (c // HALF) % 2)
    crossed = same & ((r // HALF) != (c // HALF) % 2)
    for point in range(4):
        rows = coef_ref[0, point * 8 : point * 8 + 8]
        cosine, sine = rows[0:1, :], rows[1:2, :]
        value = jnp.where(straight, cosine, jnp.where(crossed, sine, 0.0))
        high = value.astype(BF16)
        weight_ref[0, point * GROUP : (point + 1) * GROUP] = high
        weight_ref[0, (4 + point) * GROUP : (5 + point) * GROUP] = (
            value - high.astype(F32)
        ).astype(BF16)


def spread(rhs, coefs):
    block = jax.ShapeDtypeStruct((RB, BS, LANES), BF16)
    out_spec = pl.BlockSpec((RB // 4, BS, LANES), lambda i: (i, 0, 0))
    return pl.pallas_call(
        spread_kernel,
        grid=(4,),
        in_specs=[
            pl.BlockSpec((RB // 4 * BS, LANES), lambda i: (i, 0)),
            pl.BlockSpec((LANES, 2 * LANES), lambda i: (0, 0)),
            pl.BlockSpec((1, 32, 2 * LANES), lambda i: (i, 0, 0)),
        ],
        out_specs=[out_spec, out_spec, pl.BlockSpec((1, 512, 256), lambda i: (i, 0, 0))],
        out_shape=[block, block, jax.ShapeDtypeStruct((4, 512, 256), BF16)],
        compiler_params=pltpu.CompilerParams(vmem_limit_bytes=14 << 20),
        cost_estimate=pl.CostEstimate(
            flops=2 * RB * BS * LANES * 256, bytes_accessed=3 << 20, transcendentals=0
        ),
        name="spread",
    )(rhs, jnp.asarray(unit_lanes(1), BF16), coefs)


def rotate_lanes(x):
    lane = lane_ids(x.shape) % GROUP
    up = pltpu.roll(x, LANES - HALF, axis=x.ndim - 1)
    down = pltpu.roll(x, HALF, axis=x.ndim - 1)
    return jnp.where(lane < HALF, -up, down)


def sweep_kernel(
    last, index_ref, ham_ref, pre_ref, rhs_ref, z_ref, local_ref, near_ref, far_ref,
    out_ref, *rest,
):
    if last:
        second_ref, held, sems, ham_buf, pre_buf, fresh = rest
    else:
        held, sems, ham_buf, pre_buf = rest
        fresh = out_ref
    step = pl.program_id(0)
    steps = pl.num_programs(0)
    slot = step % 2

    def fetch(at, to):
        blocks = pl.ds(pl.multiple_of(at * STEP, STEP), STEP)
        return (
            pltpu.make_async_copy(ham_ref.at[blocks], ham_buf.at[to], sems.at[3 + to]),
            pltpu.make_async_copy(pre_ref.at[:, blocks], pre_buf.at[to], sems.at[5 + to]),
        )

    @pl.when(step == 0)
    def _():
        copies = []
        near_at = index_ref[RB * SLOTS]
        places = (near_at, RB, 2 * RB - near_at)
        for n, ref in enumerate((near_ref, local_ref, far_ref)):
            place = pl.multiple_of(places[n], RB)
            copies.append(pltpu.make_async_copy(ref, held.at[pl.ds(place, RB)], sems.at[n]))
            copies[-1].start()
        for copy in fetch(0, 0):
            copy.start()
        held[3 * RB] = jnp.zeros((BS, LANES), BF16)
        for copy in copies:
            copy.wait()

    @pl.when(step + 1 < steps)
    def _():
        for copy in fetch(step + 1, 1 - slot):
            copy.start()

    for copy in fetch(step, slot):
        copy.wait()

    zreal = z_ref[0:1, :]
    zimag = z_ref[1:2, :]
    totals = []
    for b in range(STEP):
        row = step * STEP + b
        right = jnp.concatenate(
            [held[index_ref[row * SLOTS + s]] for s in range(SLOTS)], axis=0
        )
        totals.append(jnp.dot(ham_buf[slot, b], right, preferred_element_type=F32))
    rights = []
    for b in range(STEP):
        current = held[RB + step * STEP + b].astype(F32)
        shifted = zreal * current + zimag * rotate_lanes(current)
        resid = (rhs_ref[b].astype(F32) - (shifted - totals[b])).astype(BF16).astype(F32)
        rights.append(split_points(resid, rotate_lanes(resid)).astype(BF16))
    for b in range(STEP):
        current = held[RB + step * STEP + b].astype(F32)
        left = jnp.concatenate([pre_buf[slot, 0, b], pre_buf[slot, 1, b]], axis=1)
        fresh[b] = (current + jnp.dot(left, rights[b], preferred_element_type=F32)).astype(BF16)
    if last:

        @pl.when(step < steps // 2)
        def _():
            out_ref[...] = fresh[...]

        @pl.when(step >= steps // 2)
        def _():
            second_ref[...] = fresh[...]


def sweep(index, ham, precond, rhs_unit, z, local, near, far, last):
    block = pl.BlockSpec((STEP, BS, LANES), lambda i, n: (i, 0, 0))
    anywhere = pl.BlockSpec(memory_space=pl.ANY)
    in_hbm = pl.BlockSpec(memory_space=pltpu.MemorySpace.HBM)
    scratch = [
        pltpu.VMEM((3 * RB + 1, BS, LANES), BF16),
        pltpu.SemaphoreType.DMA((7,)),
        pltpu.VMEM((2, STEP, BS, SLOTS * BS), BF16),
        pltpu.VMEM((2, 2, STEP, BS, LANES), BF16),
    ]
    if last:
        half = RB // STEP // 2
        out_specs = [
            pl.BlockSpec((STEP, BS, LANES), lambda i, n: (jnp.minimum(i, half - 1), 0, 0)),
            pl.BlockSpec((STEP, BS, LANES), lambda i, n: (jnp.maximum(i - half, 0), 0, 0)),
        ]
        out_shape = [jax.ShapeDtypeStruct((RB // 2, BS, LANES), BF16)] * 2
        scratch.append(pltpu.VMEM((STEP, BS, LANES), BF16))
    else:
        out_specs = [block]
        out_shape = [jax.ShapeDtypeStruct((RB, BS, LANES), BF16)]

    def kernel(*refs):
        sweep_kernel(last, *refs)

    return pl.pallas_call(
        kernel,
        grid_spec=pltpu.PrefetchScalarGridSpec(
            num_scalar_prefetch=1,
            grid=(RB // STEP,),
            in_specs=[
                in_hbm,
                in_hbm,
                block,
                pl.BlockSpec((8, LANES), lambda i, n: (0, 0)),
                anywhere,
                anywhere,
                anywhere,
            ],
            out_specs=out_specs,
            scratch_shapes=scratch,
        ),
        out_shape=out_shape,
        cost_estimate=pl.CostEstimate(
            flops=2 * RB * BS * SLOTS * BS * LANES, bytes_accessed=20 << 20, transcendentals=0
        ),
        compiler_params=pltpu.CompilerParams(vmem_limit_bytes=47 << 20),
        name="sweep_last" if last else "sweep",
    )(index, ham, precond, rhs_unit, z, local, near, far)


def combine_kernel(own_ref, peer_ref, weight_ref, send_ref, keep_ref):
    own, peer = own_ref[...], peer_ref[...]
    both = jnp.concatenate([own, peer, own, peer], axis=1)
    out = jnp.dot(both, weight_ref[0], preferred_element_type=F32)
    send_ref[...] = out[:, :LANES].astype(BF16)
    keep_ref[...] = out[:, LANES:]


def combine(own, peer, weights, which, rows_step):
    rows = peer.shape[0]
    row_spec = pl.BlockSpec((rows_step, LANES), lambda i: (i, 0))
    return pl.pallas_call(
        combine_kernel,
        grid=(rows // rows_step,),
        in_specs=[row_spec, row_spec, pl.BlockSpec((1, 4 * LANES, 2 * LANES), lambda i: (which, 0, 0))],
        out_specs=[row_spec, row_spec],
        out_shape=[
            jax.ShapeDtypeStruct((rows, LANES), BF16),
            jax.ShapeDtypeStruct((rows, LANES), F32),
        ],
        compiler_params=pltpu.CompilerParams(vmem_limit_bytes=8 << 20),
        cost_estimate=pl.CostEstimate(
            flops=2 * rows * 256 * 512, bytes_accessed=rows * LANES * 12, transcendentals=0
        ),
        name="combine",
    )(own, peer, weights)


def fold_kernel(keep1_ref, got1_ref, keep2_ref, got2_ref, send_ref, own_ref):
    top = keep1_ref[...] + got1_ref[...].astype(F32)
    bottom = keep2_ref[...] + got2_ref[...].astype(F32)
    first = lane_ids(top.shape) < GROUP
    send_ref[...] = jnp.where(first, pltpu.roll(top, GROUP, axis=1), bottom).astype(BF16)
    own_ref[...] = jnp.where(first, top, pltpu.roll(bottom, GROUP, axis=1))


def fold(keep1, got1, keep2, got2, rows, shift):
    step = 1024
    spec = pl.BlockSpec((step, LANES), lambda i: (i, 0))
    late = pl.BlockSpec((step, LANES), lambda i: (i + shift // step, 0))
    return pl.pallas_call(
        fold_kernel,
        grid=(rows // step,),
        in_specs=[spec, spec, late, late],
        out_specs=[spec, spec],
        out_shape=[
            jax.ShapeDtypeStruct((rows, LANES), BF16),
            jax.ShapeDtypeStruct((rows, LANES), F32),
        ],
        compiler_params=pltpu.CompilerParams(vmem_limit_bytes=10 << 20),
        cost_estimate=pl.CostEstimate(
            flops=rows * LANES * 8, bytes_accessed=rows * LANES * 18, transcendentals=0
        ),
        name="fold",
    )(keep1, got1, keep2, got2)


def finish_kernel(own1_ref, got1_ref, own2_ref, got2_ref, own_b_ref, got_b_ref, out_ref):
    def turn(x, shift):
        return pltpu.roll(x, shift, axis=1)

    late = pl.program_id(0) >= pl.num_programs(0) // 2
    top_a = own1_ref[...] + got1_ref[...].astype(F32)
    top_a = jnp.where(late, turn(top_a, GROUP), top_a)
    bottom_a = own2_ref[...] + got2_ref[...].astype(F32)
    bottom_a = jnp.where(late, turn(bottom_a, GROUP), bottom_a)
    unit_b = own_b_ref[...] + got_b_ref[...].astype(F32)
    quarter = lane_ids(unit_b.shape) // HALF

    def merge(first, second, third, fourth):
        low = jnp.where(quarter == 0, first, second)
        high = jnp.where(quarter == 2, third, fourth)
        return jnp.where(quarter < 2, low, high)

    out_ref[0, 0] = merge(top_a, turn(unit_b, HALF), turn(top_a, HALF), turn(unit_b, GROUP))
    out_ref[0, 1] = merge(bottom_a, turn(unit_b, 96), turn(bottom_a, HALF), unit_b)


def finish(own1, got1, own2, got2, own_b, got_b, step):
    rows = own_b.shape[0]
    half = rows // 2 // step
    spec = pl.BlockSpec((step, LANES), lambda i: (i, 0))
    spec_a = pl.BlockSpec((step, LANES), lambda i: (i % half, 0))
    return pl.pallas_call(
        finish_kernel,
        grid=(rows // step,),
        in_specs=[spec_a] * 4 + [spec] * 2,
        out_specs=pl.BlockSpec((1, 2, step, LANES), lambda i: (0, 0, i, 0)),
        out_shape=jax.ShapeDtypeStruct((1, 2, rows, LANES), F32),
        compiler_params=pltpu.CompilerParams(vmem_limit_bytes=10 << 20),
        name="finish",
    )(own1, got1, own2, got2, own_b, got_b)


def moment_coefs(plans):
    lane = lax.broadcasted_iota(jnp.int32, (1, 32, 2 * LANES), 2)
    line = lax.broadcasted_iota(jnp.int32, (1, 32, 2 * LANES), 1)
    slot, point, kind = lane // GROUP, line // 8, line % 8
    tables = []
    for owners, orders in plans:
        owner = jnp.where(point < 2, owners[0], owners[1])
        low = jnp.where(slot == 0, orders[0], orders[1])
        high = jnp.where(slot == 2, orders[2], orders[3])
        order = jnp.where(slot < 2, low, high)
        turns = ((order + 1) * (2 * (owner * 2 + point % 2) + 1)) % (2 * POINTS)
        sign = jnp.where((lane // HALF) % 2 == 0, -1.0, 1.0)
        phase = turns.astype(F32) * (math.pi / POINTS)
        quarter = jnp.where(kind == 0, math.pi / 2, 0.0)
        tables.append(jnp.where(kind == 0, 1.0, sign) * jnp.sin(phase + quarter) / POINTS)
    return jnp.concatenate(tables, axis=0)


def step(hamiltonian, columns, counts, precond, rhs):
    row_index = lax.axis_index("row")
    quad_index = lax.axis_index("quad")

    def swap(x, axis, peer_of):
        peers = [(i, peer_of(i)) for i in range(lax.axis_size(axis))]
        return lax.ppermute(x, axis, [(i, j) for i, j in peers if 0 <= j < len(peers)])

    def by_pair(i):
        return (((i // 2) ^ 1) * 2) + i % 2

    def by_mirror(i):
        return ((3 - i // 2) * 2) + i % 2

    def by_x(i):
        return i ^ 1

    def near_row(i):
        return i ^ 1

    def far_row(i):
        return i + 1 if i % 2 else i - 1

    units = list(initial(rhs, precond))

    live = jnp.arange(SLOTS)[None, :] < counts[:, None]
    index = jnp.where(live, columns - (row_index - 1) * RB, 3 * RB).reshape(RB * SLOTS)
    near_at = jnp.where(row_index % 2 == 1, 0, 2 * RB)
    index = jnp.concatenate([index, jnp.full((LANES,), near_at, jnp.int32)])
    lane = jnp.arange(LANES)[None, :]
    theta = 2.0 * jnp.pi * ((quad_index * 2 + lane // GROUP).astype(F32) + 0.5) / POINTS
    z = jnp.concatenate([jnp.cos(theta), jnp.sin(theta), jnp.zeros((6, LANES), F32)], axis=0)

    mine, other = quad_index, quad_index ^ 1
    pair, mirror = by_pair(quad_index), by_mirror(quad_index)
    coefs = moment_coefs(
        (
            ((mine, pair), (other, mirror ^ 1, mine, mirror)),
            ((mine, mirror), (other, pair ^ 1, mine, pair)),
            ((mine, pair), (mirror, mirror ^ 1, mine, other)),
            ((mine, mirror), (pair, pair ^ 1, mine, other)),
        ),
    )
    *rhs_units, weights = spread(rhs, coefs)

    grams = [None, None]
    for it in range(ITERS):
        for unit in range(2):
            y = units[unit]
            far = swap(y, "row", far_row)
            near = swap(y, "row", near_row)
            last = it == ITERS - 1
            got = sweep(
                index, hamiltonian, precond, rhs_units[unit], z, y, near, far, last
            )
            units[unit] = got[0]
            if last:
                units[unit] = got[:2]
                both = (part.reshape(-1, LANES) for part in got)
                parts = zip((rhs[: RB * BS // 2], rhs[RB * BS // 2 :]), both, strict=True)
                grams[unit] = sum(
                    lax.dot_general(x, part, (((0,), (0,)), ((), ())), preferred_element_type=F32)
                    for x, part in parts
                )

    half_rows = RB * BS // 2

    def first_stage(unit):
        top, bottom = (part.reshape(half_rows, LANES) for part in units[unit])
        got1 = swap(top, "quad", by_pair)
        got2 = swap(bottom, "quad", by_mirror)
        out1 = combine(top, got1, weights, 2 * unit, 1024)
        return out1 + combine(bottom, got2, weights, 2 * unit + 1, 1024)

    send_a1, keep_a1, send_a2, keep_a2 = first_stage(0)
    got_a1 = swap(send_a1, "quad", by_x)
    got_a2 = swap(send_a2, "quad", by_x)
    quarter = half_rows // 2
    send_a1, own_a1 = fold(keep_a1, got_a1, keep_a1, got_a1, quarter, quarter)
    send_a2, own_a2 = fold(keep_a2, got_a2, keep_a2, got_a2, quarter, quarter)

    send_b1, keep_b1, send_b2, keep_b2 = first_stage(1)
    got_b1 = swap(send_b1, "quad", by_mirror)
    got_b2 = swap(send_b2, "quad", by_pair)
    send_b, own_b = fold(keep_b1, got_b1, keep_b2, got_b2, half_rows, 0)

    gram = jnp.concatenate(grams, axis=0)
    gram = lax.reduce_precision(gram, 8, 7)
    gram = gram + swap(gram.astype(BF16), "row", lambda i: i ^ 8).astype(F32)
    for bit in (4, 2, 1):
        gram = gram + swap(gram, "row", lambda i, bit=bit: i ^ bit)
    gram = gram.astype(BF16)
    peer = swap(gram, "quad", by_pair)
    send_g, keep_g = combine(gram, peer, weights, 2, 256)
    gram_sum = keep_g + swap(send_g, "quad", by_mirror).astype(F32)
    gram_got = swap(gram_sum[:, GROUP:].astype(BF16), "quad", by_x)
    blocks = gram_sum[:, :GROUP] + gram_got.astype(F32)
    blocks = blocks * (1.0 / math.sqrt(RB * BS * 16))
    blocks = blocks.reshape(2, LANES, 2, HALF).transpose(1, 2, 0, 3).reshape(1, LANES, LANES)

    got_a1 = swap(send_a1, "quad", by_mirror)
    got_a2 = swap(send_a2, "quad", by_pair)
    got_b = swap(send_b, "quad", by_x)
    moments = finish(own_a1, got_a1, own_a2, got_a2, own_b, got_b, 512)
    return moments.reshape(1, RB * BS, LANES), blocks


def solution(mesh):
    return jax.shard_map(
        step,
        mesh=mesh,
        in_specs=(
            P("row", None, None),
            P("row", None),
            P("row"),
            P("quad", "row", None, None),
            P("row", None),
        ),
        out_specs=(P("quad", "row", None), P("quad", None, None)),
        check_vma=False,
    )
```

```python
import math

import jax
import jax.numpy as jnp
import numpy as np
from jax import lax
from jax.experimental import pallas as pl
from jax.experimental.pallas import tpu as pltpu
from jax.sharding import PartitionSpec as P

ITERS = 2
POINTS = 16
BS = 64
SLOTS = 24
RB = 64
LANES = 128
GROUP = 64
HALF = 32
STEP = 8
F32 = jnp.float32
BF16 = jnp.bfloat16


def unit_lanes(points):
    table = np.zeros((points * LANES, 2 * LANES), np.float32)
    for unit in range(2):
        for lane in range(LANES):
            point, part, col = lane // GROUP, (lane // HALF) % 2, lane % HALF
            src = (point % points) * LANES + part * GROUP + unit * HALF + col
            table[src, unit * LANES + lane] = 1.0
    return table


def lane_ids(shape):
    return lax.broadcasted_iota(jnp.int32, shape, len(shape) - 1)


def split_points(top, bottom):
    lane = lane_ids(top.shape) % LANES
    first = lane < GROUP
    zero = jnp.zeros_like(top)
    return jnp.concatenate(
        [
            jnp.where(first, top, zero),
            jnp.where(first, bottom, zero),
            jnp.where(first, zero, top),
            jnp.where(first, zero, bottom),
        ],
        axis=0,
    )


def init_kernel(x_ref, pre_ref, map_ref, y_a_ref, y_b_ref):
    rights = []
    for b in range(STEP):
        x = x_ref[b * BS : (b + 1) * BS].astype(F32)
        turned = pltpu.roll(x, GROUP, axis=1)
        turned = jnp.where(lane_ids(x.shape) < GROUP, -turned, turned)
        rights.append(jnp.concatenate([x, turned], axis=0).astype(BF16))
    outs = []
    for b in range(STEP):
        left = jnp.concatenate([pre_ref[0, b], pre_ref[1, b]], axis=0)
        outs.append(jnp.dot(left, rights[b], preferred_element_type=F32))
    outs = [out.astype(BF16) for out in outs]
    firsts = [out[:BS] for out in outs]
    seconds = [out[BS:] for out in outs]
    both = jnp.concatenate(
        [jnp.concatenate(firsts, axis=0), jnp.concatenate(seconds, axis=0)], axis=1
    )
    out = jnp.dot(both, map_ref[...], preferred_element_type=F32).astype(BF16)
    y_a_ref[...] = out[:, :LANES].reshape(STEP, BS, LANES)
    y_b_ref[...] = out[:, LANES:].reshape(STEP, BS, LANES)


def initial(rhs, precond):
    block = jax.ShapeDtypeStruct((RB, BS, LANES), BF16)
    out_spec = pl.BlockSpec((STEP, BS, LANES), lambda i: (i, 0, 0))
    return pl.pallas_call(
        init_kernel,
        grid=(RB // STEP,),
        in_specs=[
            pl.BlockSpec((STEP * BS, LANES), lambda i: (i, 0)),
            pl.BlockSpec((2, STEP, BS, LANES), lambda i: (0, i, 0, 0)),
            pl.BlockSpec((2 * LANES, 2 * LANES), lambda i: (0, 0)),
        ],
        out_specs=[out_spec] * 2,
        out_shape=[block] * 2,
        name="initial",
    )(rhs, precond, jnp.asarray(unit_lanes(2), BF16))


def spread_kernel(x_ref, map_ref, coef_ref, rhs_a_ref, rhs_b_ref, weight_ref):
    out = jnp.dot(x_ref[...], map_ref[...], preferred_element_type=F32).astype(BF16)
    rhs_a_ref[...] = out[:, :LANES].reshape(rhs_a_ref.shape)
    rhs_b_ref[...] = out[:, LANES:].reshape(rhs_b_ref.shape)
    shape = (GROUP, 2 * LANES)
    r = lax.broadcasted_iota(jnp.int32, shape, 0)
    c = lax.broadcasted_iota(jnp.int32, shape, 1)
    same = r % HALF == c % HALF
    straight = same & ((r // HALF) == (c // GROUP) % 2)
    crossed = same & ((r // HALF) != (c // GROUP) % 2)
    for point in range(4):
        rows = coef_ref[0, point * 8 : point * 8 + 8]
        cosine, sine = rows[0:1, :], rows[1:2, :]
        value = jnp.where(straight, cosine, jnp.where(crossed, sine, 0.0))
        high = value.astype(BF16)
        weight_ref[0, point * GROUP : (point + 1) * GROUP] = high
        weight_ref[0, (4 + point) * GROUP : (5 + point) * GROUP] = (
            value - high.astype(F32)
        ).astype(BF16)


def spread(rhs, coefs):
    block = jax.ShapeDtypeStruct((RB, BS, LANES), BF16)
    out_spec = pl.BlockSpec((RB // 4, BS, LANES), lambda i: (i, 0, 0))
    return pl.pallas_call(
        spread_kernel,
        grid=(4,),
        in_specs=[
            pl.BlockSpec((RB // 4 * BS, LANES), lambda i: (i, 0)),
            pl.BlockSpec((LANES, 2 * LANES), lambda i: (0, 0)),
            pl.BlockSpec((1, 32, 2 * LANES), lambda i: (i, 0, 0)),
        ],
        out_specs=[out_spec, out_spec, pl.BlockSpec((1, 512, 256), lambda i: (i, 0, 0))],
        out_shape=[block, block, jax.ShapeDtypeStruct((4, 512, 256), BF16)],
        compiler_params=pltpu.CompilerParams(vmem_limit_bytes=14 << 20),
        cost_estimate=pl.CostEstimate(
            flops=2 * RB * BS * LANES * 256, bytes_accessed=3 << 20, transcendentals=0
        ),
        name="spread",
    )(rhs, jnp.asarray(unit_lanes(1), BF16), coefs)


def rotate_lanes(x):
    lane = lane_ids(x.shape) % GROUP
    up = pltpu.roll(x, LANES - HALF, axis=x.ndim - 1)
    down = pltpu.roll(x, HALF, axis=x.ndim - 1)
    return jnp.where(lane < HALF, -up, down)


def sweep_kernel(
    last, index_ref, ham_ref, pre_ref, rhs_ref, z_ref, local_ref, near_ref, far_ref,
    out_ref, *rest,
):
    if last:
        second_ref, held, sems, ham_buf, pre_buf, fresh = rest
    else:
        held, sems, ham_buf, pre_buf = rest
        fresh = out_ref
    step = pl.program_id(0)
    steps = pl.num_programs(0)
    slot = step % 2

    def fetch(at, to):
        blocks = pl.ds(pl.multiple_of(at * STEP, STEP), STEP)
        return (
            pltpu.make_async_copy(ham_ref.at[blocks], ham_buf.at[to], sems.at[3 + to]),
            pltpu.make_async_copy(pre_ref.at[:, blocks], pre_buf.at[to], sems.at[5 + to]),
        )

    @pl.when(step == 0)
    def _():
        copies = []
        near_at = index_ref[RB * SLOTS]
        places = (near_at, RB, 2 * RB - near_at)
        for n, ref in enumerate((near_ref, local_ref, far_ref)):
            place = pl.multiple_of(places[n], RB)
            copies.append(pltpu.make_async_copy(ref, held.at[pl.ds(place, RB)], sems.at[n]))
            copies[-1].start()
        for copy in fetch(0, 0):
            copy.start()
        held[3 * RB] = jnp.zeros((BS, LANES), BF16)
        for copy in copies:
            copy.wait()

    @pl.when(step + 1 < steps)
    def _():
        for copy in fetch(step + 1, 1 - slot):
            copy.start()

    for copy in fetch(step, slot):
        copy.wait()

    zreal = z_ref[0:1, :]
    zimag = z_ref[1:2, :]
    totals = []
    for b in range(STEP):
        row = step * STEP + b
        right = jnp.concatenate(
            [held[index_ref[row * SLOTS + s]] for s in range(SLOTS)], axis=0
        )
        totals.append(jnp.dot(ham_buf[slot, b], right, preferred_element_type=F32))
    rights = []
    for b in range(STEP):
        current = held[RB + step * STEP + b].astype(F32)
        shifted = zreal * current + zimag * rotate_lanes(current)
        resid = (rhs_ref[b].astype(F32) - (shifted - totals[b])).astype(BF16).astype(F32)
        rights.append(split_points(resid, rotate_lanes(resid)).astype(BF16))
    for b in range(STEP):
        current = held[RB + step * STEP + b].astype(F32)
        left = jnp.concatenate([pre_buf[slot, 0, b], pre_buf[slot, 1, b]], axis=1)
        fresh[b] = (current + jnp.dot(left, rights[b], preferred_element_type=F32)).astype(BF16)
    if last:

        @pl.when(step < steps // 2)
        def _():
            out_ref[...] = fresh[...]

        @pl.when(step >= steps // 2)
        def _():
            second_ref[...] = fresh[...]


def sweep(index, ham, precond, rhs_unit, z, local, near, far, last):
    block = pl.BlockSpec((STEP, BS, LANES), lambda i, n: (i, 0, 0))
    anywhere = pl.BlockSpec(memory_space=pl.ANY)
    in_hbm = pl.BlockSpec(memory_space=pltpu.MemorySpace.HBM)
    scratch = [
        pltpu.VMEM((3 * RB + 1, BS, LANES), BF16),
        pltpu.SemaphoreType.DMA((7,)),
        pltpu.VMEM((2, STEP, BS, SLOTS * BS), BF16),
        pltpu.VMEM((2, 2, STEP, BS, LANES), BF16),
    ]
    if last:
        half = RB // STEP // 2
        out_specs = [
            pl.BlockSpec((STEP, BS, LANES), lambda i, n: (jnp.minimum(i, half - 1), 0, 0)),
            pl.BlockSpec((STEP, BS, LANES), lambda i, n: (jnp.maximum(i - half, 0), 0, 0)),
        ]
        out_shape = [jax.ShapeDtypeStruct((RB // 2, BS, LANES), BF16)] * 2
        scratch.append(pltpu.VMEM((STEP, BS, LANES), BF16))
    else:
        out_specs = [block]
        out_shape = [jax.ShapeDtypeStruct((RB, BS, LANES), BF16)]

    def kernel(*refs):
        sweep_kernel(last, *refs)

    return pl.pallas_call(
        kernel,
        grid_spec=pltpu.PrefetchScalarGridSpec(
            num_scalar_prefetch=1,
            grid=(RB // STEP,),
            in_specs=[
                in_hbm,
                in_hbm,
                block,
                pl.BlockSpec((8, LANES), lambda i, n: (0, 0)),
                anywhere,
                anywhere,
                anywhere,
            ],
            out_specs=out_specs,
            scratch_shapes=scratch,
        ),
        out_shape=out_shape,
        cost_estimate=pl.CostEstimate(
            flops=2 * RB * BS * SLOTS * BS * LANES, bytes_accessed=20 << 20, transcendentals=0
        ),
        compiler_params=pltpu.CompilerParams(vmem_limit_bytes=47 << 20),
        name="sweep_last" if last else "sweep",
    )(index, ham, precond, rhs_unit, z, local, near, far)


def combine_kernel(own_ref, peer_ref, weight_ref, send_ref, keep_ref):
    own, peer = own_ref[...], peer_ref[...]
    both = jnp.concatenate([own, peer, own, peer], axis=1)
    out = jnp.dot(both, weight_ref[0], preferred_element_type=F32)
    send_ref[...] = out[:, :LANES].astype(BF16)
    keep_ref[...] = out[:, LANES:]


def combine(own, peer, weights, which, rows_step):
    rows = peer.shape[0]
    row_spec = pl.BlockSpec((rows_step, LANES), lambda i: (i, 0))
    return pl.pallas_call(
        combine_kernel,
        grid=(rows // rows_step,),
        in_specs=[row_spec, row_spec, pl.BlockSpec((1, 4 * LANES, 2 * LANES), lambda i: (which, 0, 0))],
        out_specs=[row_spec, row_spec],
        out_shape=[
            jax.ShapeDtypeStruct((rows, LANES), BF16),
            jax.ShapeDtypeStruct((rows, LANES), F32),
        ],
        compiler_params=pltpu.CompilerParams(vmem_limit_bytes=8 << 20),
        cost_estimate=pl.CostEstimate(
            flops=2 * rows * 256 * 512, bytes_accessed=rows * LANES * 12, transcendentals=0
        ),
        name="combine",
    )(own, peer, weights)


def own_lanes(shape, unit):
    return (lane_ids(shape) // HALF) % 2 == unit


def to_own(x, unit):
    return pltpu.roll(x, HALF if unit else LANES - HALF, axis=1)


def from_own(x, unit):
    return pltpu.roll(x, LANES - HALF if unit else HALF, axis=1)


def fold_kernel(unit, keep1_ref, got1_ref, keep2_ref, got2_ref, send_ref, own_ref):
    top = keep1_ref[...] + got1_ref[...].astype(F32)
    bottom = keep2_ref[...] + got2_ref[...].astype(F32)
    own = own_lanes(top.shape, unit)
    send_ref[...] = jnp.where(own, to_own(top, unit), bottom).astype(BF16)
    own_ref[...] = jnp.where(own, top, from_own(bottom, unit))


def fold(unit, keep1, got1, keep2, got2, rows, shift):
    def kernel(*refs):
        fold_kernel(unit, *refs)

    step = 1024
    spec = pl.BlockSpec((step, LANES), lambda i: (i, 0))
    late = pl.BlockSpec((step, LANES), lambda i: (i + shift // step, 0))
    return pl.pallas_call(
        kernel,
        grid=(rows // step,),
        in_specs=[spec, spec, late, late],
        out_specs=[spec, spec],
        out_shape=[
            jax.ShapeDtypeStruct((rows, LANES), BF16),
            jax.ShapeDtypeStruct((rows, LANES), F32),
        ],
        compiler_params=pltpu.CompilerParams(vmem_limit_bytes=10 << 20),
        cost_estimate=pl.CostEstimate(
            flops=rows * LANES * 8, bytes_accessed=rows * LANES * 18, transcendentals=0
        ),
        name="fold",
    )(keep1, got1, keep2, got2)


def finish_kernel(own1_ref, got1_ref, own2_ref, got2_ref, own_b_ref, got_b_ref, out_ref):
    unit_b = own_b_ref[...] + got_b_ref[...].astype(F32)
    first = own_lanes(unit_b.shape, 0)
    halves = pl.num_programs(0) // 2

    def store(place):
        top_a = place(own1_ref[...] + got1_ref[...].astype(F32))
        bottom_a = place(own2_ref[...] + got2_ref[...].astype(F32))
        out_ref[0, 0] = jnp.where(first, top_a, unit_b)
        out_ref[0, 1] = jnp.where(first, bottom_a, to_own(unit_b, 1))

    @pl.when(pl.program_id(0) < halves)
    def _():
        store(lambda x: x)

    @pl.when(pl.program_id(0) >= halves)
    def _():
        store(lambda x: to_own(x, 0))


def finish(own1, got1, own2, got2, own_b, got_b, step):
    rows = own_b.shape[0]
    half = rows // 2 // step
    spec = pl.BlockSpec((step, LANES), lambda i: (i, 0))
    spec_a = pl.BlockSpec((step, LANES), lambda i: (i % half, 0))
    return pl.pallas_call(
        finish_kernel,
        grid=(rows // step,),
        in_specs=[spec_a] * 4 + [spec] * 2,
        out_specs=pl.BlockSpec((1, 2, step, LANES), lambda i: (0, 0, i, 0)),
        out_shape=jax.ShapeDtypeStruct((1, 2, rows, LANES), F32),
        compiler_params=pltpu.CompilerParams(vmem_limit_bytes=10 << 20),
        name="finish",
    )(own1, got1, own2, got2, own_b, got_b)


def moment_coefs(plans):
    lane = lax.broadcasted_iota(jnp.int32, (1, 32, 2 * LANES), 2)
    line = lax.broadcasted_iota(jnp.int32, (1, 32, 2 * LANES), 1)
    point, kind = line // 8, line % 8
    tables = []
    for unit, owners, orders in plans:
        slot = lane // LANES * 2 + ((lane // HALF) % 2 ^ unit)
        owner = jnp.where(point < 2, owners[0], owners[1])
        low = jnp.where(slot == 0, orders[0], orders[1])
        high = jnp.where(slot == 2, orders[2], orders[3])
        order = jnp.where(slot < 2, low, high)
        turns = ((order + 1) * (2 * (owner * 2 + point % 2) + 1)) % (2 * POINTS)
        sign = jnp.where((lane // GROUP) % 2 == 0, -1.0, 1.0)
        phase = turns.astype(F32) * (math.pi / POINTS)
        quarter = jnp.where(kind == 0, math.pi / 2, 0.0)
        tables.append(jnp.where(kind == 0, 1.0, sign) * jnp.sin(phase + quarter) / POINTS)
    return jnp.concatenate(tables, axis=0)


def step(hamiltonian, columns, counts, precond, rhs):
    row_index = lax.axis_index("row")
    quad_index = lax.axis_index("quad")

    def swap(x, axis, peer_of):
        peers = [(i, peer_of(i)) for i in range(lax.axis_size(axis))]
        return lax.ppermute(x, axis, [(i, j) for i, j in peers if 0 <= j < len(peers)])

    def by_pair(i):
        return (((i // 2) ^ 1) * 2) + i % 2

    def by_mirror(i):
        return ((3 - i // 2) * 2) + i % 2

    def by_x(i):
        return i ^ 1

    def near_row(i):
        return i ^ 1

    def far_row(i):
        return i + 1 if i % 2 else i - 1

    units = list(initial(rhs, precond))

    live = jnp.arange(SLOTS)[None, :] < counts[:, None]
    index = jnp.where(live, columns - (row_index - 1) * RB, 3 * RB).reshape(RB * SLOTS)
    near_at = jnp.where(row_index % 2 == 1, 0, 2 * RB)
    index = jnp.concatenate([index, jnp.full((LANES,), near_at, jnp.int32)])
    lane = jnp.arange(LANES)[None, :]
    theta = 2.0 * jnp.pi * ((quad_index * 2 + lane // GROUP).astype(F32) + 0.5) / POINTS
    z = jnp.concatenate([jnp.cos(theta), jnp.sin(theta), jnp.zeros((6, LANES), F32)], axis=0)

    mine, other = quad_index, quad_index ^ 1
    pair, mirror = by_pair(quad_index), by_mirror(quad_index)
    coefs = moment_coefs(
        (
            (0, (mine, pair), (other, mirror ^ 1, mine, mirror)),
            (0, (mine, mirror), (other, pair ^ 1, mine, pair)),
            (1, (mine, pair), (mirror, mirror ^ 1, mine, other)),
            (1, (mine, mirror), (pair, pair ^ 1, mine, other)),
        ),
    )
    *rhs_units, weights = spread(rhs, coefs)

    grams = [None, None]
    for it in range(ITERS):
        for unit in range(2):
            y = units[unit]
            far = swap(y, "row", far_row)
            near = swap(y, "row", near_row)
            last = it == ITERS - 1
            got = sweep(
                index, hamiltonian, precond, rhs_units[unit], z, y, near, far, last
            )
            units[unit] = got[0]
            if last:
                units[unit] = got[:2]
                both = (part.reshape(-1, LANES) for part in got)
                parts = zip((rhs[: RB * BS // 2], rhs[RB * BS // 2 :]), both, strict=True)
                grams[unit] = sum(
                    lax.dot_general(x, part, (((0,), (0,)), ((), ())), preferred_element_type=F32)
                    for x, part in parts
                )

    half_rows = RB * BS // 2

    def first_stage(unit):
        top, bottom = (part.reshape(half_rows, LANES) for part in units[unit])
        got1 = swap(top, "quad", by_pair)
        got2 = swap(bottom, "quad", by_mirror)
        out1 = combine(top, got1, weights, 2 * unit, 1024)
        return out1 + combine(bottom, got2, weights, 2 * unit + 1, 1024)

    send_a1, keep_a1, send_a2, keep_a2 = first_stage(0)
    got_a1 = swap(send_a1, "quad", by_x)
    got_a2 = swap(send_a2, "quad", by_x)
    quarter = half_rows // 2
    send_a1, own_a1 = fold(0, keep_a1, got_a1, keep_a1, got_a1, quarter, quarter)
    send_a2, own_a2 = fold(0, keep_a2, got_a2, keep_a2, got_a2, quarter, quarter)

    send_b1, keep_b1, send_b2, keep_b2 = first_stage(1)
    got_b1 = swap(send_b1, "quad", by_mirror)
    got_b2 = swap(send_b2, "quad", by_pair)
    send_b, own_b = fold(1, keep_b1, got_b1, keep_b2, got_b2, half_rows, 0)

    def rounded(x):
        return lax.reduce_precision(x, 8, 7)

    even = row_index % 2 == 0
    gram = jnp.where(even, grams[0], grams[1])
    gram = gram + swap(jnp.where(even, grams[1], grams[0]), "row", near_row)
    for bit in (8, 4, 2):
        gram = rounded(gram)
        peer = swap(gram.astype(BF16), "row", lambda i, bit=bit: i ^ bit)
        gram = gram + peer.astype(F32)
    gram = gram.astype(BF16)
    peer = swap(gram, "quad", by_pair)
    send_g, keep_g = combine(gram, peer, weights, 2, LANES)
    gram_sum = keep_g + swap(send_g, "quad", by_mirror).astype(F32)
    gram_got = swap(gram_sum.astype(BF16), "quad", by_x)
    gram_own = gram_sum + jnp.roll(gram_got, HALF, axis=1).astype(F32)
    gram_other = swap(gram_own, "row", near_row)
    gram_a = jnp.where(even, gram_own, gram_other)
    gram_b = jnp.where(even, gram_other, gram_own)
    first = own_lanes((LANES, LANES), 0)
    blocks = jnp.where(first, jnp.roll(gram_a, -HALF, axis=1), gram_b)
    blocks = (blocks * (1.0 / math.sqrt(RB * BS * 16)))[None]

    got_a1 = swap(send_a1, "quad", by_mirror)
    got_a2 = swap(send_a2, "quad", by_pair)
    got_b = swap(send_b, "quad", by_x)
    moments = finish(own_a1, got_a1, own_a2, got_a2, own_b, got_b, 512)
    return moments.reshape(1, RB * BS, LANES), blocks


def solution(mesh):
    return jax.shard_map(
        step,
        mesh=mesh,
        in_specs=(
            P("row", None, None),
            P("row", None),
            P("row"),
            P("quad", "row", None, None),
            P("row", None),
        ),
        out_specs=(P("quad", "row", None), P("quad", None, None)),
        check_vma=False,
    )
```

```python
import math

import jax
import jax.numpy as jnp
import numpy as np
from jax import lax
from jax.experimental import pallas as pl
from jax.experimental.pallas import tpu as pltpu
from jax.sharding import PartitionSpec as P

ITERS = 2
POINTS = 16
BS = 64
SLOTS = 24
RB = 64
LANES = 128
GROUP = 64
HALF = 32
STEP = 16
FIRST = 32
F32 = jnp.float32
BF16 = jnp.bfloat16


def unit_lanes(points):
    table = np.zeros((points * LANES, 2 * LANES), np.float32)
    for unit in range(2):
        for lane in range(LANES):
            point, part, col = lane // GROUP, (lane // HALF) % 2, lane % HALF
            src = (point % points) * LANES + part * GROUP + unit * HALF + col
            table[src, unit * LANES + lane] = 1.0
    return table


def lane_ids(shape):
    return lax.broadcasted_iota(jnp.int32, shape, len(shape) - 1)


def split_points(top, bottom):
    lane = lane_ids(top.shape) % LANES
    first = lane < GROUP
    zero = jnp.zeros_like(top)
    return jnp.concatenate(
        [
            jnp.where(first, top, zero),
            jnp.where(first, bottom, zero),
            jnp.where(first, zero, top),
            jnp.where(first, zero, bottom),
        ],
        axis=0,
    )


def init_kernel(x_ref, pre_ref, map_ref, y_a_ref, y_b_ref):
    rights = []
    for b in range(FIRST):
        x = x_ref[b * BS : (b + 1) * BS].astype(F32)
        turned = pltpu.roll(x, GROUP, axis=1)
        turned = jnp.where(lane_ids(x.shape) < GROUP, -turned, turned)
        rights.append(jnp.concatenate([x, turned], axis=0).astype(BF16))
    outs = []
    for b in range(FIRST):
        left = jnp.concatenate([pre_ref[0, b], pre_ref[1, b]], axis=0)
        outs.append(jnp.dot(left, rights[b], preferred_element_type=F32))
    outs = [out.astype(BF16) for out in outs]
    firsts = [out[:BS] for out in outs]
    seconds = [out[BS:] for out in outs]
    both = jnp.concatenate(
        [jnp.concatenate(firsts, axis=0), jnp.concatenate(seconds, axis=0)], axis=1
    )
    out = jnp.dot(both, map_ref[...], preferred_element_type=F32).astype(BF16)
    y_a_ref[...] = out[:, :LANES].reshape(FIRST, BS, LANES)
    y_b_ref[...] = out[:, LANES:].reshape(FIRST, BS, LANES)


def initial(rhs, precond):
    block = jax.ShapeDtypeStruct((RB, BS, LANES), BF16)
    out_spec = pl.BlockSpec((FIRST, BS, LANES), lambda i: (i, 0, 0))
    return pl.pallas_call(
        init_kernel,
        grid=(RB // FIRST,),
        in_specs=[
            pl.BlockSpec((FIRST * BS, LANES), lambda i: (i, 0)),
            pl.BlockSpec((2, FIRST, BS, LANES), lambda i: (0, i, 0, 0)),
            pl.BlockSpec((2 * LANES, 2 * LANES), lambda i: (0, 0)),
        ],
        out_specs=[out_spec] * 2,
        out_shape=[block] * 2,
        name="initial",
    )(rhs, precond, jnp.asarray(unit_lanes(2), BF16))


def spread_kernel(x_ref, map_ref, coef_ref, rhs_a_ref, rhs_b_ref, weight_ref):
    out = jnp.dot(x_ref[...], map_ref[...], preferred_element_type=F32).astype(BF16)
    rhs_a_ref[...] = out[:, :LANES].reshape(rhs_a_ref.shape)
    rhs_b_ref[...] = out[:, LANES:].reshape(rhs_b_ref.shape)
    shape = (GROUP, 2 * LANES)
    r = lax.broadcasted_iota(jnp.int32, shape, 0)
    c = lax.broadcasted_iota(jnp.int32, shape, 1)
    same = r % HALF == c % HALF
    straight = same & ((r // HALF) == (c // GROUP) % 2)
    crossed = same & ((r // HALF) != (c // GROUP) % 2)
    for point in range(4):
        rows = coef_ref[0, point * 8 : point * 8 + 8]
        cosine, sine = rows[0:1, :], rows[1:2, :]
        value = jnp.where(straight, cosine, jnp.where(crossed, sine, 0.0))
        high = value.astype(BF16)
        weight_ref[0, point * GROUP : (point + 1) * GROUP] = high
        weight_ref[0, (4 + point) * GROUP : (5 + point) * GROUP] = (
            value - high.astype(F32)
        ).astype(BF16)


def spread(rhs, coefs):
    block = jax.ShapeDtypeStruct((RB, BS, LANES), BF16)
    out_spec = pl.BlockSpec((RB // 4, BS, LANES), lambda i: (i, 0, 0))
    return pl.pallas_call(
        spread_kernel,
        grid=(4,),
        in_specs=[
            pl.BlockSpec((RB // 4 * BS, LANES), lambda i: (i, 0)),
            pl.BlockSpec((LANES, 2 * LANES), lambda i: (0, 0)),
            pl.BlockSpec((1, 32, 2 * LANES), lambda i: (i, 0, 0)),
        ],
        out_specs=[out_spec, out_spec, pl.BlockSpec((1, 512, 256), lambda i: (i, 0, 0))],
        out_shape=[block, block, jax.ShapeDtypeStruct((4, 512, 256), BF16)],
        compiler_params=pltpu.CompilerParams(vmem_limit_bytes=14 << 20),
        cost_estimate=pl.CostEstimate(
            flops=2 * RB * BS * LANES * 256, bytes_accessed=3 << 20, transcendentals=0
        ),
        name="spread",
    )(rhs, jnp.asarray(unit_lanes(1), BF16), coefs)


def rotate_lanes(x):
    lane = lane_ids(x.shape) % GROUP
    up = pltpu.roll(x, LANES - HALF, axis=x.ndim - 1)
    down = pltpu.roll(x, HALF, axis=x.ndim - 1)
    return jnp.where(lane < HALF, -up, down)


def sweep_kernel(
    last, index_ref, ham_ref, pre_ref, rhs_ref, z_ref, local_ref, near_ref, far_ref,
    out_ref, *rest,
):
    if last:
        second_ref, held, sems, ham_buf, pre_buf, fresh = rest
    else:
        held, sems, ham_buf, pre_buf = rest
        fresh = out_ref
    step = pl.program_id(0)
    steps = pl.num_programs(0)
    slot = step % 2

    def fetch(at, to):
        blocks = pl.ds(pl.multiple_of(at * STEP, STEP), STEP)
        return (
            pltpu.make_async_copy(ham_ref.at[blocks], ham_buf.at[to], sems.at[3 + to]),
            pltpu.make_async_copy(pre_ref.at[:, blocks], pre_buf.at[to], sems.at[5 + to]),
        )

    @pl.when(step == 0)
    def _():
        copies = []
        near_at = index_ref[RB * SLOTS]
        places = (near_at, RB, 2 * RB - near_at)
        for n, ref in enumerate((near_ref, local_ref, far_ref)):
            place = pl.multiple_of(places[n], RB)
            copies.append(pltpu.make_async_copy(ref, held.at[pl.ds(place, RB)], sems.at[n]))
            copies[-1].start()
        for copy in fetch(0, 0):
            copy.start()
        held[3 * RB] = jnp.zeros((BS, LANES), BF16)
        for copy in copies:
            copy.wait()

    @pl.when(step + 1 < steps)
    def _():
        for copy in fetch(step + 1, 1 - slot):
            copy.start()

    for copy in fetch(step, slot):
        copy.wait()

    zreal = z_ref[0:1, :]
    zimag = z_ref[1:2, :]
    totals = []
    for b in range(STEP):
        row = step * STEP + b
        right = jnp.concatenate(
            [held[index_ref[row * SLOTS + s]] for s in range(SLOTS)], axis=0
        )
        totals.append(jnp.dot(ham_buf[slot, b], right, preferred_element_type=F32))
    rights = []
    for b in range(STEP):
        current = held[RB + step * STEP + b].astype(F32)
        shifted = zreal * current + zimag * rotate_lanes(current)
        resid = (rhs_ref[b].astype(F32) - (shifted - totals[b])).astype(BF16).astype(F32)
        rights.append(split_points(resid, rotate_lanes(resid)).astype(BF16))
    for b in range(STEP):
        current = held[RB + step * STEP + b].astype(F32)
        left = jnp.concatenate([pre_buf[slot, 0, b], pre_buf[slot, 1, b]], axis=1)
        fresh[b] = (current + jnp.dot(left, rights[b], preferred_element_type=F32)).astype(BF16)
    if last:

        @pl.when(step < steps // 2)
        def _():
            out_ref[...] = fresh[...]

        @pl.when(step >= steps // 2)
        def _():
            second_ref[...] = fresh[...]


def sweep(index, ham, precond, rhs_unit, z, local, near, far, last):
    block = pl.BlockSpec((STEP, BS, LANES), lambda i, n: (i, 0, 0))
    anywhere = pl.BlockSpec(memory_space=pl.ANY)
    in_hbm = pl.BlockSpec(memory_space=pltpu.MemorySpace.HBM)
    scratch = [
        pltpu.VMEM((3 * RB + 1, BS, LANES), BF16),
        pltpu.SemaphoreType.DMA((7,)),
        pltpu.VMEM((2, STEP, BS, SLOTS * BS), BF16),
        pltpu.VMEM((2, 2, STEP, BS, LANES), BF16),
    ]
    if last:
        half = RB // STEP // 2
        out_specs = [
            pl.BlockSpec((STEP, BS, LANES), lambda i, n: (jnp.minimum(i, half - 1), 0, 0)),
            pl.BlockSpec((STEP, BS, LANES), lambda i, n: (jnp.maximum(i - half, 0), 0, 0)),
        ]
        out_shape = [jax.ShapeDtypeStruct((RB // 2, BS, LANES), BF16)] * 2
        scratch.append(pltpu.VMEM((STEP, BS, LANES), BF16))
    else:
        out_specs = [block]
        out_shape = [jax.ShapeDtypeStruct((RB, BS, LANES), BF16)]

    def kernel(*refs):
        sweep_kernel(last, *refs)

    return pl.pallas_call(
        kernel,
        grid_spec=pltpu.PrefetchScalarGridSpec(
            num_scalar_prefetch=1,
            grid=(RB // STEP,),
            in_specs=[
                in_hbm,
                in_hbm,
                block,
                pl.BlockSpec((8, LANES), lambda i, n: (0, 0)),
                anywhere,
                anywhere,
                anywhere,
            ],
            out_specs=out_specs,
            scratch_shapes=scratch,
        ),
        out_shape=out_shape,
        cost_estimate=pl.CostEstimate(
            flops=2 * RB * BS * SLOTS * BS * LANES, bytes_accessed=20 << 20, transcendentals=0
        ),
        compiler_params=pltpu.CompilerParams(vmem_limit_bytes=48 << 20),
        name="sweep_last" if last else "sweep",
    )(index, ham, precond, rhs_unit, z, local, near, far)


def weighted(own_ref, peer_ref, weight_ref):
    own, peer = own_ref[...], peer_ref[...]
    both = jnp.concatenate([own, peer, own, peer], axis=1)
    return jnp.dot(both, weight_ref[0], preferred_element_type=F32)


def combine_kernel(own_ref, peer_ref, weight_ref, send_ref):
    send_ref[...] = weighted(own_ref, peer_ref, weight_ref).astype(send_ref.dtype)


def combine(own, peer, weights, which, part, rows_step, kind=BF16):
    rows = peer.shape[0]
    row_spec = pl.BlockSpec((rows_step, LANES), lambda i: (i, 0))
    return pl.pallas_call(
        combine_kernel,
        grid=(rows // rows_step,),
        in_specs=[
            row_spec,
            row_spec,
            pl.BlockSpec((1, 4 * LANES, LANES), lambda i: (which, 0, part)),
        ],
        out_specs=row_spec,
        out_shape=jax.ShapeDtypeStruct((rows, LANES), kind),
        compiler_params=pltpu.CompilerParams(vmem_limit_bytes=8 << 20),
        cost_estimate=pl.CostEstimate(
            flops=2 * rows * 128 * 512, bytes_accessed=rows * LANES * 6, transcendentals=0
        ),
        name="combine",
    )(own, peer, weights)


def own_lanes(shape, unit):
    return (lane_ids(shape) // HALF) % 2 == unit


def to_own(x, unit):
    return pltpu.roll(x, HALF if unit else LANES - HALF, axis=1)


def from_own(x, unit):
    return pltpu.roll(x, LANES - HALF if unit else HALF, axis=1)


def fold_kernel(unit, own1, peer1, got1, weight1, own2, peer2, got2, weight2, send_ref, own_ref):
    top = weighted(own1, peer1, weight1) + got1[...].astype(F32)
    bottom = weighted(own2, peer2, weight2) + got2[...].astype(F32)
    own = own_lanes(top.shape, unit)
    send_ref[...] = jnp.where(own, to_own(top, unit), bottom).astype(BF16)
    own_ref[...] = jnp.where(own, top, from_own(bottom, unit))


def fold(unit, first, second, weights, rows, shift):
    def kernel(*refs):
        fold_kernel(unit, *refs)

    step = 1024
    spec = pl.BlockSpec((step, LANES), lambda i: (i, 0))
    late = pl.BlockSpec((step, LANES), lambda i: (i + shift // step, 0))

    def weight_spec(which):
        return pl.BlockSpec((1, 4 * LANES, LANES), lambda i: (which, 0, 1))

    return pl.pallas_call(
        kernel,
        grid=(rows // step,),
        in_specs=[spec] * 3 + [weight_spec(first[3])] + [late] * 3 + [weight_spec(second[3])],
        out_specs=[spec, spec],
        out_shape=[
            jax.ShapeDtypeStruct((rows, LANES), BF16),
            jax.ShapeDtypeStruct((rows, LANES), F32),
        ],
        compiler_params=pltpu.CompilerParams(vmem_limit_bytes=12 << 20),
        cost_estimate=pl.CostEstimate(
            flops=rows * LANES * 2048, bytes_accessed=rows * LANES * 18, transcendentals=0
        ),
        name="fold",
    )(*first[:3], weights, *second[:3], weights)


def finish_kernel(own1_ref, got1_ref, own2_ref, got2_ref, own_b_ref, got_b_ref, out_ref):
    unit_b = own_b_ref[...] + got_b_ref[...].astype(F32)
    first = own_lanes(unit_b.shape, 0)
    halves = pl.num_programs(0) // 2

    def store(place):
        top_a = place(own1_ref[...] + got1_ref[...].astype(F32))
        bottom_a = place(own2_ref[...] + got2_ref[...].astype(F32))
        out_ref[0, 0] = jnp.where(first, top_a, unit_b)
        out_ref[0, 1] = jnp.where(first, bottom_a, to_own(unit_b, 1))

    @pl.when(pl.program_id(0) < halves)
    def _():
        store(lambda x: x)

    @pl.when(pl.program_id(0) >= halves)
    def _():
        store(lambda x: to_own(x, 0))


def finish(own1, got1, own2, got2, own_b, got_b, step):
    rows = own_b.shape[0]
    half = rows // 2 // step
    spec = pl.BlockSpec((step, LANES), lambda i: (i, 0))
    spec_a = pl.BlockSpec((step, LANES), lambda i: (i % half, 0))
    return pl.pallas_call(
        finish_kernel,
        grid=(rows // step,),
        in_specs=[spec_a] * 4 + [spec] * 2,
        out_specs=pl.BlockSpec((1, 2, step, LANES), lambda i: (0, 0, i, 0)),
        out_shape=jax.ShapeDtypeStruct((1, 2, rows, LANES), F32),
        compiler_params=pltpu.CompilerParams(vmem_limit_bytes=10 << 20),
        name="finish",
    )(own1, got1, own2, got2, own_b, got_b)


def moment_coefs(plans):
    lane = lax.broadcasted_iota(jnp.int32, (1, 32, 2 * LANES), 2)
    line = lax.broadcasted_iota(jnp.int32, (1, 32, 2 * LANES), 1)
    point, kind = line // 8, line % 8
    tables = []
    for unit, owners, orders in plans:
        slot = lane // LANES * 2 + ((lane // HALF) % 2 ^ unit)
        owner = jnp.where(point < 2, owners[0], owners[1])
        low = jnp.where(slot == 0, orders[0], orders[1])
        high = jnp.where(slot == 2, orders[2], orders[3])
        order = jnp.where(slot < 2, low, high)
        turns = ((order + 1) * (2 * (owner * 2 + point % 2) + 1)) % (2 * POINTS)
        sign = jnp.where((lane // GROUP) % 2 == 0, -1.0, 1.0)
        phase = turns.astype(F32) * (math.pi / POINTS)
        quarter = jnp.where(kind == 0, math.pi / 2, 0.0)
        tables.append(jnp.where(kind == 0, 1.0, sign) * jnp.sin(phase + quarter) / POINTS)
    return jnp.concatenate(tables, axis=0)


def step(hamiltonian, columns, counts, precond, rhs):
    row_index = lax.axis_index("row")
    quad_index = lax.axis_index("quad")

    def swap(x, axis, peer_of):
        peers = [(i, peer_of(i)) for i in range(lax.axis_size(axis))]
        return lax.ppermute(x, axis, [(i, j) for i, j in peers if 0 <= j < len(peers)])

    def by_pair(i):
        return (((i // 2) ^ 1) * 2) + i % 2

    def by_mirror(i):
        return ((3 - i // 2) * 2) + i % 2

    def by_x(i):
        return i ^ 1

    def near_row(i):
        return i ^ 1

    def far_row(i):
        return i + 1 if i % 2 else i - 1

    units = list(initial(rhs, precond))

    live = jnp.arange(SLOTS)[None, :] < counts[:, None]
    index = jnp.where(live, columns - (row_index - 1) * RB, 3 * RB).reshape(RB * SLOTS)
    near_at = jnp.where(row_index % 2 == 1, 0, 2 * RB)
    index = jnp.concatenate([index, jnp.full((LANES,), near_at, jnp.int32)])
    lane = jnp.arange(LANES)[None, :]
    theta = 2.0 * jnp.pi * ((quad_index * 2 + lane // GROUP).astype(F32) + 0.5) / POINTS
    z = jnp.concatenate([jnp.cos(theta), jnp.sin(theta), jnp.zeros((6, LANES), F32)], axis=0)

    mine, other = quad_index, quad_index ^ 1
    pair, mirror = by_pair(quad_index), by_mirror(quad_index)
    coefs = moment_coefs(
        (
            (0, (mine, pair), (other, mirror ^ 1, mine, mirror)),
            (0, (mine, mirror), (other, pair ^ 1, mine, pair)),
            (1, (mine, pair), (mirror, mirror ^ 1, mine, other)),
            (1, (mine, mirror), (pair, pair ^ 1, mine, other)),
        ),
    )
    *rhs_units, weights = spread(rhs, coefs)

    grams = [None, None]
    for it in range(ITERS):
        for unit in range(2):
            y = units[unit]
            far = swap(y, "row", far_row)
            near = swap(y, "row", near_row)
            last = it == ITERS - 1
            got = sweep(
                index, hamiltonian, precond, rhs_units[unit], z, y, near, far, last
            )
            units[unit] = got[0]
            if last:
                units[unit] = got[:2]
                both = (part.reshape(-1, LANES) for part in got)
                parts = zip((rhs[: RB * BS // 2], rhs[RB * BS // 2 :]), both, strict=True)
                grams[unit] = sum(
                    lax.dot_general(x, part, (((0,), (0,)), ((), ())), preferred_element_type=F32)
                    for x, part in parts
                )

    half_rows = RB * BS // 2

    def first_stage(unit):
        top, bottom = (part.reshape(half_rows, LANES) for part in units[unit])
        got1 = swap(top, "quad", by_pair)
        got2 = swap(bottom, "quad", by_mirror)
        send1 = combine(top, got1, weights, 2 * unit, 0, 1024)
        send2 = combine(bottom, got2, weights, 2 * unit + 1, 0, 1024)
        return (top, got1), (bottom, got2), send1, send2

    pair_a1, pair_a2, send_a1, send_a2 = first_stage(0)
    got_a1 = swap(send_a1, "quad", by_x)
    got_a2 = swap(send_a2, "quad", by_x)
    quarter = half_rows // 2
    half = (*pair_a1, got_a1, 0)
    send_a1, own_a1 = fold(0, half, half, weights, quarter, quarter)
    half = (*pair_a2, got_a2, 1)
    send_a2, own_a2 = fold(0, half, half, weights, quarter, quarter)

    pair_b1, pair_b2, send_b1, send_b2 = first_stage(1)
    got_b1 = swap(send_b1, "quad", by_mirror)
    got_b2 = swap(send_b2, "quad", by_pair)
    halves = (*pair_b1, got_b1, 2), (*pair_b2, got_b2, 3)
    send_b, own_b = fold(1, *halves, weights, half_rows, 0)

    def rounded(x):
        return lax.reduce_precision(x, 8, 7)

    even = row_index % 2 == 0
    gram = jnp.where(even, grams[0], grams[1])
    gram = gram + swap(jnp.where(even, grams[1], grams[0]), "row", near_row)
    for bit in (8, 4, 2):
        gram = rounded(gram)
        peer = swap(gram.astype(BF16), "row", lambda i, bit=bit: i ^ bit)
        gram = gram + peer.astype(F32)
    gram = gram.astype(BF16)
    peer = swap(gram, "quad", by_pair)
    send_g = combine(gram, peer, weights, 2, 0, LANES)
    keep_g = combine(gram, peer, weights, 2, 1, LANES, F32)
    gram_sum = keep_g + swap(send_g, "quad", by_mirror).astype(F32)
    gram_got = swap(gram_sum.astype(BF16), "quad", by_x)
    gram_own = gram_sum + jnp.roll(gram_got, HALF, axis=1).astype(F32)
    gram_other = swap(gram_own, "row", near_row)
    gram_a = jnp.where(even, gram_own, gram_other)
    gram_b = jnp.where(even, gram_other, gram_own)
    first = own_lanes((LANES, LANES), 0)
    blocks = jnp.where(first, jnp.roll(gram_a, -HALF, axis=1), gram_b)
    blocks = (blocks * (1.0 / math.sqrt(RB * BS * 16)))[None]

    got_a1 = swap(send_a1, "quad", by_mirror)
    got_a2 = swap(send_a2, "quad", by_pair)
    got_b = swap(send_b, "quad", by_x)
    moments = finish(own_a1, got_a1, own_a2, got_a2, own_b, got_b, 512)
    return moments.reshape(1, RB * BS, LANES), blocks


def solution(mesh):
    return jax.shard_map(
        step,
        mesh=mesh,
        in_specs=(
            P("row", None, None),
            P("row", None),
            P("row"),
            P("quad", "row", None, None),
            P("row", None),
        ),
        out_specs=(P("quad", "row", None), P("quad", None, None)),
        check_vma=False,
    )
```

```python
import math

import jax
import jax.numpy as jnp
import numpy as np
from jax import lax
from jax.experimental import pallas as pl
from jax.experimental.pallas import tpu as pltpu
from jax.sharding import PartitionSpec as P

ITERS = 2
POINTS = 16
BS = 64
SLOTS = 24
RB = 64
LANES = 128
GROUP = 64
HALF = 32
STEP = 16
FIRST = 32
F32 = jnp.float32
BF16 = jnp.bfloat16


def unit_lanes(points):
    table = np.zeros((points * LANES, 2 * LANES), np.float32)
    for unit in range(2):
        for lane in range(LANES):
            point, part, col = lane // GROUP, (lane // HALF) % 2, lane % HALF
            src = (point % points) * LANES + part * GROUP + unit * HALF + col
            table[src, unit * LANES + lane] = 1.0
    return table


def in_hbm(x):
    return pltpu.with_memory_space_constraint(x, pltpu.MemorySpace.HBM)


def lane_ids(shape):
    return lax.broadcasted_iota(jnp.int32, shape, len(shape) - 1)


def split_points(top, bottom):
    lane = lane_ids(top.shape) % LANES
    first = lane < GROUP
    zero = jnp.zeros_like(top)
    return jnp.concatenate(
        [
            jnp.where(first, top, zero),
            jnp.where(first, bottom, zero),
            jnp.where(first, zero, top),
            jnp.where(first, zero, bottom),
        ],
        axis=0,
    )


def init_kernel(x_ref, pre_ref, map_ref, y_a_ref, y_b_ref):
    rights = []
    for b in range(FIRST):
        x = x_ref[b * BS : (b + 1) * BS].astype(F32)
        turned = pltpu.roll(x, GROUP, axis=1)
        turned = jnp.where(lane_ids(x.shape) < GROUP, -turned, turned)
        rights.append(jnp.concatenate([x, turned], axis=0).astype(BF16))
    outs = []
    for b in range(FIRST):
        left = jnp.concatenate([pre_ref[0, b], pre_ref[1, b]], axis=0)
        outs.append(jnp.dot(left, rights[b], preferred_element_type=F32))
    outs = [out.astype(BF16) for out in outs]
    firsts = [out[:BS] for out in outs]
    seconds = [out[BS:] for out in outs]
    both = jnp.concatenate(
        [jnp.concatenate(firsts, axis=0), jnp.concatenate(seconds, axis=0)], axis=1
    )
    out = jnp.dot(both, map_ref[...], preferred_element_type=F32).astype(BF16)
    y_a_ref[...] = out[:, :LANES].reshape(FIRST, BS, LANES)
    y_b_ref[...] = out[:, LANES:].reshape(FIRST, BS, LANES)


def initial(rhs, precond):
    block = jax.ShapeDtypeStruct((RB, BS, LANES), BF16)
    out_spec = pl.BlockSpec((FIRST, BS, LANES), lambda i: (i, 0, 0))
    return pl.pallas_call(
        init_kernel,
        grid=(RB // FIRST,),
        in_specs=[
            pl.BlockSpec((FIRST * BS, LANES), lambda i: (i, 0)),
            pl.BlockSpec((2, FIRST, BS, LANES), lambda i: (0, i, 0, 0)),
            pl.BlockSpec((2 * LANES, 2 * LANES), lambda i: (0, 0)),
        ],
        out_specs=[out_spec] * 2,
        out_shape=[block] * 2,
        name="initial",
    )(rhs, precond, jnp.asarray(unit_lanes(2), BF16))


def spread_kernel(x_ref, map_ref, coef_ref, rhs_a_ref, rhs_b_ref, weight_ref):
    out = jnp.dot(x_ref[...], map_ref[...], preferred_element_type=F32).astype(BF16)
    rhs_a_ref[...] = out[:, :LANES].reshape(rhs_a_ref.shape)
    rhs_b_ref[...] = out[:, LANES:].reshape(rhs_b_ref.shape)
    shape = (GROUP, 2 * LANES)
    r = lax.broadcasted_iota(jnp.int32, shape, 0)
    c = lax.broadcasted_iota(jnp.int32, shape, 1)
    same = r % HALF == c % HALF
    straight = same & ((r // HALF) == (c // GROUP) % 2)
    crossed = same & ((r // HALF) != (c // GROUP) % 2)
    for point in range(4):
        rows = coef_ref[0, point * 8 : point * 8 + 8]
        cosine, sine = rows[0:1, :], rows[1:2, :]
        value = jnp.where(straight, cosine, jnp.where(crossed, sine, 0.0))
        high = value.astype(BF16)
        weight_ref[0, point * GROUP : (point + 1) * GROUP] = high
        weight_ref[0, (4 + point) * GROUP : (5 + point) * GROUP] = (
            value - high.astype(F32)
        ).astype(BF16)


def spread(rhs, coefs):
    block = jax.ShapeDtypeStruct((RB, BS, LANES), BF16)
    out_spec = pl.BlockSpec((RB // 8, BS, LANES), lambda i: (i, 0, 0))
    return pl.pallas_call(
        spread_kernel,
        grid=(8,),
        in_specs=[
            pl.BlockSpec((RB // 8 * BS, LANES), lambda i: (i, 0)),
            pl.BlockSpec((LANES, 2 * LANES), lambda i: (0, 0)),
            pl.BlockSpec((1, 32, 2 * LANES), lambda i: (jnp.minimum(i, 4), 0, 0)),
        ],
        out_specs=[out_spec, out_spec, pl.BlockSpec((1, 512, 256), lambda i: (jnp.minimum(i, 4), 0, 0))],
        out_shape=[block, block, jax.ShapeDtypeStruct((5, 512, 256), BF16)],
        compiler_params=pltpu.CompilerParams(vmem_limit_bytes=14 << 20),
        cost_estimate=pl.CostEstimate(
            flops=2 * RB * BS * LANES * 256, bytes_accessed=3 << 20, transcendentals=0
        ),
        name="spread",
    )(rhs, jnp.asarray(unit_lanes(1), BF16), coefs)


def rotate_lanes(x):
    lane = lane_ids(x.shape) % GROUP
    up = pltpu.roll(x, LANES - HALF, axis=x.ndim - 1)
    down = pltpu.roll(x, HALF, axis=x.ndim - 1)
    return jnp.where(lane < HALF, -up, down)


def sweep_kernel(
    last, index_ref, ham_ref, pre_ref, rhs_ref, z_ref, local_ref, near_ref, far_ref,
    out_ref, *rest,
):
    if last:
        second_ref, held, sems, ham_buf, pre_buf, fresh = rest
    else:
        held, sems, ham_buf, pre_buf = rest
        fresh = out_ref
    step = pl.program_id(0)
    steps = pl.num_programs(0)
    slot = step % 2

    def fetch(at, to):
        blocks = pl.ds(pl.multiple_of(at * STEP, STEP), STEP)
        return (
            pltpu.make_async_copy(ham_ref.at[blocks], ham_buf.at[to], sems.at[3 + to]),
            pltpu.make_async_copy(pre_ref.at[:, blocks], pre_buf.at[to], sems.at[5 + to]),
        )

    @pl.when(step == 0)
    def _():
        copies = []
        near_at = index_ref[RB * SLOTS]
        places = (near_at, RB, 2 * RB - near_at)
        for n, ref in enumerate((near_ref, local_ref, far_ref)):
            place = pl.multiple_of(places[n], RB)
            copies.append(pltpu.make_async_copy(ref, held.at[pl.ds(place, RB)], sems.at[n]))
            copies[-1].start()
        for copy in fetch(0, 0):
            copy.start()
        held[3 * RB] = jnp.zeros((BS, LANES), BF16)
        for copy in copies:
            copy.wait()

    @pl.when(step + 1 < steps)
    def _():
        for copy in fetch(step + 1, 1 - slot):
            copy.start()

    for copy in fetch(step, slot):
        copy.wait()

    zreal = z_ref[0:1, :]
    zimag = z_ref[1:2, :]
    totals = []
    for b in range(STEP):
        row = step * STEP + b
        right = jnp.concatenate(
            [held[index_ref[row * SLOTS + s]] for s in range(SLOTS)], axis=0
        )
        totals.append(jnp.dot(ham_buf[slot, b], right, preferred_element_type=F32))
    rights = []
    for b in range(STEP):
        current = held[RB + step * STEP + b].astype(F32)
        shifted = zreal * current + zimag * rotate_lanes(current)
        resid = (rhs_ref[b].astype(F32) - (shifted - totals[b])).astype(BF16).astype(F32)
        rights.append(split_points(resid, rotate_lanes(resid)).astype(BF16))
    for b in range(STEP):
        current = held[RB + step * STEP + b].astype(F32)
        left = jnp.concatenate([pre_buf[slot, 0, b], pre_buf[slot, 1, b]], axis=1)
        fresh[b] = (current + jnp.dot(left, rights[b], preferred_element_type=F32)).astype(BF16)
    if last:

        @pl.when(step < steps // 2)
        def _():
            out_ref[...] = fresh[...]

        @pl.when(step >= steps // 2)
        def _():
            second_ref[...] = fresh[...]


def sweep(index, ham, precond, rhs_unit, z, local, near, far, last):
    block = pl.BlockSpec((STEP, BS, LANES), lambda i, n: (i, 0, 0))
    anywhere = pl.BlockSpec(memory_space=pl.ANY)
    raw = pl.BlockSpec(memory_space=pltpu.MemorySpace.HBM)
    scratch = [
        pltpu.VMEM((3 * RB + 1, BS, LANES), BF16),
        pltpu.SemaphoreType.DMA((7,)),
        pltpu.VMEM((2, STEP, BS, SLOTS * BS), BF16),
        pltpu.VMEM((2, 2, STEP, BS, LANES), BF16),
    ]
    if last:
        half = RB // STEP // 2
        out_specs = [
            pl.BlockSpec((STEP, BS, LANES), lambda i, n: (jnp.minimum(i, half - 1), 0, 0)),
            pl.BlockSpec((STEP, BS, LANES), lambda i, n: (jnp.maximum(i - half, 0), 0, 0)),
        ]
        out_shape = [jax.ShapeDtypeStruct((RB // 2, BS, LANES), BF16)] * 2
        scratch.append(pltpu.VMEM((STEP, BS, LANES), BF16))
    else:
        out_specs = [block]
        out_shape = [jax.ShapeDtypeStruct((RB, BS, LANES), BF16)]

    def kernel(*refs):
        sweep_kernel(last, *refs)

    return pl.pallas_call(
        kernel,
        grid_spec=pltpu.PrefetchScalarGridSpec(
            num_scalar_prefetch=1,
            grid=(RB // STEP,),
            in_specs=[
                raw,
                raw,
                block,
                pl.BlockSpec((8, LANES), lambda i, n: (0, 0)),
                anywhere,
                anywhere,
                anywhere,
            ],
            out_specs=out_specs,
            scratch_shapes=scratch,
        ),
        out_shape=out_shape,
        cost_estimate=pl.CostEstimate(
            flops=2 * RB * BS * SLOTS * BS * LANES, bytes_accessed=20 << 20, transcendentals=0
        ),
        compiler_params=pltpu.CompilerParams(vmem_limit_bytes=24 << 20),
        name="sweep_last" if last else "sweep",
    )(index, in_hbm(ham), in_hbm(precond), in_hbm(rhs_unit), z, in_hbm(local), near, far)


def weighted(own_ref, peer_ref, weight_ref):
    own, peer = own_ref[...], peer_ref[...]
    both = jnp.concatenate([own, peer, own, peer], axis=1)
    return jnp.dot(both, weight_ref[0], preferred_element_type=F32)


def combine_kernel(own_ref, peer_ref, weight_ref, send_ref):
    send_ref[...] = weighted(own_ref, peer_ref, weight_ref).astype(send_ref.dtype)


def combine(own, peer, weights, which, part, rows_step, kind=BF16):
    rows = peer.shape[0]
    row_spec = pl.BlockSpec((rows_step, LANES), lambda i: (i, 0))
    return pl.pallas_call(
        combine_kernel,
        grid=(rows // rows_step,),
        in_specs=[
            row_spec,
            row_spec,
            pl.BlockSpec((1, 4 * LANES, LANES), lambda i: (which, 0, part)),
        ],
        out_specs=row_spec,
        out_shape=jax.ShapeDtypeStruct((rows, LANES), kind),
        compiler_params=pltpu.CompilerParams(vmem_limit_bytes=8 << 20),
        cost_estimate=pl.CostEstimate(
            flops=2 * rows * 128 * 512, bytes_accessed=rows * LANES * 6, transcendentals=0
        ),
        name="combine",
    )(own, peer, weights)


def own_lanes(shape, unit):
    return (lane_ids(shape) // HALF) % 2 == unit


def to_own(x, unit):
    return pltpu.roll(x, HALF if unit else LANES - HALF, axis=1)


def from_own(x, unit):
    return pltpu.roll(x, LANES - HALF if unit else HALF, axis=1)


def fold_kernel(unit, own1, peer1, got1, weight1, own2, peer2, got2, weight2, send_ref, own_ref):
    top = weighted(own1, peer1, weight1) + got1[...].astype(F32)
    bottom = weighted(own2, peer2, weight2) + got2[...].astype(F32)
    own = own_lanes(top.shape, unit)
    send_ref[...] = jnp.where(own, to_own(top, unit), bottom).astype(BF16)
    own_ref[...] = jnp.where(own, top, from_own(bottom, unit))


def fold(unit, first, second, weights, rows, shift):
    def kernel(*refs):
        fold_kernel(unit, *refs)

    step = 1024
    spec = pl.BlockSpec((step, LANES), lambda i: (i, 0))
    late = pl.BlockSpec((step, LANES), lambda i: (i + shift // step, 0))

    def weight_spec(which):
        return pl.BlockSpec((1, 4 * LANES, LANES), lambda i: (which, 0, 1))

    return pl.pallas_call(
        kernel,
        grid=(rows // step,),
        in_specs=[spec] * 3 + [weight_spec(first[3])] + [late] * 3 + [weight_spec(second[3])],
        out_specs=[spec, spec],
        out_shape=[
            jax.ShapeDtypeStruct((rows, LANES), BF16),
            jax.ShapeDtypeStruct((rows, LANES), F32),
        ],
        compiler_params=pltpu.CompilerParams(vmem_limit_bytes=12 << 20),
        cost_estimate=pl.CostEstimate(
            flops=rows * LANES * 2048, bytes_accessed=rows * LANES * 18, transcendentals=0
        ),
        name="fold",
    )(*first[:3], weights, *second[:3], weights)


def finish_kernel(own1_ref, got1_ref, own2_ref, got2_ref, own_b_ref, got_b_ref, out_ref):
    unit_b = own_b_ref[...] + got_b_ref[...].astype(F32)
    first = own_lanes(unit_b.shape, 0)
    halves = pl.num_programs(0) // 2

    def store(place):
        top_a = place(own1_ref[...] + got1_ref[...].astype(F32))
        bottom_a = place(own2_ref[...] + got2_ref[...].astype(F32))
        out_ref[0, 0] = jnp.where(first, top_a, unit_b)
        out_ref[0, 1] = jnp.where(first, bottom_a, to_own(unit_b, 1))

    @pl.when(pl.program_id(0) < halves)
    def _():
        store(lambda x: x)

    @pl.when(pl.program_id(0) >= halves)
    def _():
        store(lambda x: to_own(x, 0))


def finish(own1, got1, own2, got2, own_b, got_b, step):
    rows = own_b.shape[0]
    half = rows // 2 // step
    spec = pl.BlockSpec((step, LANES), lambda i: (i, 0))
    spec_a = pl.BlockSpec((step, LANES), lambda i: (i % half, 0))
    return pl.pallas_call(
        finish_kernel,
        grid=(rows // step,),
        in_specs=[spec_a] * 4 + [spec] * 2,
        out_specs=pl.BlockSpec((1, 2, step, LANES), lambda i: (0, 0, i, 0)),
        out_shape=jax.ShapeDtypeStruct((1, 2, rows, LANES), F32),
        compiler_params=pltpu.CompilerParams(vmem_limit_bytes=10 << 20),
        name="finish",
    )(own1, got1, own2, got2, own_b, got_b)


def moment_coefs(plans):
    lane = lax.broadcasted_iota(jnp.int32, (1, 32, 2 * LANES), 2)
    line = lax.broadcasted_iota(jnp.int32, (1, 32, 2 * LANES), 1)
    point, kind = line // 8, line % 8
    tables = []
    for unit, owners, orders in plans:
        slot = lane // LANES * 2 + ((lane // HALF) % 2 ^ unit)
        owner = jnp.where(point < 2, owners[0], owners[1])
        low = jnp.where(slot == 0, orders[0], orders[1])
        high = jnp.where(slot == 2, orders[2], orders[3])
        order = jnp.where(slot < 2, low, high)
        turns = ((order + 1) * (2 * (owner * 2 + point % 2) + 1)) % (2 * POINTS)
        sign = jnp.where((lane // GROUP) % 2 == 0, -1.0, 1.0)
        phase = turns.astype(F32) * (math.pi / POINTS)
        quarter = jnp.where(kind == 0, math.pi / 2, 0.0)
        tables.append(jnp.where(kind == 0, 1.0, sign) * jnp.sin(phase + quarter) / POINTS)
    return jnp.concatenate(tables, axis=0)


def step(hamiltonian, columns, counts, precond, rhs):
    row_index = lax.axis_index("row")
    quad_index = lax.axis_index("quad")

    def swap(x, axis, peer_of):
        peers = [(i, peer_of(i)) for i in range(lax.axis_size(axis))]
        return lax.ppermute(x, axis, [(i, j) for i, j in peers if 0 <= j < len(peers)])

    def by_pair(i):
        return (((i // 2) ^ 1) * 2) + i % 2

    def by_mirror(i):
        return ((3 - i // 2) * 2) + i % 2

    def by_x(i):
        return i ^ 1

    def near_row(i):
        return i ^ 1

    def far_row(i):
        return i + 1 if i % 2 else i - 1

    units = list(initial(rhs, precond))

    live = jnp.arange(SLOTS)[None, :] < counts[:, None]
    index = jnp.where(live, columns - (row_index - 1) * RB, 3 * RB).reshape(RB * SLOTS)
    near_at = jnp.where(row_index % 2 == 1, 0, 2 * RB)
    index = jnp.concatenate([index, jnp.full((LANES,), near_at, jnp.int32)])
    lane = jnp.arange(LANES)[None, :]
    theta = 2.0 * jnp.pi * ((quad_index * 2 + lane // GROUP).astype(F32) + 0.5) / POINTS
    z = jnp.concatenate([jnp.cos(theta), jnp.sin(theta), jnp.zeros((6, LANES), F32)], axis=0)

    mine, other = quad_index, quad_index ^ 1
    pair, mirror = by_pair(quad_index), by_mirror(quad_index)
    coefs = moment_coefs(
        (
            (0, (mine, pair), (other, mirror ^ 1, mine, mirror)),
            (0, (mine, mirror), (other, pair ^ 1, mine, pair)),
            (1, (mine, pair), (mirror, mirror ^ 1, mine, other)),
            (1, (mine, mirror), (pair, pair ^ 1, mine, other)),
            (1, (mine, other), (pair, by_mirror(pair), mine, mirror)),
        ),
    )
    *rhs_units, weights = spread(rhs, coefs)

    grams = [None, None]
    for it in range(ITERS):
        for unit in range(2):
            y = units[unit]
            far = swap(y, "row", far_row)
            near = swap(y, "row", near_row)
            last = it == ITERS - 1
            got = sweep(
                index, hamiltonian, precond, rhs_units[unit], z, y, near, far, last
            )
            units[unit] = got[0]
            if last:
                units[unit] = got[:2]
                both = (part.reshape(-1, LANES) for part in got)
                parts = zip((rhs[: RB * BS // 2], rhs[RB * BS // 2 :]), both, strict=True)
                grams[unit] = sum(
                    lax.dot_general(x, part, (((0,), (0,)), ((), ())), preferred_element_type=F32)
                    for x, part in parts
                )

    half_rows = RB * BS // 2

    def first_stage(unit):
        top, bottom = (part.reshape(half_rows, LANES) for part in units[unit])
        got1 = swap(top, "quad", by_pair)
        got2 = swap(bottom, "quad", by_mirror)
        send1 = combine(top, got1, weights, 2 * unit, 0, 1024)
        send2 = combine(bottom, got2, weights, 2 * unit + 1, 0, 1024)
        return (top, got1), (bottom, got2), send1, send2

    pair_a1, pair_a2, send_a1, send_a2 = first_stage(0)
    got_a1 = swap(send_a1, "quad", by_x)
    got_a2 = swap(send_a2, "quad", by_x)
    quarter = half_rows // 2
    half = (*pair_a1, got_a1, 0)
    send_a1, own_a1 = fold(0, half, half, weights, quarter, quarter)
    half = (*pair_a2, got_a2, 1)
    send_a2, own_a2 = fold(0, half, half, weights, quarter, quarter)

    pair_b1, pair_b2, send_b1, send_b2 = first_stage(1)
    got_b1 = swap(send_b1, "quad", by_mirror)
    got_b2 = swap(send_b2, "quad", by_pair)
    halves = (*pair_b1, got_b1, 2), (*pair_b2, got_b2, 3)
    send_b, own_b = fold(1, *halves, weights, half_rows, 0)

    def rounded(x):
        return lax.reduce_precision(x, 8, 7)

    even = row_index % 2 == 0
    gram = jnp.where(even, grams[0], grams[1])
    gram = gram + swap(jnp.where(even, grams[1], grams[0]), "row", near_row)
    for bit in (8, 4, 2):
        gram = rounded(gram)
        peer = swap(gram.astype(BF16), "row", lambda i, bit=bit: i ^ bit)
        gram = gram + peer.astype(F32)
    gram = gram.astype(BF16)
    peer = swap(gram, "quad", by_x)
    send_g = combine(gram, peer, weights, 4, 0, LANES)
    keep_g = combine(gram, peer, weights, 4, 1, LANES, F32)
    gram_sum = keep_g + swap(send_g, "quad", by_pair).astype(F32)
    gram_got = swap(gram_sum.astype(BF16), "quad", by_mirror)
    gram_own = gram_sum + jnp.roll(gram_got, HALF, axis=1).astype(F32)
    gram_other = swap(gram_own, "row", near_row)
    gram_a = jnp.where(even, gram_own, gram_other)
    gram_b = jnp.where(even, gram_other, gram_own)
    first = own_lanes((LANES, LANES), 0)
    blocks = jnp.where(first, jnp.roll(gram_a, -HALF, axis=1), gram_b)
    blocks = (blocks * (1.0 / math.sqrt(RB * BS * 16)))[None]

    got_a1 = swap(send_a1, "quad", by_mirror)
    got_a2 = swap(send_a2, "quad", by_pair)
    got_b = swap(send_b, "quad", by_x)
    moments = finish(own_a1, got_a1, own_a2, got_a2, own_b, got_b, 512)
    return moments.reshape(1, RB * BS, LANES), blocks


def solution(mesh):
    return jax.shard_map(
        step,
        mesh=mesh,
        in_specs=(
            P("row", None, None),
            P("row", None),
            P("row"),
            P("quad", "row", None, None),
            P("row", None),
        ),
        out_specs=(P("quad", "row", None), P("quad", None, None)),
        check_vma=False,
    )
```

```python
import math

import jax
import jax.numpy as jnp
import numpy as np
from jax import lax
from jax.experimental import pallas as pl
from jax.experimental.pallas import tpu as pltpu
from jax.sharding import PartitionSpec as P

ITERS = 2
POINTS = 16
BS = 64
SLOTS = 24
RB = 64
LANES = 128
GROUP = 64
HALF = 32
STEP = 16
FIRST = 32
F32 = jnp.float32
BF16 = jnp.bfloat16


def unit_lanes(points):
    table = np.zeros((points * LANES, 2 * LANES), np.float32)
    for unit in range(2):
        for lane in range(LANES):
            point, part, col = lane // GROUP, (lane // HALF) % 2, lane % HALF
            src = (point % points) * LANES + part * GROUP + unit * HALF + col
            table[src, unit * LANES + lane] = 1.0
    return table


def lane_ids(shape):
    return lax.broadcasted_iota(jnp.int32, shape, len(shape) - 1)


def split_points(top, bottom):
    lane = lane_ids(top.shape) % LANES
    first = lane < GROUP
    zero = jnp.zeros_like(top)
    return jnp.concatenate(
        [
            jnp.where(first, top, zero),
            jnp.where(first, bottom, zero),
            jnp.where(first, zero, top),
            jnp.where(first, zero, bottom),
        ],
        axis=0,
    )


def init_kernel(x_ref, pre_ref, map_ref, y_a_ref, y_b_ref):
    rights = []
    for b in range(FIRST):
        x = x_ref[b * BS : (b + 1) * BS].astype(F32)
        turned = pltpu.roll(x, GROUP, axis=1)
        turned = jnp.where(lane_ids(x.shape) < GROUP, -turned, turned)
        rights.append(jnp.concatenate([x, turned], axis=0).astype(BF16))
    outs = []
    for b in range(FIRST):
        left = jnp.concatenate([pre_ref[0, b], pre_ref[1, b]], axis=0)
        outs.append(jnp.dot(left, rights[b], preferred_element_type=F32))
    outs = [out.astype(BF16) for out in outs]
    firsts = [out[:BS] for out in outs]
    seconds = [out[BS:] for out in outs]
    both = jnp.concatenate(
        [jnp.concatenate(firsts, axis=0), jnp.concatenate(seconds, axis=0)], axis=1
    )
    out = jnp.dot(both, map_ref[...], preferred_element_type=F32).astype(BF16)
    y_a_ref[...] = out[:, :LANES].reshape(FIRST, BS, LANES)
    y_b_ref[...] = out[:, LANES:].reshape(FIRST, BS, LANES)


def initial(rhs, precond):
    block = jax.ShapeDtypeStruct((RB, BS, LANES), BF16)
    out_spec = pl.BlockSpec((FIRST, BS, LANES), lambda i: (i, 0, 0))
    return pl.pallas_call(
        init_kernel,
        grid=(RB // FIRST,),
        in_specs=[
            pl.BlockSpec((FIRST * BS, LANES), lambda i: (i, 0)),
            pl.BlockSpec((2, FIRST, BS, LANES), lambda i: (0, i, 0, 0)),
            pl.BlockSpec((2 * LANES, 2 * LANES), lambda i: (0, 0)),
        ],
        out_specs=[out_spec] * 2,
        out_shape=[block] * 2,
        name="initial",
    )(rhs, precond, jnp.asarray(unit_lanes(2), BF16))


def spread_kernel(x_ref, map_ref, coef_ref, rhs_a_ref, rhs_b_ref, weight_ref):
    out = jnp.dot(x_ref[...], map_ref[...], preferred_element_type=F32).astype(BF16)
    rhs_a_ref[...] = out[:, :LANES].reshape(rhs_a_ref.shape)
    rhs_b_ref[...] = out[:, LANES:].reshape(rhs_b_ref.shape)
    shape = (GROUP, 2 * LANES)
    r = lax.broadcasted_iota(jnp.int32, shape, 0)
    c = lax.broadcasted_iota(jnp.int32, shape, 1)
    same = r % HALF == c % HALF
    straight = same & ((r // HALF) == (c // GROUP) % 2)
    crossed = same & ((r // HALF) != (c // GROUP) % 2)
    for point in range(4):
        rows = coef_ref[0, point * 8 : point * 8 + 8]
        cosine, sine = rows[0:1, :], rows[1:2, :]
        value = jnp.where(straight, cosine, jnp.where(crossed, sine, 0.0))
        high = value.astype(BF16)
        weight_ref[0, point * GROUP : (point + 1) * GROUP] = high
        weight_ref[0, (4 + point) * GROUP : (5 + point) * GROUP] = (
            value - high.astype(F32)
        ).astype(BF16)


def spread(rhs, coefs):
    block = jax.ShapeDtypeStruct((RB, BS, LANES), BF16)
    out_spec = pl.BlockSpec((RB // 8, BS, LANES), lambda i: (i, 0, 0))
    return pl.pallas_call(
        spread_kernel,
        grid=(8,),
        in_specs=[
            pl.BlockSpec((RB // 8 * BS, LANES), lambda i: (i, 0)),
            pl.BlockSpec((LANES, 2 * LANES), lambda i: (0, 0)),
            pl.BlockSpec((1, 32, 2 * LANES), lambda i: (jnp.minimum(i, 4), 0, 0)),
        ],
        out_specs=[out_spec, out_spec, pl.BlockSpec((1, 512, 256), lambda i: (jnp.minimum(i, 4), 0, 0))],
        out_shape=[block, block, jax.ShapeDtypeStruct((5, 512, 256), BF16)],
        compiler_params=pltpu.CompilerParams(vmem_limit_bytes=14 << 20),
        cost_estimate=pl.CostEstimate(
            flops=2 * RB * BS * LANES * 256, bytes_accessed=3 << 20, transcendentals=0
        ),
        name="spread",
    )(rhs, jnp.asarray(unit_lanes(1), BF16), coefs)


def rotate_lanes(x):
    lane = lane_ids(x.shape) % GROUP
    up = pltpu.roll(x, LANES - HALF, axis=x.ndim - 1)
    down = pltpu.roll(x, HALF, axis=x.ndim - 1)
    return jnp.where(lane < HALF, -up, down)


def sweep_kernel(
    last, index_ref, ham_ref, pre_ref, rhs_ref, z_ref, local_ref, near_ref, far_ref,
    out_ref, *rest,
):
    if last:
        second_ref, held, sems, ham_buf, pre_buf, fresh = rest
    else:
        held, sems, ham_buf, pre_buf = rest
        fresh = out_ref
    step = pl.program_id(0)
    steps = pl.num_programs(0)
    slot = step % 2

    def fetch(at, to):
        blocks = pl.ds(pl.multiple_of(at * STEP, STEP), STEP)
        return (
            pltpu.make_async_copy(ham_ref.at[blocks], ham_buf.at[to], sems.at[3 + to]),
            pltpu.make_async_copy(pre_ref.at[:, blocks], pre_buf.at[to], sems.at[5 + to]),
        )

    @pl.when(step == 0)
    def _():
        copies = []
        near_at = index_ref[RB * SLOTS]
        places = (near_at, RB, 2 * RB - near_at)
        for n, ref in enumerate((near_ref, local_ref, far_ref)):
            place = pl.multiple_of(places[n], RB)
            copies.append(pltpu.make_async_copy(ref, held.at[pl.ds(place, RB)], sems.at[n]))
            copies[-1].start()
        for copy in fetch(0, 0):
            copy.start()
        held[3 * RB] = jnp.zeros((BS, LANES), BF16)
        for copy in copies:
            copy.wait()

    @pl.when(step + 1 < steps)
    def _():
        for copy in fetch(step + 1, 1 - slot):
            copy.start()

    for copy in fetch(step, slot):
        copy.wait()

    zreal = z_ref[0:1, :]
    zimag = z_ref[1:2, :]
    totals = []
    for b in range(STEP):
        row = step * STEP + b
        right = jnp.concatenate(
            [held[index_ref[row * SLOTS + s]] for s in range(SLOTS)], axis=0
        )
        totals.append(jnp.dot(ham_buf[slot, b], right, preferred_element_type=F32))
    rights = []
    for b in range(STEP):
        current = held[RB + step * STEP + b].astype(F32)
        shifted = zreal * current + zimag * rotate_lanes(current)
        resid = (rhs_ref[b].astype(F32) - (shifted - totals[b])).astype(BF16).astype(F32)
        rights.append(split_points(resid, rotate_lanes(resid)).astype(BF16))
    for b in range(STEP):
        current = held[RB + step * STEP + b].astype(F32)
        left = jnp.concatenate([pre_buf[slot, 0, b], pre_buf[slot, 1, b]], axis=1)
        fresh[b] = (current + jnp.dot(left, rights[b], preferred_element_type=F32)).astype(BF16)
    if last:

        @pl.when(step < steps // 2)
        def _():
            out_ref[...] = fresh[...]

        @pl.when(step >= steps // 2)
        def _():
            second_ref[...] = fresh[...]


def sweep(index, ham, precond, rhs_unit, z, local, near, far, last):
    block = pl.BlockSpec((STEP, BS, LANES), lambda i, n: (i, 0, 0))
    anywhere = pl.BlockSpec(memory_space=pl.ANY)
    raw = pl.BlockSpec(memory_space=pltpu.MemorySpace.HBM)
    scratch = [
        pltpu.VMEM((3 * RB + 1, BS, LANES), BF16),
        pltpu.SemaphoreType.DMA((7,)),
        pltpu.VMEM((2, STEP, BS, SLOTS * BS), BF16),
        pltpu.VMEM((2, 2, STEP, BS, LANES), BF16),
    ]
    if last:
        half = RB // STEP // 2
        out_specs = [
            pl.BlockSpec((STEP, BS, LANES), lambda i, n: (jnp.minimum(i, half - 1), 0, 0)),
            pl.BlockSpec((STEP, BS, LANES), lambda i, n: (jnp.maximum(i - half, 0), 0, 0)),
        ]
        out_shape = [jax.ShapeDtypeStruct((RB // 2, BS, LANES), BF16)] * 2
        scratch.append(pltpu.VMEM((STEP, BS, LANES), BF16))
    else:
        out_specs = [block]
        out_shape = [jax.ShapeDtypeStruct((RB, BS, LANES), BF16)]

    def kernel(*refs):
        sweep_kernel(last, *refs)

    return pl.pallas_call(
        kernel,
        grid_spec=pltpu.PrefetchScalarGridSpec(
            num_scalar_prefetch=1,
            grid=(RB // STEP,),
            in_specs=[
                raw,
                raw,
                block,
                pl.BlockSpec((8, LANES), lambda i, n: (0, 0)),
                anywhere,
                anywhere,
                anywhere,
            ],
            out_specs=out_specs,
            scratch_shapes=scratch,
        ),
        out_shape=out_shape,
        cost_estimate=pl.CostEstimate(
            flops=2 * RB * BS * SLOTS * BS * LANES, bytes_accessed=20 << 20, transcendentals=0
        ),
        compiler_params=pltpu.CompilerParams(vmem_limit_bytes=48 << 20),
        name="sweep_last" if last else "sweep",
    )(index, ham, precond, rhs_unit, z, local, near, far)


def combine_kernel(own_ref, peer_ref, weight_ref, send_ref, keep_ref):
    own, peer = own_ref[...], peer_ref[...]
    both = jnp.concatenate([own, peer, own, peer], axis=1)
    out = jnp.dot(both, weight_ref[0], preferred_element_type=F32)
    send_ref[...] = out[:, :LANES].astype(BF16)
    keep_ref[...] = out[:, LANES:].astype(keep_ref.dtype)


def combine(own, peer, weights, which, rows_step, kind=BF16):
    rows = peer.shape[0]
    row_spec = pl.BlockSpec((rows_step, LANES), lambda i: (i, 0))
    return pl.pallas_call(
        combine_kernel,
        grid=(rows // rows_step,),
        in_specs=[
            row_spec,
            row_spec,
            pl.BlockSpec((1, 4 * LANES, 2 * LANES), lambda i: (which, 0, 0)),
        ],
        out_specs=[row_spec, row_spec],
        out_shape=[
            jax.ShapeDtypeStruct((rows, LANES), BF16),
            jax.ShapeDtypeStruct((rows, LANES), kind),
        ],
        compiler_params=pltpu.CompilerParams(vmem_limit_bytes=8 << 20),
        cost_estimate=pl.CostEstimate(
            flops=2 * rows * 256 * 512, bytes_accessed=rows * LANES * 8, transcendentals=0
        ),
        name="combine",
    )(own, peer, weights)


def own_lanes(shape, unit):
    return (lane_ids(shape) // HALF) % 2 == unit


def to_own(x, unit):
    return pltpu.roll(x, HALF if unit else LANES - HALF, axis=1)


def from_own(x, unit):
    return pltpu.roll(x, LANES - HALF if unit else HALF, axis=1)


def fold_kernel(unit, keep1_ref, got1_ref, keep2_ref, got2_ref, send_ref, own_ref):
    top = keep1_ref[...].astype(F32) + got1_ref[...].astype(F32)
    bottom = keep2_ref[...].astype(F32) + got2_ref[...].astype(F32)
    own = own_lanes(top.shape, unit)
    send_ref[...] = jnp.where(own, to_own(top, unit), bottom).astype(BF16)
    own_ref[...] = jnp.where(own, top, from_own(bottom, unit))


def fold(unit, first, second, rows, shift):
    def kernel(*refs):
        fold_kernel(unit, *refs)

    step = 1024
    spec = pl.BlockSpec((step, LANES), lambda i: (i, 0))
    late = pl.BlockSpec((step, LANES), lambda i: (i + shift // step, 0))
    return pl.pallas_call(
        kernel,
        grid=(rows // step,),
        in_specs=[spec, spec, late, late],
        out_specs=[spec, spec],
        out_shape=[
            jax.ShapeDtypeStruct((rows, LANES), BF16),
            jax.ShapeDtypeStruct((rows, LANES), F32),
        ],
        compiler_params=pltpu.CompilerParams(vmem_limit_bytes=10 << 20),
        cost_estimate=pl.CostEstimate(
            flops=rows * LANES * 8, bytes_accessed=rows * LANES * 14, transcendentals=0
        ),
        name="fold",
    )(*first, *second)


def finish_kernel(own1_ref, got1_ref, own2_ref, got2_ref, own_b_ref, got_b_ref, out_ref):
    unit_b = own_b_ref[...] + got_b_ref[...].astype(F32)
    first = own_lanes(unit_b.shape, 0)
    halves = pl.num_programs(0) // 2

    def store(place):
        top_a = place(own1_ref[...] + got1_ref[...].astype(F32))
        bottom_a = place(own2_ref[...] + got2_ref[...].astype(F32))
        out_ref[0, 0] = jnp.where(first, top_a, unit_b)
        out_ref[0, 1] = jnp.where(first, bottom_a, to_own(unit_b, 1))

    @pl.when(pl.program_id(0) < halves)
    def _():
        store(lambda x: x)

    @pl.when(pl.program_id(0) >= halves)
    def _():
        store(lambda x: to_own(x, 0))


def finish(own1, got1, own2, got2, own_b, got_b, step):
    rows = own_b.shape[0]
    half = rows // 2 // step
    spec = pl.BlockSpec((step, LANES), lambda i: (i, 0))
    spec_a = pl.BlockSpec((step, LANES), lambda i: (i % half, 0))
    return pl.pallas_call(
        finish_kernel,
        grid=(rows // step,),
        in_specs=[spec_a] * 4 + [spec] * 2,
        out_specs=pl.BlockSpec((1, 2, step, LANES), lambda i: (0, 0, i, 0)),
        out_shape=jax.ShapeDtypeStruct((1, 2, rows, LANES), F32),
        compiler_params=pltpu.CompilerParams(vmem_limit_bytes=10 << 20),
        name="finish",
    )(own1, got1, own2, got2, own_b, got_b)


def moment_coefs(plans):
    lane = lax.broadcasted_iota(jnp.int32, (1, 32, 2 * LANES), 2)
    line = lax.broadcasted_iota(jnp.int32, (1, 32, 2 * LANES), 1)
    point, kind = line // 8, line % 8
    tables = []
    for unit, owners, orders in plans:
        slot = lane // LANES * 2 + ((lane // HALF) % 2 ^ unit)
        owner = jnp.where(point < 2, owners[0], owners[1])
        low = jnp.where(slot == 0, orders[0], orders[1])
        high = jnp.where(slot == 2, orders[2], orders[3])
        order = jnp.where(slot < 2, low, high)
        turns = ((order + 1) * (2 * (owner * 2 + point % 2) + 1)) % (2 * POINTS)
        sign = jnp.where((lane // GROUP) % 2 == 0, -1.0, 1.0)
        phase = turns.astype(F32) * (math.pi / POINTS)
        quarter = jnp.where(kind == 0, math.pi / 2, 0.0)
        tables.append(jnp.where(kind == 0, 1.0, sign) * jnp.sin(phase + quarter) / POINTS)
    return jnp.concatenate(tables, axis=0)


def step(hamiltonian, columns, counts, precond, rhs):
    row_index = lax.axis_index("row")
    quad_index = lax.axis_index("quad")

    def swap(x, axis, peer_of):
        peers = [(i, peer_of(i)) for i in range(lax.axis_size(axis))]
        return lax.ppermute(x, axis, [(i, j) for i, j in peers if 0 <= j < len(peers)])

    def by_pair(i):
        return (((i // 2) ^ 1) * 2) + i % 2

    def by_mirror(i):
        return ((3 - i // 2) * 2) + i % 2

    def by_x(i):
        return i ^ 1

    def near_row(i):
        return i ^ 1

    def far_row(i):
        return i + 1 if i % 2 else i - 1

    units = list(initial(rhs, precond))

    live = jnp.arange(SLOTS)[None, :] < counts[:, None]
    index = jnp.where(live, columns - (row_index - 1) * RB, 3 * RB).reshape(RB * SLOTS)
    near_at = jnp.where(row_index % 2 == 1, 0, 2 * RB)
    index = jnp.concatenate([index, jnp.full((LANES,), near_at, jnp.int32)])
    lane = jnp.arange(LANES)[None, :]
    theta = 2.0 * jnp.pi * ((quad_index * 2 + lane // GROUP).astype(F32) + 0.5) / POINTS
    z = jnp.concatenate([jnp.cos(theta), jnp.sin(theta), jnp.zeros((6, LANES), F32)], axis=0)

    mine, other = quad_index, quad_index ^ 1
    pair, mirror = by_pair(quad_index), by_mirror(quad_index)
    coefs = moment_coefs(
        (
            (0, (mine, pair), (other, mirror ^ 1, mine, mirror)),
            (0, (mine, mirror), (other, pair ^ 1, mine, pair)),
            (1, (mine, pair), (mirror, mirror ^ 1, mine, other)),
            (1, (mine, mirror), (pair, pair ^ 1, mine, other)),
            (1, (mine, other), (pair, by_mirror(pair), mine, mirror)),
        ),
    )
    *rhs_units, weights = spread(rhs, coefs)

    grams = [None, None]
    for it in range(ITERS):
        for unit in range(2):
            y = units[unit]
            far = swap(y, "row", far_row)
            near = swap(y, "row", near_row)
            last = it == ITERS - 1
            got = sweep(
                index, hamiltonian, precond, rhs_units[unit], z, y, near, far, last
            )
            units[unit] = got[0]
            if last:
                units[unit] = got[:2]
                both = (part.reshape(-1, LANES) for part in got)
                parts = zip((rhs[: RB * BS // 2], rhs[RB * BS // 2 :]), both, strict=True)
                grams[unit] = sum(
                    lax.dot_general(x, part, (((0,), (0,)), ((), ())), preferred_element_type=F32)
                    for x, part in parts
                )

    half_rows = RB * BS // 2

    def first_stage(unit):
        top, bottom = (part.reshape(half_rows, LANES) for part in units[unit])
        got1 = swap(top, "quad", by_pair)
        got2 = swap(bottom, "quad", by_mirror)
        out1 = combine(top, got1, weights, 2 * unit, 1024)
        out2 = combine(bottom, got2, weights, 2 * unit + 1, 1024)
        return *out1, *out2

    send_a1, keep_a1, send_a2, keep_a2 = first_stage(0)
    got_a1 = swap(send_a1, "quad", by_x)
    got_a2 = swap(send_a2, "quad", by_x)
    quarter = half_rows // 2
    half = (keep_a1, got_a1)
    send_a1, own_a1 = fold(0, half, half, quarter, quarter)
    half = (keep_a2, got_a2)
    send_a2, own_a2 = fold(0, half, half, quarter, quarter)

    send_b1, keep_b1, send_b2, keep_b2 = first_stage(1)
    got_b1 = swap(send_b1, "quad", by_mirror)
    got_b2 = swap(send_b2, "quad", by_pair)
    send_b, own_b = fold(1, (keep_b1, got_b1), (keep_b2, got_b2), half_rows, 0)

    def rounded(x):
        return lax.reduce_precision(x, 8, 7)

    even = row_index % 2 == 0
    gram = jnp.where(even, grams[0], grams[1])
    gram = gram + swap(jnp.where(even, grams[1], grams[0]), "row", near_row)
    for bit in (8, 4, 2):
        gram = rounded(gram)
        peer = swap(gram.astype(BF16), "row", lambda i, bit=bit: i ^ bit)
        gram = gram + peer.astype(F32)
    gram = gram.astype(BF16)
    peer = swap(gram, "quad", by_x)
    send_g, keep_g = combine(gram, peer, weights, 4, LANES, F32)
    gram_sum = keep_g + swap(send_g, "quad", by_pair).astype(F32)
    gram_got = swap(gram_sum.astype(BF16), "quad", by_mirror)
    gram_own = gram_sum + jnp.roll(gram_got, HALF, axis=1).astype(F32)
    gram_other = swap(gram_own, "row", near_row)
    gram_a = jnp.where(even, gram_own, gram_other)
    gram_b = jnp.where(even, gram_other, gram_own)
    first = own_lanes((LANES, LANES), 0)
    blocks = jnp.where(first, jnp.roll(gram_a, -HALF, axis=1), gram_b)
    blocks = (blocks * (1.0 / math.sqrt(RB * BS * 16)))[None]

    got_a1 = swap(send_a1, "quad", by_mirror)
    got_a2 = swap(send_a2, "quad", by_pair)
    got_b = swap(send_b, "quad", by_x)
    moments = finish(own_a1, got_a1, own_a2, got_a2, own_b, got_b, 512)
    return moments.reshape(1, RB * BS, LANES), blocks


def solution(mesh):
    return jax.shard_map(
        step,
        mesh=mesh,
        in_specs=(
            P("row", None, None),
            P("row", None),
            P("row"),
            P("quad", "row", None, None),
            P("row", None),
        ),
        out_specs=(P("quad", "row", None), P("quad", None, None)),
        check_vma=False,
    )
```

```python
import math

import jax
import jax.numpy as jnp
import numpy as np
from jax import lax
from jax.experimental import pallas as pl
from jax.experimental.pallas import tpu as pltpu
from jax.sharding import PartitionSpec as P

ITERS = 2
POINTS = 16
BS = 64
SLOTS = 24
RB = 64
LANES = 128
GROUP = 64
HALF = 32
STEP = 16
FIRST = 32
F32 = jnp.float32
BF16 = jnp.bfloat16


def unit_lanes(points):
    table = np.zeros((points * LANES, 2 * LANES), np.float32)
    for unit in range(2):
        for lane in range(LANES):
            point, part, col = lane // GROUP, (lane // HALF) % 2, lane % HALF
            src = (point % points) * LANES + part * GROUP + unit * HALF + col
            table[src, unit * LANES + lane] = 1.0
    return table


def in_hbm(x):
    return pltpu.with_memory_space_constraint(x, pltpu.MemorySpace.HBM)


def lane_ids(shape):
    return lax.broadcasted_iota(jnp.int32, shape, len(shape) - 1)


def split_points(top, bottom):
    lane = lane_ids(top.shape) % LANES
    first = lane < GROUP
    zero = jnp.zeros_like(top)
    return jnp.concatenate(
        [
            jnp.where(first, top, zero),
            jnp.where(first, bottom, zero),
            jnp.where(first, zero, top),
            jnp.where(first, zero, bottom),
        ],
        axis=0,
    )


def init_kernel(x_ref, pre_ref, map_ref, y_a_ref, y_b_ref):
    rights = []
    for b in range(FIRST):
        x = x_ref[b * BS : (b + 1) * BS].astype(F32)
        turned = pltpu.roll(x, GROUP, axis=1)
        turned = jnp.where(lane_ids(x.shape) < GROUP, -turned, turned)
        rights.append(jnp.concatenate([x, turned], axis=0).astype(BF16))
    outs = []
    for b in range(FIRST):
        left = jnp.concatenate([pre_ref[0, b], pre_ref[1, b]], axis=0)
        outs.append(jnp.dot(left, rights[b], preferred_element_type=F32))
    outs = [out.astype(BF16) for out in outs]
    firsts = [out[:BS] for out in outs]
    seconds = [out[BS:] for out in outs]
    both = jnp.concatenate(
        [jnp.concatenate(firsts, axis=0), jnp.concatenate(seconds, axis=0)], axis=1
    )
    out = jnp.dot(both, map_ref[...], preferred_element_type=F32).astype(BF16)
    y_a_ref[...] = out[:, :LANES].reshape(FIRST, BS, LANES)
    y_b_ref[...] = out[:, LANES:].reshape(FIRST, BS, LANES)


def initial(rhs, precond):
    block = jax.ShapeDtypeStruct((RB, BS, LANES), BF16)
    out_spec = pl.BlockSpec((FIRST, BS, LANES), lambda i: (i, 0, 0))
    return pl.pallas_call(
        init_kernel,
        grid=(RB // FIRST,),
        in_specs=[
            pl.BlockSpec((FIRST * BS, LANES), lambda i: (i, 0)),
            pl.BlockSpec((2, FIRST, BS, LANES), lambda i: (0, i, 0, 0)),
            pl.BlockSpec((2 * LANES, 2 * LANES), lambda i: (0, 0)),
        ],
        out_specs=[out_spec] * 2,
        out_shape=[block] * 2,
        name="initial",
    )(rhs, precond, jnp.asarray(unit_lanes(2), BF16))


def spread_kernel(x_ref, map_ref, coef_ref, rhs_a_ref, rhs_b_ref, weight_ref):
    out = jnp.dot(x_ref[...], map_ref[...], preferred_element_type=F32).astype(BF16)
    rhs_a_ref[...] = out[:, :LANES].reshape(rhs_a_ref.shape)
    rhs_b_ref[...] = out[:, LANES:].reshape(rhs_b_ref.shape)
    shape = (GROUP, 2 * LANES)
    r = lax.broadcasted_iota(jnp.int32, shape, 0)
    c = lax.broadcasted_iota(jnp.int32, shape, 1)
    same = r % HALF == c % HALF
    straight = same & ((r // HALF) == (c // GROUP) % 2)
    crossed = same & ((r // HALF) != (c // GROUP) % 2)
    for point in range(4):
        rows = coef_ref[0, point * 8 : point * 8 + 8]
        cosine, sine = rows[0:1, :], rows[1:2, :]
        value = jnp.where(straight, cosine, jnp.where(crossed, sine, 0.0))
        high = value.astype(BF16)
        weight_ref[0, point * GROUP : (point + 1) * GROUP] = high
        weight_ref[0, (4 + point) * GROUP : (5 + point) * GROUP] = (
            value - high.astype(F32)
        ).astype(BF16)


def spread(rhs, coefs):
    block = jax.ShapeDtypeStruct((RB, BS, LANES), BF16)
    out_spec = pl.BlockSpec((RB // 8, BS, LANES), lambda i: (i, 0, 0))
    return pl.pallas_call(
        spread_kernel,
        grid=(8,),
        in_specs=[
            pl.BlockSpec((RB // 8 * BS, LANES), lambda i: (i, 0)),
            pl.BlockSpec((LANES, 2 * LANES), lambda i: (0, 0)),
            pl.BlockSpec((1, 32, 2 * LANES), lambda i: (jnp.minimum(i, 4), 0, 0)),
        ],
        out_specs=[out_spec, out_spec, pl.BlockSpec((1, 512, 256), lambda i: (jnp.minimum(i, 4), 0, 0))],
        out_shape=[block, block, jax.ShapeDtypeStruct((5, 512, 256), BF16)],
        compiler_params=pltpu.CompilerParams(vmem_limit_bytes=14 << 20),
        cost_estimate=pl.CostEstimate(
            flops=2 * RB * BS * LANES * 256, bytes_accessed=3 << 20, transcendentals=0
        ),
        name="spread",
    )(rhs, jnp.asarray(unit_lanes(1), BF16), coefs)


def rotate_lanes(x):
    lane = lane_ids(x.shape) % GROUP
    up = pltpu.roll(x, LANES - HALF, axis=x.ndim - 1)
    down = pltpu.roll(x, HALF, axis=x.ndim - 1)
    return jnp.where(lane < HALF, -up, down)


def sweep_kernel(
    last, index_ref, ham_ref, pre_ref, rhs_ref, z_ref, local_ref, near_ref, far_ref,
    out_ref, *rest,
):
    if last:
        second_ref, held, sems, ham_buf, pre_buf, fresh = rest
    else:
        held, sems, ham_buf, pre_buf = rest
        fresh = out_ref
    step = pl.program_id(0)
    steps = pl.num_programs(0)
    slot = step % 2

    def fetch(at, to):
        blocks = pl.ds(pl.multiple_of(at * STEP, STEP), STEP)
        return (
            pltpu.make_async_copy(ham_ref.at[blocks], ham_buf.at[to], sems.at[3 + to]),
            pltpu.make_async_copy(pre_ref.at[:, blocks], pre_buf.at[to], sems.at[5 + to]),
        )

    @pl.when(step == 0)
    def _():
        copies = []
        near_at = index_ref[RB * SLOTS]
        places = (near_at, RB, 2 * RB - near_at)
        for n, ref in enumerate((near_ref, local_ref, far_ref)):
            place = pl.multiple_of(places[n], RB)
            copies.append(pltpu.make_async_copy(ref, held.at[pl.ds(place, RB)], sems.at[n]))
            copies[-1].start()
        for copy in fetch(0, 0):
            copy.start()
        held[3 * RB] = jnp.zeros((BS, LANES), BF16)
        for copy in copies:
            copy.wait()

    @pl.when(step + 1 < steps)
    def _():
        for copy in fetch(step + 1, 1 - slot):
            copy.start()

    for copy in fetch(step, slot):
        copy.wait()

    zreal = z_ref[0:1, :]
    zimag = z_ref[1:2, :]
    totals = []
    for b in range(STEP):
        row = step * STEP + b
        right = jnp.concatenate(
            [held[index_ref[row * SLOTS + s]] for s in range(SLOTS)], axis=0
        )
        totals.append(jnp.dot(ham_buf[slot, b], right, preferred_element_type=F32))
    rights = []
    for b in range(STEP):
        current = held[RB + step * STEP + b].astype(F32)
        shifted = zreal * current + zimag * rotate_lanes(current)
        resid = (rhs_ref[b].astype(F32) - (shifted - totals[b])).astype(BF16).astype(F32)
        rights.append(split_points(resid, rotate_lanes(resid)).astype(BF16))
    for b in range(STEP):
        current = held[RB + step * STEP + b].astype(F32)
        left = jnp.concatenate([pre_buf[slot, 0, b], pre_buf[slot, 1, b]], axis=1)
        fresh[b] = (current + jnp.dot(left, rights[b], preferred_element_type=F32)).astype(BF16)
    if last:

        @pl.when(step < steps // 2)
        def _():
            out_ref[...] = fresh[...]

        @pl.when(step >= steps // 2)
        def _():
            second_ref[...] = fresh[...]


def sweep(index, ham, precond, rhs_unit, z, local, near, far, last):
    block = pl.BlockSpec((STEP, BS, LANES), lambda i, n: (i, 0, 0))
    anywhere = pl.BlockSpec(memory_space=pl.ANY)
    raw = pl.BlockSpec(memory_space=pltpu.MemorySpace.HBM)
    scratch = [
        pltpu.VMEM((3 * RB + 1, BS, LANES), BF16),
        pltpu.SemaphoreType.DMA((7,)),
        pltpu.VMEM((2, STEP, BS, SLOTS * BS), BF16),
        pltpu.VMEM((2, 2, STEP, BS, LANES), BF16),
    ]
    if last:
        half = RB // STEP // 2
        out_specs = [
            pl.BlockSpec((STEP, BS, LANES), lambda i, n: (jnp.minimum(i, half - 1), 0, 0)),
            pl.BlockSpec((STEP, BS, LANES), lambda i, n: (jnp.maximum(i - half, 0), 0, 0)),
        ]
        out_shape = [jax.ShapeDtypeStruct((RB // 2, BS, LANES), BF16)] * 2
        scratch.append(pltpu.VMEM((STEP, BS, LANES), BF16))
    else:
        out_specs = [block]
        out_shape = [jax.ShapeDtypeStruct((RB, BS, LANES), BF16)]

    def kernel(*refs):
        sweep_kernel(last, *refs)

    return pl.pallas_call(
        kernel,
        grid_spec=pltpu.PrefetchScalarGridSpec(
            num_scalar_prefetch=1,
            grid=(RB // STEP,),
            in_specs=[
                raw,
                raw,
                block,
                pl.BlockSpec((8, LANES), lambda i, n: (0, 0)),
                anywhere,
                anywhere,
                anywhere,
            ],
            out_specs=out_specs,
            scratch_shapes=scratch,
        ),
        out_shape=out_shape,
        cost_estimate=pl.CostEstimate(
            flops=2 * RB * BS * SLOTS * BS * LANES, bytes_accessed=20 << 20, transcendentals=0
        ),
        compiler_params=pltpu.CompilerParams(vmem_limit_bytes=48 << 20),
        name="sweep_last" if last else "sweep",
    )(index, ham, precond, rhs_unit, z, local, near, far)


def combine_kernel(own_ref, peer_ref, weight_ref, send_ref, keep_ref):
    own, peer = own_ref[...], peer_ref[...]
    both = jnp.concatenate([own, peer, own, peer], axis=1)
    out = jnp.dot(both, weight_ref[0], preferred_element_type=F32)
    send_ref[...] = out[:, :LANES].astype(BF16)
    keep_ref[...] = out[:, LANES:].astype(keep_ref.dtype)


def combine(own, peer, weights, which, rows_step, kind=BF16):
    rows = peer.shape[0]
    row_spec = pl.BlockSpec((rows_step, LANES), lambda i: (i, 0))
    return pl.pallas_call(
        combine_kernel,
        grid=(rows // rows_step,),
        in_specs=[
            row_spec,
            row_spec,
            pl.BlockSpec((1, 4 * LANES, 2 * LANES), lambda i: (which, 0, 0)),
        ],
        out_specs=[row_spec, row_spec],
        out_shape=[
            jax.ShapeDtypeStruct((rows, LANES), BF16),
            jax.ShapeDtypeStruct((rows, LANES), kind),
        ],
        compiler_params=pltpu.CompilerParams(vmem_limit_bytes=8 << 20),
        cost_estimate=pl.CostEstimate(
            flops=2 * rows * 256 * 512, bytes_accessed=rows * LANES * 8, transcendentals=0
        ),
        name="combine",
    )(own, peer, weights)


def own_lanes(shape, unit):
    return (lane_ids(shape) // HALF) % 2 == unit


def to_own(x, unit):
    return pltpu.roll(x, HALF if unit else LANES - HALF, axis=1)


def from_own(x, unit):
    return pltpu.roll(x, LANES - HALF if unit else HALF, axis=1)


def fold_kernel(unit, keep1_ref, got1_ref, keep2_ref, got2_ref, send_ref, own_ref):
    top = keep1_ref[...].astype(F32) + got1_ref[...].astype(F32)
    bottom = keep2_ref[...].astype(F32) + got2_ref[...].astype(F32)
    own = own_lanes(top.shape, unit)
    send_ref[...] = jnp.where(own, to_own(top, unit), bottom).astype(BF16)
    own_ref[...] = jnp.where(own, top, from_own(bottom, unit))


def fold(unit, first, second, rows, shift):
    def kernel(*refs):
        fold_kernel(unit, *refs)

    step = 1024
    spec = pl.BlockSpec((step, LANES), lambda i: (i, 0))
    late = pl.BlockSpec((step, LANES), lambda i: (i + shift // step, 0))
    return pl.pallas_call(
        kernel,
        grid=(rows // step,),
        in_specs=[spec, spec, late, late],
        out_specs=[spec, spec],
        out_shape=[
            jax.ShapeDtypeStruct((rows, LANES), BF16),
            jax.ShapeDtypeStruct((rows, LANES), F32),
        ],
        compiler_params=pltpu.CompilerParams(vmem_limit_bytes=10 << 20),
        cost_estimate=pl.CostEstimate(
            flops=rows * LANES * 8, bytes_accessed=rows * LANES * 14, transcendentals=0
        ),
        name="fold",
    )(*first, *second)


def finish_kernel(own1_ref, got1_ref, own2_ref, got2_ref, own_b_ref, got_b_ref, out_ref):
    unit_b = own_b_ref[...] + got_b_ref[...].astype(F32)
    first = own_lanes(unit_b.shape, 0)
    halves = pl.num_programs(0) // 2

    def store(place):
        top_a = place(own1_ref[...] + got1_ref[...].astype(F32))
        bottom_a = place(own2_ref[...] + got2_ref[...].astype(F32))
        out_ref[0, 0] = jnp.where(first, top_a, unit_b)
        out_ref[0, 1] = jnp.where(first, bottom_a, to_own(unit_b, 1))

    @pl.when(pl.program_id(0) < halves)
    def _():
        store(lambda x: x)

    @pl.when(pl.program_id(0) >= halves)
    def _():
        store(lambda x: to_own(x, 0))


def finish(own1, got1, own2, got2, own_b, got_b, step):
    rows = own_b.shape[0]
    half = rows // 2 // step
    spec = pl.BlockSpec((step, LANES), lambda i: (i, 0))
    spec_a = pl.BlockSpec((step, LANES), lambda i: (i % half, 0))
    return pl.pallas_call(
        finish_kernel,
        grid=(rows // step,),
        in_specs=[spec_a] * 4 + [spec] * 2,
        out_specs=pl.BlockSpec((1, 2, step, LANES), lambda i: (0, 0, i, 0)),
        out_shape=jax.ShapeDtypeStruct((1, 2, rows, LANES), F32),
        compiler_params=pltpu.CompilerParams(vmem_limit_bytes=10 << 20),
        name="finish",
    )(own1, got1, own2, got2, own_b, got_b)


def moment_coefs(plans):
    lane = lax.broadcasted_iota(jnp.int32, (1, 32, 2 * LANES), 2)
    line = lax.broadcasted_iota(jnp.int32, (1, 32, 2 * LANES), 1)
    point, kind = line // 8, line % 8
    tables = []
    for unit, owners, orders in plans:
        slot = lane // LANES * 2 + ((lane // HALF) % 2 ^ unit)
        owner = jnp.where(point < 2, owners[0], owners[1])
        low = jnp.where(slot == 0, orders[0], orders[1])
        high = jnp.where(slot == 2, orders[2], orders[3])
        order = jnp.where(slot < 2, low, high)
        turns = ((order + 1) * (2 * (owner * 2 + point % 2) + 1)) % (2 * POINTS)
        sign = jnp.where((lane // GROUP) % 2 == 0, -1.0, 1.0)
        phase = turns.astype(F32) * (math.pi / POINTS)
        quarter = jnp.where(kind == 0, math.pi / 2, 0.0)
        tables.append(jnp.where(kind == 0, 1.0, sign) * jnp.sin(phase + quarter) / POINTS)
    return jnp.concatenate(tables, axis=0)


def step(hamiltonian, columns, counts, precond, rhs):
    row_index = lax.axis_index("row")
    quad_index = lax.axis_index("quad")

    def swap(x, axis, peer_of):
        peers = [(i, peer_of(i)) for i in range(lax.axis_size(axis))]
        return lax.ppermute(x, axis, [(i, j) for i, j in peers if 0 <= j < len(peers)])

    def by_pair(i):
        return (((i // 2) ^ 1) * 2) + i % 2

    def by_mirror(i):
        return ((3 - i // 2) * 2) + i % 2

    def by_x(i):
        return i ^ 1

    def near_row(i):
        return i ^ 1

    def far_row(i):
        return i + 1 if i % 2 else i - 1

    units = list(initial(rhs, precond))

    live = jnp.arange(SLOTS)[None, :] < counts[:, None]
    index = jnp.where(live, columns - (row_index - 1) * RB, 3 * RB).reshape(RB * SLOTS)
    near_at = jnp.where(row_index % 2 == 1, 0, 2 * RB)
    index = jnp.concatenate([index, jnp.full((LANES,), near_at, jnp.int32)])
    lane = jnp.arange(LANES)[None, :]
    theta = 2.0 * jnp.pi * ((quad_index * 2 + lane // GROUP).astype(F32) + 0.5) / POINTS
    z = jnp.concatenate([jnp.cos(theta), jnp.sin(theta), jnp.zeros((6, LANES), F32)], axis=0)

    mine, other = quad_index, quad_index ^ 1
    pair, mirror = by_pair(quad_index), by_mirror(quad_index)
    coefs = moment_coefs(
        (
            (0, (mine, pair), (other, mirror ^ 1, mine, mirror)),
            (0, (mine, mirror), (other, pair ^ 1, mine, pair)),
            (1, (mine, pair), (mirror, mirror ^ 1, mine, other)),
            (1, (mine, mirror), (pair, pair ^ 1, mine, other)),
            (1, (mine, other), (pair, by_mirror(pair), mine, mirror)),
        ),
    )
    *rhs_units, weights = spread(rhs, coefs)

    grams = [None, None]
    for it in range(ITERS):
        for unit in range(2):
            y = units[unit]
            far = swap(y, "row", far_row)
            near = swap(y, "row", near_row)
            last = it == ITERS - 1
            local = y if it else in_hbm(y)
            got = sweep(
                index, hamiltonian, precond, rhs_units[unit], z, local, near, far, last
            )
            units[unit] = got[0]
            if last:
                units[unit] = got[:2]
                both = (part.reshape(-1, LANES) for part in got)
                parts = zip((rhs[: RB * BS // 2], rhs[RB * BS // 2 :]), both, strict=True)
                grams[unit] = sum(
                    lax.dot_general(x, part, (((0,), (0,)), ((), ())), preferred_element_type=F32)
                    for x, part in parts
                )

    half_rows = RB * BS // 2

    def first_stage(unit):
        top, bottom = (part.reshape(half_rows, LANES) for part in units[unit])
        got1 = swap(top, "quad", by_pair)
        got2 = swap(bottom, "quad", by_mirror)
        out1 = combine(top, got1, weights, 2 * unit, 1024)
        out2 = combine(bottom, got2, weights, 2 * unit + 1, 1024)
        return *out1, *out2

    send_a1, keep_a1, send_a2, keep_a2 = first_stage(0)
    quarter = half_rows // 2
    got_a1 = swap(send_a1, "quad", by_x)
    got_a2 = swap(send_a2, "quad", by_x)
    half = (keep_a1, got_a1)
    send_a1, own_a1 = fold(0, half, half, quarter, quarter)
    half = (keep_a2, got_a2)
    send_a2, own_a2 = fold(0, half, half, quarter, quarter)

    send_b1, keep_b1, send_b2, keep_b2 = first_stage(1)
    got_b1 = swap(send_b1, "quad", by_mirror)
    got_b2 = swap(send_b2, "quad", by_pair)
    send_b, own_b = fold(1, (keep_b1, got_b1), (keep_b2, got_b2), half_rows, 0)

    def rounded(x):
        return lax.reduce_precision(x, 8, 7)

    even = row_index % 2 == 0
    gram = jnp.where(even, grams[0], grams[1])
    gram = gram + swap(jnp.where(even, grams[1], grams[0]), "row", near_row)
    for bit in (8, 4, 2):
        gram = rounded(gram)
        peer = swap(gram.astype(BF16), "row", lambda i, bit=bit: i ^ bit)
        gram = gram + peer.astype(F32)
    gram = gram.astype(BF16)
    peer = swap(gram, "quad", by_x)
    send_g, keep_g = combine(gram, peer, weights, 4, LANES, F32)
    gram_sum = keep_g + swap(send_g, "quad", by_pair).astype(F32)
    gram_got = swap(gram_sum.astype(BF16), "quad", by_mirror)
    gram_own = gram_sum + jnp.roll(gram_got, HALF, axis=1).astype(F32)
    gram_other = swap(gram_own, "row", near_row)
    gram_a = jnp.where(even, gram_own, gram_other)
    gram_b = jnp.where(even, gram_other, gram_own)
    first = own_lanes((LANES, LANES), 0)
    blocks = jnp.where(first, jnp.roll(gram_a, -HALF, axis=1), gram_b)
    blocks = (blocks * (1.0 / math.sqrt(RB * BS * 16)))[None]

    got_a1 = swap(send_a1, "quad", by_mirror)
    got_a2 = swap(send_a2, "quad", by_pair)
    got_b = swap(send_b, "quad", by_x)
    moments = finish(own_a1, got_a1, in_hbm(own_a2), got_a2, own_b, got_b, 1024)
    return moments.reshape(1, RB * BS, LANES), blocks


def solution(mesh):
    return jax.shard_map(
        step,
        mesh=mesh,
        in_specs=(
            P("row", None, None),
            P("row", None),
            P("row"),
            P("quad", "row", None, None),
            P("row", None),
        ),
        out_specs=(P("quad", "row", None), P("quad", None, None)),
        check_vma=False,
    )
```

```python
import math

import jax
import jax.numpy as jnp
import numpy as np
from jax import lax
from jax.experimental import pallas as pl
from jax.experimental.pallas import tpu as pltpu
from jax.sharding import PartitionSpec as P

ITERS = 2
POINTS = 16
BS = 64
SLOTS = 24
RB = 64
LANES = 128
GROUP = 64
HALF = 32
STEP = 16
FIRST = 32
F32 = jnp.float32
BF16 = jnp.bfloat16


def unit_lanes(points):
    table = np.zeros((points * LANES, 2 * LANES), np.float32)
    for unit in range(2):
        for lane in range(LANES):
            point, part, col = lane // GROUP, (lane // HALF) % 2, lane % HALF
            src = (point % points) * LANES + part * GROUP + unit * HALF + col
            table[src, unit * LANES + lane] = 1.0
    return table


def in_hbm(x):
    return pltpu.with_memory_space_constraint(x, pltpu.MemorySpace.HBM)


def lane_ids(shape):
    return lax.broadcasted_iota(jnp.int32, shape, len(shape) - 1)


def split_points(top, bottom):
    lane = lane_ids(top.shape) % LANES
    first = lane < GROUP
    zero = jnp.zeros_like(top)
    return jnp.concatenate(
        [
            jnp.where(first, top, zero),
            jnp.where(first, bottom, zero),
            jnp.where(first, zero, top),
            jnp.where(first, zero, bottom),
        ],
        axis=0,
    )


def init_kernel(x_ref, pre_ref, map_ref, y_a_ref, y_b_ref):
    rights = []
    for b in range(FIRST):
        x = x_ref[b * BS : (b + 1) * BS].astype(F32)
        turned = pltpu.roll(x, GROUP, axis=1)
        turned = jnp.where(lane_ids(x.shape) < GROUP, -turned, turned)
        rights.append(jnp.concatenate([x, turned], axis=0).astype(BF16))
    outs = []
    for b in range(FIRST):
        left = jnp.concatenate([pre_ref[0, b], pre_ref[1, b]], axis=0)
        outs.append(jnp.dot(left, rights[b], preferred_element_type=F32))
    outs = [out.astype(BF16) for out in outs]
    firsts = [out[:BS] for out in outs]
    seconds = [out[BS:] for out in outs]
    both = jnp.concatenate(
        [jnp.concatenate(firsts, axis=0), jnp.concatenate(seconds, axis=0)], axis=1
    )
    out = jnp.dot(both, map_ref[...], preferred_element_type=F32).astype(BF16)
    y_a_ref[...] = out[:, :LANES].reshape(FIRST, BS, LANES)
    y_b_ref[...] = out[:, LANES:].reshape(FIRST, BS, LANES)


def initial(rhs, precond):
    block = jax.ShapeDtypeStruct((RB, BS, LANES), BF16)
    out_spec = pl.BlockSpec((FIRST, BS, LANES), lambda i: (i, 0, 0))
    return pl.pallas_call(
        init_kernel,
        grid=(RB // FIRST,),
        in_specs=[
            pl.BlockSpec((FIRST * BS, LANES), lambda i: (i, 0)),
            pl.BlockSpec((2, FIRST, BS, LANES), lambda i: (0, i, 0, 0)),
            pl.BlockSpec((2 * LANES, 2 * LANES), lambda i: (0, 0)),
        ],
        out_specs=[out_spec] * 2,
        out_shape=[block] * 2,
        name="initial",
    )(rhs, precond, jnp.asarray(unit_lanes(2), BF16))


def spread_kernel(x_ref, map_ref, coef_ref, rhs_a_ref, rhs_b_ref, weight_ref):
    out = jnp.dot(x_ref[...], map_ref[...], preferred_element_type=F32).astype(BF16)
    rhs_a_ref[...] = out[:, :LANES].reshape(rhs_a_ref.shape)
    rhs_b_ref[...] = out[:, LANES:].reshape(rhs_b_ref.shape)
    shape = (GROUP, 2 * LANES)
    r = lax.broadcasted_iota(jnp.int32, shape, 0)
    c = lax.broadcasted_iota(jnp.int32, shape, 1)
    same = r % HALF == c % HALF
    straight = same & ((r // HALF) == (c // GROUP) % 2)
    crossed = same & ((r // HALF) != (c // GROUP) % 2)
    for point in range(4):
        rows = coef_ref[0, point * 8 : point * 8 + 8]
        cosine, sine = rows[0:1, :], rows[1:2, :]
        value = jnp.where(straight, cosine, jnp.where(crossed, sine, 0.0))
        high = value.astype(BF16)
        weight_ref[0, point * GROUP : (point + 1) * GROUP] = high
        weight_ref[0, (4 + point) * GROUP : (5 + point) * GROUP] = (
            value - high.astype(F32)
        ).astype(BF16)


def spread(rhs, coefs):
    block = jax.ShapeDtypeStruct((RB, BS, LANES), BF16)
    out_spec = pl.BlockSpec((RB // 8, BS, LANES), lambda i: (i, 0, 0))
    return pl.pallas_call(
        spread_kernel,
        grid=(8,),
        in_specs=[
            pl.BlockSpec((RB // 8 * BS, LANES), lambda i: (i, 0)),
            pl.BlockSpec((LANES, 2 * LANES), lambda i: (0, 0)),
            pl.BlockSpec((1, 32, 2 * LANES), lambda i: (jnp.minimum(i, 4), 0, 0)),
        ],
        out_specs=[out_spec, out_spec, pl.BlockSpec((1, 512, 256), lambda i: (jnp.minimum(i, 4), 0, 0))],
        out_shape=[block, block, jax.ShapeDtypeStruct((5, 512, 256), BF16)],
        compiler_params=pltpu.CompilerParams(vmem_limit_bytes=14 << 20),
        cost_estimate=pl.CostEstimate(
            flops=2 * RB * BS * LANES * 256, bytes_accessed=3 << 20, transcendentals=0
        ),
        name="spread",
    )(rhs, jnp.asarray(unit_lanes(1), BF16), coefs)


def rotate_lanes(x):
    lane = lane_ids(x.shape) % GROUP
    up = pltpu.roll(x, LANES - HALF, axis=x.ndim - 1)
    down = pltpu.roll(x, HALF, axis=x.ndim - 1)
    return jnp.where(lane < HALF, -up, down)


def sweep_kernel(
    last, index_ref, ham_ref, pre_ref, rhs_ref, z_ref, local_ref, near_ref, far_ref,
    out_ref, *rest,
):
    if last:
        second_ref, held, sems, ham_buf, pre_buf, fresh = rest
    else:
        held, sems, ham_buf, pre_buf = rest
        fresh = out_ref
    step = pl.program_id(0)
    steps = pl.num_programs(0)
    slot = step % 2

    def fetch(at, to):
        blocks = pl.ds(pl.multiple_of(at * STEP, STEP), STEP)
        return (
            pltpu.make_async_copy(ham_ref.at[blocks], ham_buf.at[to], sems.at[3 + to]),
            pltpu.make_async_copy(pre_ref.at[:, blocks], pre_buf.at[to], sems.at[5 + to]),
        )

    @pl.when(step == 0)
    def _():
        copies = []
        near_at = index_ref[RB * SLOTS]
        places = (near_at, RB, 2 * RB - near_at)
        for n, ref in enumerate((near_ref, local_ref, far_ref)):
            place = pl.multiple_of(places[n], RB)
            copies.append(pltpu.make_async_copy(ref, held.at[pl.ds(place, RB)], sems.at[n]))
            copies[-1].start()
        for copy in fetch(0, 0):
            copy.start()
        held[3 * RB] = jnp.zeros((BS, LANES), BF16)
        for copy in copies:
            copy.wait()

    @pl.when(step + 1 < steps)
    def _():
        for copy in fetch(step + 1, 1 - slot):
            copy.start()

    for copy in fetch(step, slot):
        copy.wait()

    zreal = z_ref[0:1, :]
    zimag = z_ref[1:2, :]
    totals = []
    for b in range(STEP):
        row = step * STEP + b
        right = jnp.concatenate(
            [held[index_ref[row * SLOTS + s]] for s in range(SLOTS)], axis=0
        )
        totals.append(jnp.dot(ham_buf[slot, b], right, preferred_element_type=F32))
    rights = []
    for b in range(STEP):
        current = held[RB + step * STEP + b].astype(F32)
        shifted = zreal * current + zimag * rotate_lanes(current)
        resid = (rhs_ref[b].astype(F32) - (shifted - totals[b])).astype(BF16).astype(F32)
        rights.append(split_points(resid, rotate_lanes(resid)).astype(BF16))
    for b in range(STEP):
        current = held[RB + step * STEP + b].astype(F32)
        left = jnp.concatenate([pre_buf[slot, 0, b], pre_buf[slot, 1, b]], axis=1)
        fresh[b] = (current + jnp.dot(left, rights[b], preferred_element_type=F32)).astype(BF16)
    if last:

        @pl.when(step < steps // 2)
        def _():
            out_ref[...] = fresh[...]

        @pl.when(step >= steps // 2)
        def _():
            second_ref[...] = fresh[...]


def sweep(index, ham, precond, rhs_unit, z, local, near, far, last):
    block = pl.BlockSpec((STEP, BS, LANES), lambda i, n: (i, 0, 0))
    anywhere = pl.BlockSpec(memory_space=pl.ANY)
    raw = pl.BlockSpec(memory_space=pltpu.MemorySpace.HBM)
    scratch = [
        pltpu.VMEM((3 * RB + 1, BS, LANES), BF16),
        pltpu.SemaphoreType.DMA((7,)),
        pltpu.VMEM((2, STEP, BS, SLOTS * BS), BF16),
        pltpu.VMEM((2, 2, STEP, BS, LANES), BF16),
    ]
    if last:
        half = RB // STEP // 2
        out_specs = [
            pl.BlockSpec((STEP, BS, LANES), lambda i, n: (jnp.minimum(i, half - 1), 0, 0)),
            pl.BlockSpec((STEP, BS, LANES), lambda i, n: (jnp.maximum(i - half, 0), 0, 0)),
        ]
        out_shape = [jax.ShapeDtypeStruct((RB // 2, BS, LANES), BF16)] * 2
        scratch.append(pltpu.VMEM((STEP, BS, LANES), BF16))
    else:
        out_specs = [block]
        out_shape = [jax.ShapeDtypeStruct((RB, BS, LANES), BF16)]

    def kernel(*refs):
        sweep_kernel(last, *refs)

    return pl.pallas_call(
        kernel,
        grid_spec=pltpu.PrefetchScalarGridSpec(
            num_scalar_prefetch=1,
            grid=(RB // STEP,),
            in_specs=[
                raw,
                raw,
                block,
                pl.BlockSpec((8, LANES), lambda i, n: (0, 0)),
                anywhere,
                anywhere,
                anywhere,
            ],
            out_specs=out_specs,
            scratch_shapes=scratch,
        ),
        out_shape=out_shape,
        cost_estimate=pl.CostEstimate(
            flops=2 * RB * BS * SLOTS * BS * LANES, bytes_accessed=20 << 20, transcendentals=0
        ),
        compiler_params=pltpu.CompilerParams(vmem_limit_bytes=48 << 20),
        name="sweep_last" if last else "sweep",
    )(index, ham, precond, rhs_unit, z, local, near, far)


def combine_kernel(own_ref, peer_ref, weight_ref, send_ref, keep_ref):
    own, peer = own_ref[...], peer_ref[...]
    both = jnp.concatenate([own, peer, own, peer], axis=1)
    out = jnp.dot(both, weight_ref[0], preferred_element_type=F32)
    send_ref[...] = out[:, :LANES].astype(BF16)
    keep_ref[...] = out[:, LANES:].astype(keep_ref.dtype)


def combine(own, peer, weights, which, rows_step, kind=BF16):
    rows = peer.shape[0]
    row_spec = pl.BlockSpec((rows_step, LANES), lambda i: (i, 0))
    return pl.pallas_call(
        combine_kernel,
        grid=(rows // rows_step,),
        in_specs=[
            row_spec,
            row_spec,
            pl.BlockSpec((1, 4 * LANES, 2 * LANES), lambda i: (which, 0, 0)),
        ],
        out_specs=[row_spec, row_spec],
        out_shape=[
            jax.ShapeDtypeStruct((rows, LANES), BF16),
            jax.ShapeDtypeStruct((rows, LANES), kind),
        ],
        compiler_params=pltpu.CompilerParams(vmem_limit_bytes=8 << 20),
        cost_estimate=pl.CostEstimate(
            flops=2 * rows * 256 * 512, bytes_accessed=rows * LANES * 8, transcendentals=0
        ),
        name="combine",
    )(own, peer, weights)


def own_lanes(shape, unit):
    return (lane_ids(shape) // HALF) % 2 == unit


def to_own(x, unit):
    return pltpu.roll(x, HALF if unit else LANES - HALF, axis=1)


def from_own(x, unit):
    return pltpu.roll(x, LANES - HALF if unit else HALF, axis=1)


def fold_kernel(unit, keep1_ref, got1_ref, keep2_ref, got2_ref, send_ref, own_ref):
    top = keep1_ref[...].astype(F32) + got1_ref[...].astype(F32)
    bottom = keep2_ref[...].astype(F32) + got2_ref[...].astype(F32)
    own = own_lanes(top.shape, unit)
    send_ref[...] = jnp.where(own, to_own(top, unit), bottom).astype(BF16)
    own_ref[...] = jnp.where(own, top, from_own(bottom, unit))


def fold(unit, first, second, rows, shift):
    def kernel(*refs):
        fold_kernel(unit, *refs)

    step = 1024
    spec = pl.BlockSpec((step, LANES), lambda i: (i, 0))
    late = pl.BlockSpec((step, LANES), lambda i: (i + shift // step, 0))
    return pl.pallas_call(
        kernel,
        grid=(rows // step,),
        in_specs=[spec, spec, late, late],
        out_specs=[spec, spec],
        out_shape=[
            jax.ShapeDtypeStruct((rows, LANES), BF16),
            jax.ShapeDtypeStruct((rows, LANES), F32),
        ],
        compiler_params=pltpu.CompilerParams(vmem_limit_bytes=10 << 20),
        cost_estimate=pl.CostEstimate(
            flops=rows * LANES * 8, bytes_accessed=rows * LANES * 14, transcendentals=0
        ),
        name="fold",
    )(*first, *second)


def finish_kernel(own1_ref, got1_ref, own2_ref, got2_ref, own_b_ref, got_b_ref, out_ref):
    unit_b = own_b_ref[...] + got_b_ref[...].astype(F32)
    first = own_lanes(unit_b.shape, 0)
    halves = pl.num_programs(0) // 2

    def store(place):
        top_a = place(own1_ref[...] + got1_ref[...].astype(F32))
        bottom_a = place(own2_ref[...] + got2_ref[...].astype(F32))
        out_ref[0, 0] = jnp.where(first, top_a, unit_b)
        out_ref[0, 1] = jnp.where(first, bottom_a, to_own(unit_b, 1))

    @pl.when(pl.program_id(0) < halves)
    def _():
        store(lambda x: x)

    @pl.when(pl.program_id(0) >= halves)
    def _():
        store(lambda x: to_own(x, 0))


def finish(own1, got1, own2, got2, own_b, got_b, step):
    rows = own_b.shape[0]
    half = rows // 2 // step
    spec = pl.BlockSpec((step, LANES), lambda i: (i, 0))
    spec_a = pl.BlockSpec((step, LANES), lambda i: (i % half, 0))
    return pl.pallas_call(
        finish_kernel,
        grid=(rows // step,),
        in_specs=[spec_a] * 4 + [spec] * 2,
        out_specs=pl.BlockSpec((1, 2, step, LANES), lambda i: (0, 0, i, 0)),
        out_shape=jax.ShapeDtypeStruct((1, 2, rows, LANES), F32),
        compiler_params=pltpu.CompilerParams(vmem_limit_bytes=10 << 20),
        name="finish",
    )(own1, got1, own2, got2, own_b, got_b)


def moment_coefs(plans):
    lane = lax.broadcasted_iota(jnp.int32, (1, 32, 2 * LANES), 2)
    line = lax.broadcasted_iota(jnp.int32, (1, 32, 2 * LANES), 1)
    point, kind = line // 8, line % 8
    tables = []
    for unit, owners, orders in plans:
        slot = lane // LANES * 2 + ((lane // HALF) % 2 ^ unit)
        owner = jnp.where(point < 2, owners[0], owners[1])
        low = jnp.where(slot == 0, orders[0], orders[1])
        high = jnp.where(slot == 2, orders[2], orders[3])
        order = jnp.where(slot < 2, low, high)
        turns = ((order + 1) * (2 * (owner * 2 + point % 2) + 1)) % (2 * POINTS)
        sign = jnp.where((lane // GROUP) % 2 == 0, -1.0, 1.0)
        phase = turns.astype(F32) * (math.pi / POINTS)
        quarter = jnp.where(kind == 0, math.pi / 2, 0.0)
        tables.append(jnp.where(kind == 0, 1.0, sign) * jnp.sin(phase + quarter) / POINTS)
    return jnp.concatenate(tables, axis=0)


def step(hamiltonian, columns, counts, precond, rhs):
    row_index = lax.axis_index("row")
    quad_index = lax.axis_index("quad")

    def swap(x, axis, peer_of):
        peers = [(i, peer_of(i)) for i in range(lax.axis_size(axis))]
        return lax.ppermute(x, axis, [(i, j) for i, j in peers if 0 <= j < len(peers)])

    def by_pair(i):
        return (((i // 2) ^ 1) * 2) + i % 2

    def by_mirror(i):
        return ((3 - i // 2) * 2) + i % 2

    def by_x(i):
        return i ^ 1

    def near_row(i):
        return i ^ 1

    def far_row(i):
        return i + 1 if i % 2 else i - 1

    units = list(initial(rhs, precond))

    live = jnp.arange(SLOTS)[None, :] < counts[:, None]
    index = jnp.where(live, columns - (row_index - 1) * RB, 3 * RB).reshape(RB * SLOTS)
    near_at = jnp.where(row_index % 2 == 1, 0, 2 * RB)
    index = jnp.concatenate([index, jnp.full((LANES,), near_at, jnp.int32)])
    lane = jnp.arange(LANES)[None, :]
    theta = 2.0 * jnp.pi * ((quad_index * 2 + lane // GROUP).astype(F32) + 0.5) / POINTS
    z = jnp.concatenate([jnp.cos(theta), jnp.sin(theta), jnp.zeros((6, LANES), F32)], axis=0)

    mine, other = quad_index, quad_index ^ 1
    pair, mirror = by_pair(quad_index), by_mirror(quad_index)
    coefs = moment_coefs(
        (
            (0, (mine, pair), (other, mirror ^ 1, mine, mirror)),
            (0, (mine, mirror), (other, pair ^ 1, mine, pair)),
            (1, (mine, pair), (mirror, mirror ^ 1, mine, other)),
            (1, (mine, mirror), (pair, pair ^ 1, mine, other)),
            (1, (mine, other), (mirror, by_pair(mirror), mine, pair)),
        ),
    )
    *rhs_units, weights = spread(rhs, coefs)

    grams = [None, None]
    for it in range(ITERS):
        for unit in range(2):
            y = units[unit]
            far = swap(y, "row", far_row)
            near = swap(y, "row", near_row)
            last = it == ITERS - 1
            local = y if it else in_hbm(y)
            got = sweep(
                index, hamiltonian, precond, rhs_units[unit], z, local, near, far, last
            )
            units[unit] = got[0]
            if last:
                units[unit] = got[:2]
                both = (part.reshape(-1, LANES) for part in got)
                parts = zip((rhs[: RB * BS // 2], rhs[RB * BS // 2 :]), both, strict=True)
                grams[unit] = sum(
                    lax.dot_general(x, part, (((0,), (0,)), ((), ())), preferred_element_type=F32)
                    for x, part in parts
                )

    half_rows = RB * BS // 2

    def first_stage(unit):
        top, bottom = (part.reshape(half_rows, LANES) for part in units[unit])
        got1 = swap(top, "quad", by_pair)
        got2 = swap(bottom, "quad", by_mirror)
        out1 = combine(top, got1, weights, 2 * unit, 1024)
        out2 = combine(bottom, got2, weights, 2 * unit + 1, 1024)
        return *out1, *out2

    send_a1, keep_a1, send_a2, keep_a2 = first_stage(0)
    quarter = half_rows // 2
    got_a1 = swap(send_a1, "quad", by_x)
    got_a2 = swap(send_a2, "quad", by_x)
    half = (keep_a1, got_a1)
    send_a1, own_a1 = fold(0, half, half, quarter, quarter)
    half = (keep_a2, got_a2)
    send_a2, own_a2 = fold(0, half, half, quarter, quarter)

    send_b1, keep_b1, send_b2, keep_b2 = first_stage(1)
    got_b1 = swap(send_b1, "quad", by_mirror)
    got_b2 = swap(send_b2, "quad", by_pair)
    send_b, own_b = fold(1, (keep_b1, got_b1), (keep_b2, got_b2), half_rows, 0)

    def rounded(x):
        return lax.reduce_precision(x, 8, 7)

    even = row_index % 2 == 0
    gram = jnp.where(even, grams[0], grams[1])
    gram = gram + swap(jnp.where(even, grams[1], grams[0]), "row", near_row)
    for bit in (8, 4, 2):
        gram = rounded(gram)
        peer = swap(gram.astype(BF16), "row", lambda i, bit=bit: i ^ bit)
        gram = gram + peer.astype(F32)
    gram = gram.astype(BF16)
    peer = swap(gram, "quad", by_x)
    send_g, keep_g = combine(gram, peer, weights, 4, LANES, F32)
    gram_sum = keep_g + swap(send_g, "quad", by_mirror).astype(F32)
    gram_got = swap(gram_sum.astype(BF16), "quad", by_pair)
    gram_own = gram_sum + jnp.roll(gram_got, HALF, axis=1).astype(F32)
    gram_other = swap(gram_own, "row", near_row)
    gram_a = jnp.where(even, gram_own, gram_other)
    gram_b = jnp.where(even, gram_other, gram_own)
    first = own_lanes((LANES, LANES), 0)
    blocks = jnp.where(first, jnp.roll(gram_a, -HALF, axis=1), gram_b)
    blocks = (blocks * (1.0 / math.sqrt(RB * BS * 16)))[None]

    got_a1 = swap(send_a1, "quad", by_mirror)
    got_a2 = swap(send_a2, "quad", by_pair)
    got_b = swap(send_b, "quad", by_x)
    moments = finish(own_a1, got_a1, in_hbm(own_a2), got_a2, own_b, got_b, 1024)
    return moments.reshape(1, RB * BS, LANES), blocks


def solution(mesh):
    return jax.shard_map(
        step,
        mesh=mesh,
        in_specs=(
            P("row", None, None),
            P("row", None),
            P("row"),
            P("quad", "row", None, None),
            P("row", None),
        ),
        out_specs=(P("quad", "row", None), P("quad", None, None)),
        check_vma=False,
    )
```
